32 devices in a mesh: gx: 8 (over y, x, core), gy: 4 (over z).
Axes of the slice: x: 2, y: 2, z: 4, core: 2. Of those that a mesh axis runs over, the one named last changes fastest.
Arguments:
- elevation: float32 [8, 128, 1024], P(None, 'gy', 'gx'), may hold values from -4 to 4
- east_velocity: float32 [8, 128, 1024], P(None, 'gy', 'gx'), may hold values from -3 to 3
- north_velocity: float32 [8, 128, 1024], P(None, 'gy', 'gx'), may hold values from -3 to 3
- water_depth: float32 [128, 1024], P('gy', 'gx'), may hold values from 0.3 to 1
- land_sea: int32 [128, 1024], P('gy', 'gx'), may hold values 0 or 1
Outputs:
- surface: float32 [8, 128, 1024], P(None, 'gy', 'gx')
- east_flow: float32 [8, 128, 1024], P(None, 'gy', 'gx')
- north_flow: float32 [8, 128, 1024], P(None, 'gy', 'gx')
- loading: float32 [8, 16, 128], P(None, 'gy', 'gx')
The draws below stay inside these ranges and needn't reach their ends.
All inputs are finite; a program needn't handle non-finite values. No bound on the sum of `land_sea` on one device may be relied on, other than what follows from the above.
Results may differ from the reference program's by a relative error of at most 0.0032.
Values may be sent and summed in bfloat16 or wider, within the bound.
A program may use at most 64 MiB of HBM per device.

```python
import math
import jax
import jax.numpy as jnp
from jax import lax

MEMBERS = 8
STEPS = 4
INTERVALS = 2
BLOCK = 8
NX = 1024
NY = 128


def draw_elevation(key, part):
    full_shape = (MEMBERS, NY, NX)
    return jnp.clip(jax.random.normal(jax.random.fold_in(key, 12), full_shape, jnp.float32), -4.0, 4.0)


def place_ends(result, key, smallest, top_value):
    extent = result.shape
    place = [jax.random.randint(jax.random.fold_in(key, axis), (), 0, extent[axis]) for axis in range(len(extent))]
    result = result.at[tuple(place)].set(smallest)
    longest = extent.index(max(extent))
    place[longest] = (place[longest] + 1) % extent[longest]
    return result.at[tuple(place)].set(top_value)


def levels(own_key, dims, split, smallest, top_value):
    gain = 1.0
    for axis_at, blocks in split:
        steps = jax.random.uniform(jax.random.fold_in(jax.random.fold_in(own_key, 6), axis_at), (blocks,), jnp.float32, smallest / len(split), top_value / len(split))
        gain = gain * jnp.repeat(jnp.exp(steps), dims[axis_at] // blocks).reshape((-1,) + (1,) * (len(dims) - 1 - axis_at))
    return gain


def noise(stream_key, extent, width, limit, pieces=(), held_as=jnp.bfloat16):
    drawn = width * jax.random.normal(stream_key, extent, jnp.float32)
    if pieces:
        drawn = drawn * levels(stream_key, extent, pieces, -0.22, 0.18)
    return jnp.clip(drawn, -limit, limit).astype(held_as)


def setup_inputs(seed: int = 0) -> dict:
    splits = jax.random.split(jax.random.key(seed), 6)
    elevation = draw_elevation(jax.random.fold_in(splits[5], 71), 0)
    east_velocity = noise(splits[1], (MEMBERS, NY, NX), 0.5, 3.0, ((1, 4), (2, 8)), jnp.float32)
    north_velocity = noise(splits[2], (MEMBERS, NY, NX), 0.5, 3.0, ((1, 4), (2, 8)), jnp.float32)
    water_depth = jnp.clip(0.3 + 0.7 * jax.random.uniform(splits[3], (NY, NX), jnp.float32) ** levels(splits[3], (NY, NX), ((0, 4), (1, 8)), -0.2, 0.2), 0.3, 1.0)
    land_sea = place_ends((jax.random.randint(splits[4], (NY, NX), 0, 10) < 7).astype(jnp.int32), jax.random.fold_in(splits[4], 1), 0, 1)
    return dict(elevation=elevation, east_velocity=east_velocity, north_velocity=north_velocity, water_depth=water_depth, land_sea=land_sea)


COURANT = 0.35
FRICTION = 0.02
CORIOLIS = 0.3
GREEN_SCALE = 0.25

def latitude(row_ids, row_count):
    return ((row_ids.astype(jnp.float32) + 0.5) / row_count - 0.5) * jnp.pi

def longitude(col_ids, col_count):
    return (col_ids.astype(jnp.float32) + 0.5) / col_count * (2.0 * jnp.pi)

def unit_vectors(lat_angle, lon_angle):
    return (jnp.cos(lat_angle) * jnp.cos(lon_angle), jnp.cos(lat_angle) * jnp.sin(lon_angle), jnp.sin(lat_angle))

def green_block(source, target, coarse_rows):
    first = source[0][:, None] - target[0][None, :]
    second = source[1][:, None] - target[1][None, :]
    third = source[2][:, None] - target[2][None, :]
    chord_len = jnp.sqrt(first * first + second * second + third * third)
    return (GREEN_SCALE / (1.0 + chord_len * (coarse_rows / math.pi))).astype(jnp.bfloat16)

def coarse_loads(height, ocean):
    members, row_total, col_total = height.shape
    blocks = (ocean * height).reshape(members, row_total // BLOCK, BLOCK, col_total // BLOCK, BLOCK)
    return (lax.optimization_barrier(jnp.sum(blocks, axis=(2, 4))) / BLOCK).astype(jnp.bfloat16)

def refine(loading):
    members, row_blocks, col_blocks = loading.shape
    spread = jnp.broadcast_to(loading[:, :, None, :, None], (members, row_blocks, BLOCK, col_blocks, BLOCK))
    return spread.reshape(members, row_blocks * BLOCK, col_blocks * BLOCK)

def velocities(padded, east_now, north_now, ocean, turning):
    grad_east = (padded[:, 1:-1, 2:] - padded[:, 1:-1, :-2]) * 0.5
    grad_north = (padded[:, 2:, 1:-1] - padded[:, :-2, 1:-1]) * 0.5
    east_next = ocean * (east_now + turning * north_now - COURANT * grad_east - FRICTION * east_now)
    north_next = ocean * (north_now - turning * east_now - COURANT * grad_north - FRICTION * north_now)
    return (east_next, north_next)

def surface_update(height, east_rim, north_rim, ocean):
    outflow = (east_rim[:, :, 2:] - east_rim[:, :, :-2]) * 0.5 + (north_rim[:, 2:, :] - north_rim[:, :-2, :]) * 0.5
    return height - ocean * COURANT * outflow

def wrap_east(field):
    return jnp.concatenate([field[:, :, -1:], field, field[:, :, :1]], axis=2)

def zero_north(field):
    return jnp.pad(field, ((0, 0), (1, 1), (0, 0)))

def reference(elevation, east_velocity, north_velocity, water_depth, land_sea):
    ocean = land_sea.astype(jnp.float32)
    row_blocks = NY // BLOCK
    col_blocks = NX // BLOCK
    turning = (CORIOLIS * jnp.sin(latitude(jnp.arange(NY, dtype=jnp.int32), NY)))[:, None]
    block_rows = jnp.arange(row_blocks, dtype=jnp.int32)
    block_cols = jnp.arange(col_blocks, dtype=jnp.int32)
    source = unit_vectors(latitude(jnp.repeat(block_rows, col_blocks), row_blocks), longitude(jnp.tile(block_cols, row_blocks), col_blocks))
    target_lon = longitude(block_cols, col_blocks)
    height, east_now, north_now = (elevation, east_velocity, north_velocity)
    loading = jnp.zeros((MEMBERS, row_blocks, col_blocks), jnp.float32)
    for interval in range(INTERVALS):
        block_loads = coarse_loads(height, ocean).reshape(MEMBERS, row_blocks * col_blocks).astype(jnp.float32)

        def target_row(row_index):
            row_ids = jnp.zeros((col_blocks,), jnp.int32) + row_index
            target = unit_vectors(latitude(row_ids, row_blocks), target_lon)
            green = green_block(source, target, row_blocks).astype(jnp.float32)
            return jnp.dot(block_loads, green, precision=lax.Precision.HIGHEST)
        loading = jnp.transpose(lax.map(target_row, block_rows), (1, 0, 2))
        fine_sal = refine(loading)
        for substep in range(STEPS):
            effective = zero_north(wrap_east(height - fine_sal))
            east_next, north_next = velocities(effective, east_now, north_now, ocean, turning)
            east_rim = wrap_east(water_depth * east_next)
            north_rim = zero_north(water_depth * north_next)
            height = surface_update(height, east_rim, north_rim, ocean)
            east_now, north_now = (east_next, north_next)
    return (height, east_now, north_now, loading)
```

```python
import functools
import math

import jax
import jax.numpy as jnp
from jax import lax
from jax.experimental import pallas as pl
from jax.experimental.pallas import tpu as pltpu
from jax.sharding import PartitionSpec as P

STEPS = 4
INTERVALS = 2
BLOCK = 8
HALO = 2 * STEPS

COURANT = 0.35
FRICTION = 0.02
CORIOLIS = 0.3
GREEN_SCALE = 0.25
KEEP = 1.0 - FRICTION
HALF = 0.5 * COURANT

MESH = pl.DeviceIdType.MESH
F32 = jnp.float32
BF16 = jnp.bfloat16
DIRS = ((0, 1), (0, -1), (1, 0), (-1, 0), (1, 1), (1, -1), (-1, 1), (-1, -1))

SIDE = 8
SLOTS = 9


def iota(shape, dim):
    return lax.broadcasted_iota(jnp.int32, shape, dim)


def latitude(row_ids, row_count):
    return ((row_ids.astype(F32) + 0.5) / row_count - 0.5) * jnp.pi


def longitude(col_ids, col_count):
    return (col_ids.astype(F32) + 0.5) / col_count * (2.0 * jnp.pi)


def unit_vectors(lat_angle, lon_angle):
    cos_lat = jnp.cos(lat_angle)
    return (cos_lat * jnp.cos(lon_angle), cos_lat * jnp.sin(lon_angle), jnp.sin(lat_angle))


def lanes():
    return iota((8, 128), 1)


def pick(x, index):
    return jnp.take_along_axis(x, index, axis=1)


def exchange(values):
    lane = lanes()
    values = list(values)
    for bit in range(3):
        step = 1 << bit
        low = (lane & step) == 0
        index = lane ^ step
        for a in range(8):
            if a & step:
                continue
            b = a | step
            moved = pick(jnp.where(low, values[b], values[a]), index)
            values[a], values[b] = jnp.where(low, values[a], moved), jnp.where(low, moved, values[b])
    return values


def band(t):
    return pl.ds(BLOCK + t * BLOCK, BLOCK)


def shifted(t, by):
    return pl.ds(BLOCK + t * BLOCK + by, BLOCK)


def x_differences(values, with_side=True):
    lane = lanes()
    first, last = lane < 8, lane >= 120
    edge_east, edge_west = pltpu.roll(values[7], 8, 1), pltpu.roll(values[0], 120, 1)
    side = values[SIDE]
    left = [jnp.where(first, pltpu.roll(side, 8, 1), edge_east)] + values[:7]
    right = values[1:8] + [jnp.where(last, pltpu.roll(side, 120, 1), edge_west)]
    if with_side:
        left.append(jnp.where(first, edge_east, pltpu.roll(side, 16, 1)))
        right.append(jnp.where(last, edge_west, pltpu.roll(side, 112, 1)))
    return [r - l for l, r in zip(left, right)]


def move_flow(tiles, n, last, eta, p_in, q_in, p_out, q_out, depth, turn):
    for t in range(tiles):
        inner = not last or 0 < t < tiles - 1
        coriolis = turn[t]
        if inner:
            diff = x_differences([eta[j, band(t), :] for j in range(SLOTS)])
        for j in range(SLOTS if inner else SIDE):
            d = depth[n, j, t * BLOCK : (t + 1) * BLOCK, :]
            p, q = p_in[j, band(t), :], q_in[j, band(t), :]
            if inner:
                p_out[j, band(t), :] = p + coriolis * q - d * diff[j]
            north = eta[j, shifted(t, 1), :] - eta[j, shifted(t, -1), :]
            q_out[j, band(t), :] = q - coriolis * p - d * north


def surface_change(t, n, with_side, p, q, wet):
    diff = x_differences([p[j, band(t), :] for j in range(SLOTS)], with_side)
    return [
        wet[n, j, t * BLOCK : (t + 1) * BLOCK, :]
        * (diff[j] + (q[j, shifted(t, 1), :] - q[j, shifted(t, -1), :]))
        for j in range(SLOTS if with_side else SIDE)
    ]


def move_surface(tiles, n, eta_in, eta_out, p, q, wet):
    for t in range(tiles):
        change = surface_change(t, n, True, p, q, wet)
        for j in range(SLOTS):
            eta_out[j, band(t), :] = eta_in[j, band(t), :] - change[j]


def kernel(
    nx, ny, members, rows, cols,
    h_in, u_in, v_in, d_in, o_in,
    eta, pp, qq, depth1, wet1, turn, restore, fine, l_out,
    in3, in_d, in_o, strips, land, slab_out, slab, st, st_land, st_ns, base, depth0, wet0, green, tiles,
    in_sem, gs_sem, gr_sem, hs_sem, hr_sem, ss_sem, sr_sem,
):
    gx, gy = lax.axis_index("gx"), lax.axis_index("gy")
    n = nx * ny
    rb_own, cb_own = rows // BLOCK, cols // BLOCK
    per_device = rb_own * cb_own
    pair_rows = 2 * per_device
    coarse_rows, coarse_cols = rb_own * ny, cb_own * nx
    ext = rows + 2 * HALO
    ext_tiles = ext // BLOCK
    my_slot = ((gx // 2) * ny + gy) * 2 + gx % 2
    fields = (eta, pp, qq)

    inputs = [
        pltpu.make_async_copy(src, dst, in_sem.at[k])
        for k, (src, dst) in enumerate(
            ((d_in, in_d), (o_in, in_o), (h_in, in3.at[0]), (u_in, in3.at[1]), (v_in, in3.at[2]))
        )
    ]
    for copy in inputs:
        copy.start()

    def wrap(index, size):
        return jnp.where(index >= size, index - size, index)

    def to_all_others(fn):
        others = [wrap(gy + dy, ny) for dy in range(ny)]
        for y in others[1:]:
            fn({"gx": gx, "gy": y})

        def column(dx, carry):
            x = wrap(gx + dx, nx)
            for y in others:
                fn({"gx": x, "gy": y})
            return carry

        lax.fori_loop(1, nx, column, 0)

    barrier = pltpu.get_barrier_semaphore()

    to_all_others(
        lambda device: pl.semaphore_signal(barrier, inc=1, device_id=device, device_id_type=MESH)
    )

    def target_of(dx, dy):
        return {"gx": wrap(jnp.where(gx + dx < 0, gx + dx + nx, gx + dx), nx), "gy": gy + dy}

    def when(dy, sending, fn):
        if dy == 0:
            fn()
        else:
            beyond = gy + (dy if sending else -dy)
            pl.when((beyond >= 0) & (beyond < ny))(fn)

    def static_copy(k):
        dx, dy = DIRS[k]
        side = 0 if dx > 0 else 1
        if dy == 0:
            src, dst = st, st_land.at[side, pl.ds(HALO, rows)]
        else:
            src = st.at[pl.ds(rows - HALO if dy > 0 else 0, HALO)]
            at = 0 if dy > 0 else HALO + rows
            dst = st_ns.at[0 if dy > 0 else 1] if dx == 0 else st_land.at[side, pl.ds(at, HALO)]
        return pltpu.make_async_remote_copy(
            src_ref=src, dst_ref=dst, send_sem=ss_sem.at[k], recv_sem=sr_sem.at[k],
            device_id=target_of(dx, dy), device_id_type=MESH,
        )

    def halo_copy(i, k):
        dx, dy = DIRS[k]
        side = 0 if dx > 0 else 1
        if dx == 0:
            at = 0 if dy > 0 else 1
            src, dst = slab_out.at[i, at], slab.at[i, at]
        elif dy == 0:
            src, dst = strips.at[i], land.at[i, side, :, pl.ds(1, rb_own)]
        else:
            src = strips.at[i, :, pl.ds(rb_own - 1 if dy > 0 else 0, 1)]
            dst = land.at[i, side, :, pl.ds(0 if dy > 0 else ext_tiles - 1, 1)]
        return pltpu.make_async_remote_copy(
            src_ref=src, dst_ref=dst, send_sem=hs_sem.at[i, k], recv_sem=hr_sem.at[i, k],
            device_id=target_of(dx, dy), device_id_type=MESH,
        )

    def clear(side):
        at = 0 if side == 0 else ext_tiles - 1
        slab[:, side] = jnp.zeros_like(slab[:, side])
        land[:, :, :, at] = jnp.zeros_like(land[:, :, :, at])
        st_ns[side] = jnp.zeros_like(st_ns[side])
        st_land[:, at * BLOCK : (at + 1) * BLOCK] = jnp.zeros((2, HALO, cols), F32)

    pl.when(gy == 0)(lambda: clear(0))
    pl.when(gy == ny - 1)(lambda: clear(1))

    lane = lanes()
    sub = iota((8, 128), 0)

    def put_base(t, source, slots):
        for j in slots:
            base[j, t * BLOCK : (t + 1) * BLOCK, :] = pick(source, (lane & -8) + j)

    def send_loads(i, sums):
        spread = None
        for t, total in enumerate(sums):
            total = jnp.broadcast_to(jnp.sum(total, axis=0, keepdims=True), (8, 128)) * (1.0 / (BLOCK * HALF))
            mine = pick(total, (lane & 15) * 8 + sub)
            here = lane // cb_own == t + rb_own * (gx % 2)
            spread = jnp.where(here, mine, 0.0 if spread is None else spread)
        tiles[i, my_slot] = spread.astype(BF16)

    def pack(i, f):
        ref = fields[f]
        for at, t in enumerate((rb_own, 1)):
            for k in range(4):
                both = jnp.concatenate([ref[2 * k, band(t), :], ref[2 * k + 1, band(t), :]], axis=0)
                slab_out[i, at, f, k] = both.astype(BF16)
        packed = [None] * rb_own
        for j in range(8):
            index = (lane + (128 - 16 * j - 8)) & 127
            for b in range(rb_own):
                moved = pick(ref[j, band(b + 1), :], index)
                packed[b] = moved if j == 0 else jnp.where(lane // 16 == j, moved, packed[b])
        for b in range(rb_own):
            strips[i, f, b] = packed[b]

    def assemble(i):
        west = (lane & 8) != 0
        for f, ref in enumerate(fields):
            for t in range(ext_tiles):
                both = jnp.where(west, land[i, 1, f, t], land[i, 0, f, t])
                ref[SIDE, band(t), :] = pick(both, lane ^ 8)
            for at, t in enumerate((0, ext_tiles - 1)):
                for k in range(4):
                    both = slab[i, at, f, k].astype(F32)
                    ref[2 * k, band(t), :] = both[:8]
                    ref[2 * k + 1, band(t), :] = both[8:]

    def tables(first, depth, wet):
        def fill(t, carry):
            part = pl.ds(t * BLOCK, BLOCK)
            for j in range(SLOTS):
                d = base[j, part, :]
                w = jnp.where(d > 0.0, 1.0, 0.0)
                for k in range(STEPS):
                    depth[k, j, part, :] = d * KEEP ** -(first + k + 1)
                    wet[k, j, part, :] = w * KEEP ** (first + k + 1)
            return carry

        lax.fori_loop(0, ext_tiles, fill, 0)

    def start_interval(i):
        def send(device):
            pltpu.make_async_remote_copy(
                src_ref=tiles.at[i, my_slot], dst_ref=tiles.at[i, my_slot],
                send_sem=gs_sem.at[i], recv_sem=gr_sem.at[i],
                device_id=device, device_id_type=MESH,
            ).start()

        to_all_others(send)

    def start_halos(i):
        for k in range(len(DIRS)):
            when(DIRS[k][1], True, lambda k=k: halo_copy(i, k).start())

    def wait_halos(i):
        for k in range(len(DIRS)):
            when(DIRS[k][1], False, lambda k=k: halo_copy(i, k).wait_recv())

    def finish_sends(i):
        for k in range(len(DIRS)):
            when(DIRS[k][1], True, lambda k=k: halo_copy(i, k).wait_send())

    def everyone(i):
        return pltpu.make_async_remote_copy(
            src_ref=tiles.at[i, pl.ds(0, n - 1)], dst_ref=tiles.at[i, pl.ds(0, n - 1)],
            send_sem=gs_sem.at[i], recv_sem=gr_sem.at[i],
            device_id=target_of(1, 0), device_id_type=MESH,
        )

    def make_turning():
        for e in range(ext_tiles):
            row_ids = gy * rows - HALO + e * BLOCK + iota((BLOCK, cols), 0)
            turn[e] = (CORIOLIS / KEEP) * jnp.sin(latitude(row_ids, rows * ny))

    def make_green():
        t = iota((8, 128), 1)
        north = per_device
        south = north + cb_own
        west = south + cb_own
        east = west + rb_own + 2
        t_row = jnp.where(t < north, t // cb_own, jnp.where(t < south, -1, rb_own))
        t_col = jnp.where(t < north, t % cb_own, jnp.where(t < south, t - north, t - south))
        t_row = jnp.where(t >= east, t - east - 1, jnp.where(t >= west, t - west - 1, t_row))
        t_col = jnp.where(t >= east, cb_own, jnp.where(t >= west, -1, t_col))
        t_row = gy * rb_own + t_row
        t_col = gx * cb_own + t_col
        t_col = jnp.where(t_col < 0, t_col + coarse_cols, t_col)
        t_col = jnp.where(t_col >= coarse_cols, t_col - coarse_cols, t_col)
        target = unit_vectors(latitude(t_row, coarse_rows), longitude(t_col, coarse_cols))
        target = [jnp.broadcast_to(x[:1], (pair_rows, 128)) for x in target]

        def green_group(g, carry):
            p = g * 8 + iota((8, pair_rows), 0)
            k = iota((8, pair_rows), 1)
            s_col = ((p // ny) * 2 + k // per_device) * cb_own + k % cb_own
            s_row = (p % ny) * rb_own + (k % per_device) // cb_own
            source = unit_vectors(latitude(s_row, coarse_rows), longitude(s_col, coarse_cols))
            source = [jnp.transpose(x) for x in source]
            for j in range(8):
                square = None
                for s, t_vec in zip(source, target):
                    diff = jnp.broadcast_to(s[:, j : j + 1], (pair_rows, 128)) - t_vec
                    square = diff * diff if square is None else square + diff * diff
                value = GREEN_SCALE / (1.0 + jnp.sqrt(square) * (coarse_rows / math.pi))
                green[g * 8 + j] = value.astype(BF16)
            return carry

        lax.fori_loop(0, n // 16, green_group, 0)

    def finish_base():
        scale = HALF * HALF
        for t, side in ((0, 0), (ext_tiles - 1, 1)):
            put_base(t, st_ns[side] * scale, range(8))
        for t in range(ext_tiles):
            part = slice(t * BLOCK, (t + 1) * BLOCK)
            east = pick(st_land[1, part], lane // 16)
            west = pick(st_land[0, part], lane // 16 + (cols - 8))
            base[SIDE, part, :] = jnp.where((lane & 8) != 0, west, east) * scale

    def load(i):
        group = 16 if n // 2 % 16 == 0 else 1

        def add_group(g, total):
            for j in range(group):
                p = g * group + j
                tile = tiles[i, 2 * p].astype(F32) + tiles[i, 2 * p + 1].astype(F32)
                total = total + jnp.dot(tile.astype(BF16), green[p], preferred_element_type=F32)
            return total

        loading = lax.fori_loop(0, n // 2 // group, add_group, jnp.zeros((members, 128), F32))
        l_out[...] = loading
        loading = loading * HALF
        north = per_device
        south = north + cb_own
        west = south + cb_own
        east = west + rb_own + 2
        own_member = (lane & 7) == sub
        for t in range(ext_tiles):
            first = north if t == 0 else south if t == ext_tiles - 1 else (t - 1) * cb_own
            main = pick(loading, lane // 8 + first)
            side = pick(loading, jnp.where((lane & 8) != 0, west + t, east + t))
            both = []
            for value in (main, side):
                value = jnp.where(own_member, value, 0.0)
                if t == 0:
                    value = jnp.where(gy == 0, 0.0, value)
                if t == ext_tiles - 1:
                    value = jnp.where(gy == ny - 1, 0.0, value)
                both.append(jnp.broadcast_to(jnp.sum(value, axis=0, keepdims=True), (8, 128)))
            fine[t] = both[0]
            for j in range(8):
                eta[j, band(t), :] = eta[j, band(t), :] - both[0]
            eta[SIDE, band(t), :] = eta[SIDE, band(t), :] - both[1]

    def interval(i):
        def step(n, carry):
            move_flow(ext_tiles, n, False, eta, pp, qq, pp, qq, depth0, turn)
            move_surface(ext_tiles, n, eta, eta, pp, qq, wet0)
            return carry

        lax.fori_loop(0, STEPS - 1, step, 0)
        move_flow(ext_tiles, STEPS - 1, True, eta, pp, qq, pp, qq, depth0, turn)
        sums = []
        for t in range(1, ext_tiles - 1):
            change = surface_change(t, STEPS - 1, False, pp, qq, wet0)
            total = None
            for j in range(8):
                value = eta[j, band(t), :] - change[j] + fine[t]
                eta[j, band(t), :] = value
                value = value * wet0[STEPS - 1, j, t * BLOCK : (t + 1) * BLOCK, :]
                total = value if total is None else total + value
            sums.append(total * KEEP ** -STEPS)
        return sums

    for copy in inputs[:3]:
        copy.wait()
    st[...] = jnp.where(in_o[...] > 0, in_d[...], 0.0)
    sums = []
    for t in range(1, ext_tiles - 1):
        part = slice((t - 1) * BLOCK, t * BLOCK)
        put_base(t, st[part, :] * (HALF * HALF), range(8))
        total = None
        for j, value in enumerate(exchange([in3[0, m, part, :] for m in range(8)])):
            value = value * HALF
            eta[j, band(t), :] = value
            value = jnp.where(base[j, t * BLOCK : (t + 1) * BLOCK, :] > 0.0, value, 0.0)
            total = value if total is None else total + value
        sums.append(total)
    send_loads(0, sums)
    for copy in inputs[3:]:
        copy.wait()
    for f in (1, 2):
        for t in range(1, ext_tiles - 1):
            part = slice((t - 1) * BLOCK, t * BLOCK)
            for j, value in enumerate(exchange([in3[f, m, part, :] for m in range(8)])):
                fields[f][j, band(t), :] = value * base[j, t * BLOCK : (t + 1) * BLOCK, :]
    for f in range(3):
        pack(0, f)
    pl.semaphore_wait(barrier, n - 1)
    start_interval(0)
    for k, (dx, dy) in enumerate(DIRS):
        when(dy, True, lambda k=k: static_copy(k).start())
    start_halos(0)

    make_turning()
    make_green()
    for k, (dx, dy) in enumerate(DIRS):
        when(dy, False, lambda k=k: static_copy(k).wait_recv())
    finish_base()
    tables(0, depth0, wet0)
    wait_halos(0)
    assemble(0)
    everyone(0).wait_recv()
    load(0)
    send_loads(1, interval(0))
    start_interval(1)
    for f in range(3):
        pack(1, f)
    start_halos(1)
    tables(STEPS, depth1, wet1)
    for j in range(8):
        d = base[j, BLOCK : BLOCK + rows, :]
        restore[j] = jnp.where(d > 0.0, KEEP ** (2 * STEPS) / jnp.where(d > 0.0, d, 1.0), 0.0)
    for k, (dx, dy) in enumerate(DIRS):
        when(dy, True, lambda k=k: static_copy(k).wait_send())
    everyone(0).wait_send()
    finish_sends(0)
    wait_halos(1)
    assemble(1)
    everyone(1).wait_recv()
    load(1)
    finish_sends(1)
    everyone(1).wait_send()


def finish(
    members, rows, cols,
    eta_in, p_in, q_in, depth, wet, turn, restore, fine, l_in,
    h_out, u_out, v_out, l_out,
    eta, pp, qq, staged, l_staged, sem,
):
    ext_tiles = (rows + 2 * HALO) // BLOCK
    blocks, width = l_staged.shape[1:]
    for b in range(blocks):
        l_staged[:, b, :] = l_in[:, b * width : (b + 1) * width]
    l_copy = pltpu.make_async_copy(l_staged, l_out, sem.at[3])
    l_copy.start()

    move_flow(ext_tiles, 0, False, eta_in, p_in, q_in, pp, qq, depth, turn)
    move_surface(ext_tiles, 0, eta_in, eta, pp, qq, wet)

    def step(n, carry):
        move_flow(ext_tiles, n, False, eta, pp, qq, pp, qq, depth, turn)
        move_surface(ext_tiles, n, eta, eta, pp, qq, wet)
        return carry

    lax.fori_loop(1, STEPS - 1, step, 0)
    move_flow(ext_tiles, STEPS - 1, True, eta, pp, qq, pp, qq, depth, turn)
    copies = [pltpu.make_async_copy(staged.at[f], out, sem.at[f]) for f, out in enumerate((h_out, u_out, v_out))]

    def place(f, t, values):
        for m, value in enumerate(exchange(values)):
            staged[f, m, (t - 1) * BLOCK : t * BLOCK, :] = value

    for f, ref in ((1, pp), (2, qq)):
        for t in range(1, ext_tiles - 1):
            part = slice((t - 1) * BLOCK, t * BLOCK)
            place(f, t, [ref[j, band(t), :] * restore[j, part, :] for j in range(8)])
        copies[f].start()
    for t in range(1, ext_tiles - 1):
        change = surface_change(t, STEPS - 1, False, pp, qq, wet)
        place(0, t, [(eta[j, band(t), :] - change[j] + fine[t]) * (1.0 / HALF) for j in range(8)])
    copies[0].start()
    for copy in copies:
        copy.wait()
    l_copy.wait()


def shards(nx, ny, elevation, east_velocity, north_velocity, water_depth, land_sea):
    members, rows, cols = elevation.shape
    rb_own, cb_own = rows // BLOCK, cols // BLOCK
    n = nx * ny
    ext = rows + 2 * HALO
    tiles = ext // BLOCK
    hbm_spec = pl.BlockSpec(memory_space=pltpu.HBM)
    vmem_spec = pl.BlockSpec(memory_space=pltpu.VMEM)
    dma = pltpu.SemaphoreType.DMA
    field = (SLOTS, ext + 2 * BLOCK, cols)
    table = (STEPS, SLOTS, ext, cols)
    shape = (members, rows, cols)
    outs = tuple(
        jax.ShapeDtypeStruct(s, F32)
        for s in (
            field, field, field, table, table, (tiles, BLOCK, cols), (8, rows, cols), (tiles, BLOCK, cols),
            (members, 128),
        )
    )
    state = pl.pallas_call(
        functools.partial(kernel, nx, ny, members, rows, cols),
        out_shape=outs,
        in_specs=[hbm_spec] * 5,
        out_specs=(vmem_spec,) * len(outs),
        scratch_shapes=[
            pltpu.VMEM((3,) + shape, F32),
            pltpu.VMEM((rows, cols), F32),
            pltpu.VMEM((rows, cols), jnp.int32),
            pltpu.VMEM((INTERVALS, 3, rb_own, 8, cols), F32),
            pltpu.VMEM((INTERVALS, 2, 3, tiles, 8, cols), F32),
            pltpu.VMEM((INTERVALS, 2, 3, 4, 16, cols), BF16),
            pltpu.VMEM((INTERVALS, 2, 3, 4, 16, cols), BF16),
            pltpu.VMEM((rows, cols), F32),
            pltpu.VMEM((2, ext, cols), F32),
            pltpu.VMEM((2, HALO, cols), F32),
            pltpu.VMEM((SLOTS, ext, cols), F32),
            pltpu.VMEM(table, F32),
            pltpu.VMEM(table, F32),
            pltpu.VMEM((n // 2, 2 * rb_own * cb_own, 128), BF16),
            pltpu.VMEM((INTERVALS, n, members, 2 * rb_own * cb_own), BF16),
            dma((5,)),
            dma((INTERVALS,)),
            dma((INTERVALS,)),
            dma((INTERVALS, len(DIRS))),
            dma((INTERVALS, len(DIRS))),
            dma((len(DIRS),)),
            dma((len(DIRS),)),
        ],
        compiler_params=pltpu.CompilerParams(
            collective_id=0, has_side_effects=True, vmem_limit_bytes=40 * 1024 * 1024
        ),
        name="tide",
    )(
        *(
            pltpu.with_memory_space_constraint(x, pltpu.HBM)
            for x in (elevation, east_velocity, north_velocity, water_depth, land_sea)
        )
    )
    coarse = jax.ShapeDtypeStruct((members, rb_own, cb_own), F32)
    whole = jax.ShapeDtypeStruct(shape, F32)
    return pl.pallas_call(
        functools.partial(finish, members, rows, cols),
        out_shape=(whole, whole, whole, coarse),
        in_specs=[vmem_spec] * len(outs),
        out_specs=(hbm_spec,) * 4,
        scratch_shapes=[
            pltpu.VMEM(field, F32),
            pltpu.VMEM(field, F32),
            pltpu.VMEM(field, F32),
            pltpu.VMEM((3,) + shape, F32),
            pltpu.VMEM(coarse.shape, F32),
            dma((4,)),
        ],
        compiler_params=pltpu.CompilerParams(vmem_limit_bytes=8 * 1024 * 1024),
        name="finish",
    )(*state)


def solution(mesh):
    nx, ny = mesh.shape["gx"], mesh.shape["gy"]
    tile = P(None, "gy", "gx")
    return jax.shard_map(
        functools.partial(shards, nx, ny),
        mesh=mesh,
        in_specs=(tile, tile, tile, P("gy", "gx"), P("gy", "gx")),
        out_specs=(tile, tile, tile, tile),
        check_vma=False,
    )
```

```python
import functools
import math

import jax
import jax.numpy as jnp
from jax import lax
from jax.experimental import pallas as pl
from jax.experimental.pallas import tpu as pltpu
from jax.sharding import PartitionSpec as P

STEPS = 4
INTERVALS = 2
BLOCK = 8
HALO = 2 * STEPS

COURANT = 0.35
FRICTION = 0.02
CORIOLIS = 0.3
GREEN_SCALE = 0.25
KEEP = 1.0 - FRICTION
HALF = 0.5 * COURANT

MESH = pl.DeviceIdType.MESH
F32 = jnp.float32
BF16 = jnp.bfloat16

SIDE = 8
SLOTS = 9


def iota(shape, dim):
    return lax.broadcasted_iota(jnp.int32, shape, dim)


def latitude(row_ids, row_count):
    return ((row_ids.astype(F32) + 0.5) / row_count - 0.5) * jnp.pi


def longitude(col_ids, col_count):
    return (col_ids.astype(F32) + 0.5) / col_count * (2.0 * jnp.pi)


def unit_vectors(lat_angle, lon_angle):
    cos_lat = jnp.cos(lat_angle)
    return (cos_lat * jnp.cos(lon_angle), cos_lat * jnp.sin(lon_angle), jnp.sin(lat_angle))


def lanes():
    return iota((8, 128), 1)


def pick(x, index):
    return jnp.take_along_axis(x, index, axis=1)


def exchange(values):
    lane = lanes()
    values = list(values)
    for bit in range(3):
        step = 1 << bit
        low = (lane & step) == 0
        index = lane ^ step
        for a in range(8):
            if a & step:
                continue
            b = a | step
            moved = pick(jnp.where(low, values[b], values[a]), index)
            values[a], values[b] = jnp.where(low, values[a], moved), jnp.where(low, moved, values[b])
    return values


def band(t):
    return pl.ds(BLOCK + t * BLOCK, BLOCK)


def shifted(t, by):
    return pl.ds(BLOCK + t * BLOCK + by, BLOCK)


def x_differences(values, with_side=True):
    lane = lanes()
    first, last = lane < 8, lane >= 120
    edge_east, edge_west = pltpu.roll(values[7], 8, 1), pltpu.roll(values[0], 120, 1)
    side = values[SIDE]
    left = [jnp.where(first, pltpu.roll(side, 8, 1), edge_east)] + values[:7]
    right = values[1:8] + [jnp.where(last, pltpu.roll(side, 120, 1), edge_west)]
    if with_side:
        left.append(jnp.where(first, edge_east, pltpu.roll(side, 16, 1)))
        right.append(jnp.where(last, edge_west, pltpu.roll(side, 112, 1)))
    return [r - l for l, r in zip(left, right)]


def move_flow(tiles, n, last, eta, p_in, q_in, p_out, q_out, depth, turn):
    for t in range(tiles):
        inner = not last or 0 < t < tiles - 1
        coriolis = turn[t]
        if inner:
            diff = x_differences([eta[j, band(t), :] for j in range(SLOTS)])
        for j in range(SLOTS if inner else SIDE):
            d = depth[n, j, t * BLOCK : (t + 1) * BLOCK, :]
            p, q = p_in[j, band(t), :], q_in[j, band(t), :]
            if inner:
                p_out[j, band(t), :] = p + coriolis * q - d * diff[j]
            north = eta[j, shifted(t, 1), :] - eta[j, shifted(t, -1), :]
            q_out[j, band(t), :] = q - coriolis * p - d * north


def surface_change(t, n, with_side, p, q, wet):
    diff = x_differences([p[j, band(t), :] for j in range(SLOTS)], with_side)
    return [
        wet[n, j, t * BLOCK : (t + 1) * BLOCK, :]
        * (diff[j] + (q[j, shifted(t, 1), :] - q[j, shifted(t, -1), :]))
        for j in range(SLOTS if with_side else SIDE)
    ]


def move_surface(tiles, n, eta_in, eta_out, p, q, wet):
    for t in range(tiles):
        change = surface_change(t, n, True, p, q, wet)
        for j in range(SLOTS):
            eta_out[j, band(t), :] = eta_in[j, band(t), :] - change[j]


def kernel(
    nx, ny, members, rows, cols,
    h_in, u_in, v_in, d_in, o_in,
    eta, pp, qq, depth1, wet1, turn, restore, fine, l_out,
    in3, in_d, in_o, strips, land, slab_out, slab, counted, st, base, depth0, wet0, green, tiles,
    in_sem, gs_sem, gr_sem, hs_sem, hr_sem,
):
    gx, gy = lax.axis_index("gx"), lax.axis_index("gy")
    n = nx * ny
    rb_own, cb_own = rows // BLOCK, cols // BLOCK
    per_device = rb_own * cb_own
    pair_rows = 2 * per_device
    coarse_rows, coarse_cols = rb_own * ny, cb_own * nx
    ext = rows + 2 * HALO
    ext_tiles = ext // BLOCK
    my_slot = ((gx // 2) * ny + gy) * 2 + gx % 2
    fields = (eta, pp, qq)

    inputs = [
        pltpu.make_async_copy(src, dst, in_sem.at[k])
        for k, (src, dst) in enumerate(
            ((d_in, in_d), (o_in, in_o), (h_in, in3.at[0]), (u_in, in3.at[1]), (v_in, in3.at[2]))
        )
    ]
    for copy in inputs:
        copy.start()

    def wrap(index, size):
        return jnp.where(index >= size, index - size, index)

    def to_all_others(fn):
        others = [wrap(gy + dy, ny) for dy in range(ny)]
        for y in others[1:]:
            fn({"gx": gx, "gy": y})

        def column(dx, carry):
            x = wrap(gx + dx, nx)
            for y in others:
                fn({"gx": x, "gy": y})
            return carry

        lax.fori_loop(1, nx, column, 0)

    barrier = pltpu.get_barrier_semaphore()

    to_all_others(
        lambda device: pl.semaphore_signal(barrier, inc=1, device_id=device, device_id_type=MESH)
    )

    def target_of(dx, dy):
        return {"gx": wrap(jnp.where(gx + dx < 0, gx + dx + nx, gx + dx), nx), "gy": gy + dy}

    def when(dy, sending, fn):
        if dy == 0:
            fn()
        else:
            beyond = gy + (dy if sending else -dy)
            pl.when((beyond >= 0) & (beyond < ny))(fn)

    planes, layers = (5, 3), (13, 12)

    def remote(src, dst, i, group, dx, dy):
        return pltpu.make_async_remote_copy(
            src_ref=src, dst_ref=dst, send_sem=hs_sem.at[i, group], recv_sem=hr_sem.at[i, group],
            device_id=target_of(dx, dy), device_id_type=MESH,
        )

    def beside(i, dx):
        part = pl.ds(0, planes[i])
        return remote(
            strips.at[i, :, part], land.at[i, 0 if dx > 0 else 1, pl.ds(1, rb_own), part], i, 0, dx, 0
        )

    def beside_all(i):
        both = land.at[i, :, pl.ds(1, rb_own), pl.ds(0, planes[i])]
        return remote(both, both, i, 0, 1, 0)

    def start_beyond(i, dy):
        at, group = (0, 1) if dy > 0 else (1, 2)
        part, rest = pl.ds(0, planes[i]), pl.ds(0, layers[i])
        remote(slab_out.at[i, at, rest], slab.at[i, at, rest], i, group, 0, dy).start()
        for dx in (1, -1):
            src = strips.at[i, pl.ds(rb_own - 1 if dy > 0 else 0, 1), part]
            dst = land.at[i, 0 if dx > 0 else 1, pl.ds(0 if dy > 0 else ext_tiles - 1, 1), part]
            remote(src, dst, i, group, dx, dy).start()

    def beyond_all(i, dy):
        every = counted.at[pl.ds(0, layers[i] + planes[i])]
        return remote(every, every, i, 1 if dy > 0 else 2, 1, 0)

    def clear(side):
        at = 0 if side == 0 else ext_tiles - 1
        slab[:, side] = jnp.zeros_like(slab[:, side])
        land[:, :, at] = jnp.zeros_like(land[:, :, at])

    pl.when(gy == 0)(lambda: clear(0))
    pl.when(gy == ny - 1)(lambda: clear(1))

    lane = lanes()
    sub = iota((8, 128), 0)

    def put_base(t, source, slots):
        for j in slots:
            base[j, band(t), :] = pick(source, (lane & -8) + j)

    def send_loads(i, sums):
        spread = None
        for t, total in enumerate(sums):
            total = jnp.broadcast_to(jnp.sum(total, axis=0, keepdims=True), (8, 128)) * (1.0 / (BLOCK * HALF))
            mine = pick(total, (lane & 15) * 8 + sub)
            here = lane // cb_own == t + rb_own * (gx % 2)
            spread = jnp.where(here, mine, 0.0 if spread is None else spread)
        tiles[i, my_slot] = spread.astype(BF16)

    def two_parts(x):
        high = x.astype(BF16).astype(F32)
        return high, x - high

    def pack(i, f):
        ref = (*fields, base)[f]
        for at, t in enumerate((rb_own, 1)):
            if f == 3:
                edge = two_parts(st[(t - 1) * BLOCK : t * BLOCK, :] * (HALF * HALF))
                slab_out[i, at, 12] = jnp.concatenate(edge, axis=0).astype(BF16)
                continue
            for k in range(4):
                both = jnp.concatenate([ref[2 * k, band(t), :], ref[2 * k + 1, band(t), :]], axis=0)
                slab_out[i, at, 4 * f + k] = both.astype(BF16)
        packed = [None] * rb_own
        for j in range(8):
            index = (lane + (128 - 16 * j - 8)) & 127
            for b in range(rb_own):
                moved = pick(ref[j, band(b + 1), :], index)
                packed[b] = moved if j == 0 else jnp.where(lane // 16 == j, moved, packed[b])
        for b in range(rb_own):
            parts = two_parts(packed[b]) if f == 3 else (packed[b],)
            for k, part in enumerate(parts):
                strips[i, b, f + k] = part.astype(BF16)

    def side_of(i, t, planes):
        west, east = (sum(land[i, side, t, k].astype(F32) for k in planes) for side in (0, 1))
        return pick(jnp.where((lane & 8) != 0, east, west), lane ^ 8)

    def assemble(i):
        for f, ref in enumerate(fields):
            for t in range(ext_tiles):
                ref[SIDE, band(t), :] = side_of(i, t, (f,))
            for at, t in enumerate((0, ext_tiles - 1)):
                for k in range(4):
                    both = slab[i, at, 4 * f + k].astype(F32)
                    ref[2 * k, band(t), :] = both[:8]
                    ref[2 * k + 1, band(t), :] = both[8:]

    def finish_base():
        for at, t in enumerate((0, ext_tiles - 1)):
            both = slab[0, at, 12].astype(F32)
            put_base(t, both[:8] + both[8:], range(8))
        for t in range(ext_tiles):
            base[SIDE, band(t), :] = side_of(0, t, (3, 4))

    def table(j, t, first, depth, wet):
        d = base[j, band(t), :]
        w = jnp.where(d > 0.0, 1.0, 0.0)
        part = pl.ds(t * BLOCK, BLOCK)
        for k in range(STEPS):
            depth[k, j, part, :] = d * KEEP ** -(first + k + 1)
            wet[k, j, part, :] = w * KEEP ** (first + k + 1)

    def own_tables(first, depth, wet):
        def fill(t, carry):
            for j in range(8):
                table(j, t, first, depth, wet)
            return carry

        lax.fori_loop(1, ext_tiles - 1, fill, 0)

    def edge_tables(first, depth, wet):
        for t in range(ext_tiles):
            for j in range(8) if t in (0, ext_tiles - 1) else ():
                table(j, t, first, depth, wet)
            table(SIDE, t, first, depth, wet)

    def start_interval(i):
        def send(device):
            pltpu.make_async_remote_copy(
                src_ref=tiles.at[i, my_slot], dst_ref=tiles.at[i, my_slot],
                send_sem=gs_sem.at[i], recv_sem=gr_sem.at[i],
                device_id=device, device_id_type=MESH,
            ).start()

        to_all_others(send)

    def start_halos(i):
        for dx in (1, -1):
            beside(i, dx).start()
        for dy in (1, -1):
            when(dy, True, lambda dy=dy: start_beyond(i, dy))

    def wait_halos(i):
        beside_all(i).wait_recv()
        for dy in (1, -1):
            when(dy, False, lambda dy=dy: beyond_all(i, dy).wait_recv())

    def finish_sends(i):
        beside_all(i).wait_send()
        for dy in (1, -1):
            when(dy, True, lambda dy=dy: beyond_all(i, dy).wait_send())

    def everyone(i):
        return pltpu.make_async_remote_copy(
            src_ref=tiles.at[i, pl.ds(0, n - 1)], dst_ref=tiles.at[i, pl.ds(0, n - 1)],
            send_sem=gs_sem.at[i], recv_sem=gr_sem.at[i],
            device_id=target_of(1, 0), device_id_type=MESH,
        )

    def make_turning():
        for e in range(ext_tiles):
            row_ids = gy * rows - HALO + e * BLOCK + iota((BLOCK, cols), 0)
            turn[e] = (CORIOLIS / KEEP) * jnp.sin(latitude(row_ids, rows * ny))

    def make_green():
        t = iota((8, 128), 1)
        north = per_device
        south = north + cb_own
        west = south + cb_own
        east = west + rb_own + 2
        t_row = jnp.where(t < north, t // cb_own, jnp.where(t < south, -1, rb_own))
        t_col = jnp.where(t < north, t % cb_own, jnp.where(t < south, t - north, t - south))
        t_row = jnp.where(t >= east, t - east - 1, jnp.where(t >= west, t - west - 1, t_row))
        t_col = jnp.where(t >= east, cb_own, jnp.where(t >= west, -1, t_col))
        t_row = gy * rb_own + t_row
        t_col = gx * cb_own + t_col
        t_col = jnp.where(t_col < 0, t_col + coarse_cols, t_col)
        t_col = jnp.where(t_col >= coarse_cols, t_col - coarse_cols, t_col)
        target = unit_vectors(latitude(t_row, coarse_rows), longitude(t_col, coarse_cols))
        target = [jnp.broadcast_to(x[:1], (pair_rows, 128)) for x in target]

        def green_group(g, carry):
            p = g * 8 + iota((8, pair_rows), 0)
            k = iota((8, pair_rows), 1)
            s_col = ((p // ny) * 2 + k // per_device) * cb_own + k % cb_own
            s_row = (p % ny) * rb_own + (k % per_device) // cb_own
            source = unit_vectors(latitude(s_row, coarse_rows), longitude(s_col, coarse_cols))
            source = [jnp.transpose(x) for x in source]
            for j in range(8):
                square = None
                for s, t_vec in zip(source, target):
                    diff = jnp.broadcast_to(s[:, j : j + 1], (pair_rows, 128)) - t_vec
                    square = diff * diff if square is None else square + diff * diff
                value = GREEN_SCALE / (1.0 + jnp.sqrt(square) * (coarse_rows / math.pi))
                green[g * 8 + j] = value.astype(BF16)
            return carry

        lax.fori_loop(0, n // 16, green_group, 0)

    def load(i):
        half = n // 4
        group = math.gcd(8, half)

        def pair(p):
            return tiles[i, 2 * p].astype(F32) + tiles[i, 2 * p + 1].astype(F32)

        def add_group(g, total):
            left, right = [], []
            for k in range(group):
                q = g * group + k
                left.append(jnp.concatenate([pair(q), pair(q + half)], axis=0).astype(BF16))
                right.append(jnp.concatenate([green[q], green[q + half]], axis=1))
            return total + jnp.dot(
                jnp.concatenate(left, axis=1), jnp.concatenate(right, axis=0), preferred_element_type=F32
            )

        both = lax.fori_loop(0, half // group, add_group, jnp.zeros((2 * members, 256), F32))
        loading = both[:members, :128] + both[members:, 128:]
        l_out[...] = loading
        loading = loading * HALF
        north = per_device
        south = north + cb_own
        west = south + cb_own
        east = west + rb_own + 2
        own_member = (lane & 7) == sub
        for t in range(ext_tiles):
            first = north if t == 0 else south if t == ext_tiles - 1 else (t - 1) * cb_own
            main = pick(loading, lane // 8 + first)
            side = pick(loading, jnp.where((lane & 8) != 0, west + t, east + t))
            both = []
            for value in (main, side):
                value = jnp.where(own_member, value, 0.0)
                if t == 0:
                    value = jnp.where(gy == 0, 0.0, value)
                if t == ext_tiles - 1:
                    value = jnp.where(gy == ny - 1, 0.0, value)
                both.append(jnp.broadcast_to(jnp.sum(value, axis=0, keepdims=True), (8, 128)))
            fine[t] = both[0]
            for j in range(8):
                eta[j, band(t), :] = eta[j, band(t), :] - both[0]
            eta[SIDE, band(t), :] = eta[SIDE, band(t), :] - both[1]

    def interval(i):
        def step(n, carry):
            move_flow(ext_tiles, n, False, eta, pp, qq, pp, qq, depth0, turn)
            move_surface(ext_tiles, n, eta, eta, pp, qq, wet0)
            return carry

        lax.fori_loop(0, STEPS - 1, step, 0)
        move_flow(ext_tiles, STEPS - 1, True, eta, pp, qq, pp, qq, depth0, turn)
        sums = []
        for t in range(1, ext_tiles - 1):
            change = surface_change(t, STEPS - 1, False, pp, qq, wet0)
            total = None
            for j in range(8):
                value = eta[j, band(t), :] - change[j] + fine[t]
                eta[j, band(t), :] = value
                value = value * wet0[STEPS - 1, j, t * BLOCK : (t + 1) * BLOCK, :]
                total = value if total is None else total + value
            sums.append(total * KEEP ** -STEPS)
        return sums

    for copy in inputs[:3]:
        copy.wait()
    st[...] = jnp.where(in_o[...] > 0, in_d[...], 0.0)
    sums = []
    for t in range(1, ext_tiles - 1):
        part = slice((t - 1) * BLOCK, t * BLOCK)
        put_base(t, st[part, :] * (HALF * HALF), range(8))
        total = None
        for j, value in enumerate(exchange([in3[0, m, part, :] for m in range(8)])):
            value = value * HALF
            eta[j, band(t), :] = value
            value = jnp.where(base[j, band(t), :] > 0.0, value, 0.0)
            total = value if total is None else total + value
        sums.append(total)
    send_loads(0, sums)
    for copy in inputs[3:]:
        copy.wait()
    for f in (1, 2):
        for t in range(1, ext_tiles - 1):
            part = slice((t - 1) * BLOCK, t * BLOCK)
            for j, value in enumerate(exchange([in3[f, m, part, :] for m in range(8)])):
                fields[f][j, band(t), :] = value * base[j, band(t), :]
    for f in range(4):
        pack(0, f)
    pl.semaphore_wait(barrier, n - 1)
    start_interval(0)
    start_halos(0)

    make_turning()
    make_green()
    own_tables(0, depth0, wet0)
    wait_halos(0)
    assemble(0)
    finish_base()
    edge_tables(0, depth0, wet0)
    everyone(0).wait_recv()
    load(0)
    send_loads(1, interval(0))
    start_interval(1)
    for f in range(3):
        pack(1, f)
    start_halos(1)
    own_tables(STEPS, depth1, wet1)
    edge_tables(STEPS, depth1, wet1)
    for j in range(8):
        d = base[j, 2 * BLOCK : 2 * BLOCK + rows, :]
        restore[j] = jnp.where(d > 0.0, KEEP ** (2 * STEPS) / jnp.where(d > 0.0, d, 1.0), 0.0)
    everyone(0).wait_send()
    finish_sends(0)
    wait_halos(1)
    assemble(1)
    everyone(1).wait_recv()
    load(1)
    finish_sends(1)
    everyone(1).wait_send()


def finish(
    members, rows, cols,
    eta_in, p_in, q_in, depth, wet, turn, restore, fine, l_in,
    h_out, u_out, v_out, l_out,
    eta, pp, qq, staged, l_staged, sem,
):
    ext_tiles = (rows + 2 * HALO) // BLOCK
    blocks, width = l_staged.shape[1:]
    for b in range(blocks):
        l_staged[:, b, :] = l_in[:, b * width : (b + 1) * width]
    l_copy = pltpu.make_async_copy(l_staged, l_out, sem.at[3])
    l_copy.start()

    move_flow(ext_tiles, 0, False, eta_in, p_in, q_in, pp, qq, depth, turn)
    move_surface(ext_tiles, 0, eta_in, eta, pp, qq, wet)

    def step(n, carry):
        move_flow(ext_tiles, n, False, eta, pp, qq, pp, qq, depth, turn)
        move_surface(ext_tiles, n, eta, eta, pp, qq, wet)
        return carry

    lax.fori_loop(1, STEPS - 1, step, 0)
    move_flow(ext_tiles, STEPS - 1, True, eta, pp, qq, pp, qq, depth, turn)
    copies = [pltpu.make_async_copy(staged.at[f], out, sem.at[f]) for f, out in ((1, u_out), (2, v_out))]
    for t in range(rows // BLOCK):
        part = pl.ds(t * BLOCK, BLOCK)
        copies.append(pltpu.make_async_copy(staged.at[0, :, part], h_out.at[:, part], sem.at[4 + t]))

    def place(f, t, values):
        for m, value in enumerate(exchange(values)):
            staged[f, m, (t - 1) * BLOCK : t * BLOCK, :] = value

    for f, ref in ((1, pp), (2, qq)):
        for t in range(1, ext_tiles - 1):
            part = slice((t - 1) * BLOCK, t * BLOCK)
            place(f, t, [ref[j, band(t), :] * restore[j, part, :] for j in range(8)])
        copies[f - 1].start()
    for t in range(1, ext_tiles - 1):
        change = surface_change(t, STEPS - 1, False, pp, qq, wet)
        place(0, t, [(eta[j, band(t), :] - change[j] + fine[t]) * (1.0 / HALF) for j in range(8)])
        copies[1 + t].start()
    for copy in copies:
        copy.wait()
    l_copy.wait()


def shards(nx, ny, elevation, east_velocity, north_velocity, water_depth, land_sea):
    members, rows, cols = elevation.shape
    rb_own, cb_own = rows // BLOCK, cols // BLOCK
    n = nx * ny
    ext = rows + 2 * HALO
    tiles = ext // BLOCK
    hbm_spec = pl.BlockSpec(memory_space=pltpu.HBM)
    vmem_spec = pl.BlockSpec(memory_space=pltpu.VMEM)
    dma = pltpu.SemaphoreType.DMA
    field = (SLOTS, ext + 2 * BLOCK, cols)
    table = (STEPS, SLOTS, ext, cols)
    shape = (members, rows, cols)
    outs = tuple(
        jax.ShapeDtypeStruct(s, F32)
        for s in (
            field, field, field, table, table, (tiles, BLOCK, cols), (8, rows, cols), (tiles, BLOCK, cols),
            (members, 128),
        )
    )
    state = pl.pallas_call(
        functools.partial(kernel, nx, ny, members, rows, cols),
        out_shape=outs,
        in_specs=[hbm_spec] * 5,
        out_specs=(vmem_spec,) * len(outs),
        scratch_shapes=[
            pltpu.VMEM((3,) + shape, F32),
            pltpu.VMEM((rows, cols), F32),
            pltpu.VMEM((rows, cols), jnp.int32),
            pltpu.VMEM((INTERVALS, rb_own, 5, 8, cols), BF16),
            pltpu.VMEM((INTERVALS, 2, tiles, 5, 8, cols), BF16),
            pltpu.VMEM((INTERVALS, 2, 13, 16, cols), BF16),
            pltpu.VMEM((INTERVALS, 2, 13, 16, cols), BF16),
            pltpu.VMEM((18, 16, cols), BF16),
            pltpu.VMEM((rows, cols), F32),
            pltpu.VMEM(field, F32),
            pltpu.VMEM(table, F32),
            pltpu.VMEM(table, F32),
            pltpu.VMEM((n // 2, 2 * rb_own * cb_own, 128), BF16),
            pltpu.VMEM((INTERVALS, n, members, 2 * rb_own * cb_own), BF16),
            dma((5,)),
            dma((INTERVALS,)),
            dma((INTERVALS,)),
            dma((INTERVALS, 3)),
            dma((INTERVALS, 3)),
        ],
        compiler_params=pltpu.CompilerParams(
            collective_id=0, has_side_effects=True, vmem_limit_bytes=40 * 1024 * 1024
        ),
        name="tide",
    )(
        *(
            pltpu.with_memory_space_constraint(x, pltpu.HBM)
            for x in (elevation, east_velocity, north_velocity, water_depth, land_sea)
        )
    )
    coarse = jax.ShapeDtypeStruct((members, rb_own, cb_own), F32)
    whole = jax.ShapeDtypeStruct(shape, F32)
    return pl.pallas_call(
        functools.partial(finish, members, rows, cols),
        out_shape=(whole, whole, whole, coarse),
        in_specs=[vmem_spec] * len(outs),
        out_specs=(hbm_spec,) * 4,
        scratch_shapes=[
            pltpu.VMEM(field, F32),
            pltpu.VMEM(field, F32),
            pltpu.VMEM(field, F32),
            pltpu.VMEM((3,) + shape, F32),
            pltpu.VMEM(coarse.shape, F32),
            dma((4 + rb_own,)),
        ],
        compiler_params=pltpu.CompilerParams(vmem_limit_bytes=8 * 1024 * 1024),
        name="finish",
    )(*state)


def solution(mesh):
    nx, ny = mesh.shape["gx"], mesh.shape["gy"]
    tile = P(None, "gy", "gx")
    return jax.shard_map(
        functools.partial(shards, nx, ny),
        mesh=mesh,
        in_specs=(tile, tile, tile, P("gy", "gx"), P("gy", "gx")),
        out_specs=(tile, tile, tile, tile),
        check_vma=False,
    )
```

```python
import functools
import math

import jax
import jax.numpy as jnp
from jax import lax
from jax.experimental import pallas as pl
from jax.experimental.pallas import tpu as pltpu
from jax.sharding import PartitionSpec as P

STEPS = 4
INTERVALS = 2
BLOCK = 8
HALO = 2 * STEPS

COURANT = 0.35
FRICTION = 0.02
CORIOLIS = 0.3
GREEN_SCALE = 0.25
KEEP = 1.0 - FRICTION
HALF = 0.5 * COURANT

MESH = pl.DeviceIdType.MESH
F32 = jnp.float32
BF16 = jnp.bfloat16

SIDE = 8
SLOTS = 9


def iota(shape, dim):
    return lax.broadcasted_iota(jnp.int32, shape, dim)


def latitude(row_ids, row_count):
    return ((row_ids.astype(F32) + 0.5) / row_count - 0.5) * jnp.pi


def longitude(col_ids, col_count):
    return (col_ids.astype(F32) + 0.5) / col_count * (2.0 * jnp.pi)


def unit_vectors(lat_angle, lon_angle):
    cos_lat = jnp.cos(lat_angle)
    return (cos_lat * jnp.cos(lon_angle), cos_lat * jnp.sin(lon_angle), jnp.sin(lat_angle))


def lanes():
    return iota((8, 128), 1)


def pick(x, index):
    return jnp.take_along_axis(x, index, axis=1)


def exchange(values):
    lane = lanes()
    values = list(values)
    for bit in range(3):
        step = 1 << bit
        low = (lane & step) == 0
        index = lane ^ step
        for a in range(8):
            if a & step:
                continue
            b = a | step
            moved = pick(jnp.where(low, values[b], values[a]), index)
            values[a], values[b] = jnp.where(low, values[a], moved), jnp.where(low, moved, values[b])
    return values


def band(t):
    return pl.ds(BLOCK + t * BLOCK, BLOCK)


def shifted(t, by):
    return pl.ds(BLOCK + t * BLOCK + by, BLOCK)


def x_differences(values, with_side=True):
    lane = lanes()
    first, last = lane < 8, lane >= 120
    edge_east, edge_west = pltpu.roll(values[7], 8, 1), pltpu.roll(values[0], 120, 1)
    side = values[SIDE]
    left = [jnp.where(first, pltpu.roll(side, 8, 1), edge_east)] + values[:7]
    right = values[1:8] + [jnp.where(last, pltpu.roll(side, 120, 1), edge_west)]
    if with_side:
        left.append(jnp.where(first, edge_east, pltpu.roll(side, 16, 1)))
        right.append(jnp.where(last, edge_west, pltpu.roll(side, 112, 1)))
    return [r - l for l, r in zip(left, right)]


def move_flow(tiles, n, last, eta, p_in, q_in, p_out, q_out, depth, turn):
    for t in range(tiles):
        inner = not last or 0 < t < tiles - 1
        coriolis = turn[t]
        if inner:
            diff = x_differences([eta[j, band(t), :] for j in range(SLOTS)])
        for j in range(SLOTS if inner else SIDE):
            d = depth[n, j, t * BLOCK : (t + 1) * BLOCK, :]
            p, q = p_in[j, band(t), :], q_in[j, band(t), :]
            if inner:
                p_out[j, band(t), :] = p + coriolis * q - d * diff[j]
            north = eta[j, shifted(t, 1), :] - eta[j, shifted(t, -1), :]
            q_out[j, band(t), :] = q - coriolis * p - d * north


def surface_change(t, n, with_side, p, q, wet):
    diff = x_differences([p[j, band(t), :] for j in range(SLOTS)], with_side)
    return [
        wet[n, j, t * BLOCK : (t + 1) * BLOCK, :]
        * (diff[j] + (q[j, shifted(t, 1), :] - q[j, shifted(t, -1), :]))
        for j in range(SLOTS if with_side else SIDE)
    ]


def move_surface(tiles, n, eta_in, eta_out, p, q, wet):
    for t in range(tiles):
        change = surface_change(t, n, True, p, q, wet)
        for j in range(SLOTS):
            eta_out[j, band(t), :] = eta_in[j, band(t), :] - change[j]


def kernel(
    nx, ny, members, rows, cols,
    h_in, u_in, v_in, d_in, o_in,
    eta, pp, qq, depth1, wet1, turn, restore, fine, l_out,
    in3, in_d, in_o, strips, land, slab_out, slab, counted, st, base, depth0, wet0, green, plane, pairs, tiles,
    in_sem, gs_sem, gr_sem, hs_sem, hr_sem,
):
    gx, gy = lax.axis_index("gx"), lax.axis_index("gy")
    n = nx * ny
    rb_own, cb_own = rows // BLOCK, cols // BLOCK
    per_device = rb_own * cb_own
    pair_rows = 2 * per_device
    coarse_rows, coarse_cols = rb_own * ny, cb_own * nx
    ext = rows + 2 * HALO
    ext_tiles = ext // BLOCK
    my_slot = gy * nx + gx
    fields = (eta, pp, qq)

    inputs = [
        pltpu.make_async_copy(src, dst, in_sem.at[k])
        for k, (src, dst) in enumerate(
            ((d_in, in_d), (o_in, in_o), (h_in, in3.at[0]), (u_in, in3.at[1]), (v_in, in3.at[2]))
        )
    ]
    for copy in inputs:
        copy.start()

    def wrap(index, size):
        return jnp.where(index >= size, index - size, index)

    def to_all_others(fn):
        others = [wrap(gy + dy, ny) for dy in range(ny)]
        for y in others[1:]:
            fn({"gx": gx, "gy": y})

        def column(dx, carry):
            x = wrap(gx + dx, nx)
            for y in others:
                fn({"gx": x, "gy": y})
            return carry

        lax.fori_loop(1, nx, column, 0)

    def to_band(fn):
        def one(dx, carry):
            fn({"gx": wrap(gx + dx, nx), "gy": gy})
            return carry

        lax.fori_loop(1, nx, one, 0)

    def to_column(fn):
        for dy in range(1, ny):
            fn({"gx": gx, "gy": wrap(gy + dy, ny)})

    barrier = pltpu.get_barrier_semaphore()

    def greet(device):
        pl.semaphore_signal(barrier, inc=1, device_id=device, device_id_type=MESH)


    def target_of(dx, dy):
        return {"gx": wrap(jnp.where(gx + dx < 0, gx + dx + nx, gx + dx), nx), "gy": gy + dy}

    def when(dy, sending, fn):
        if dy == 0:
            fn()
        else:
            beyond = gy + (dy if sending else -dy)
            pl.when((beyond >= 0) & (beyond < ny))(fn)

    to_band(greet)
    to_column(greet)
    for dy in (1, -1):
        when(dy, True, lambda dy=dy: [greet(target_of(dx, dy)) for dx in (1, -1)] and None)
    greeted = nx + ny - 2 + 2 * jnp.where(gy > 0, 1, 0) + 2 * jnp.where(gy < ny - 1, 1, 0)

    planes, layers = (5, 3), (13, 12)

    def remote(src, dst, i, group, dx, dy):
        return pltpu.make_async_remote_copy(
            src_ref=src, dst_ref=dst, send_sem=hs_sem.at[i, group], recv_sem=hr_sem.at[i, group],
            device_id=target_of(dx, dy), device_id_type=MESH,
        )

    def beside(i, dx):
        part = pl.ds(0, planes[i])
        return remote(
            strips.at[i, :, part], land.at[i, 0 if dx > 0 else 1, pl.ds(1, rb_own), part], i, 0, dx, 0
        )

    def beside_all(i):
        both = land.at[i, :, pl.ds(1, rb_own), pl.ds(0, planes[i])]
        return remote(both, both, i, 0, 1, 0)

    def start_beyond(i, dy):
        at, group = (0, 1) if dy > 0 else (1, 2)
        part, rest = pl.ds(0, planes[i]), pl.ds(0, layers[i])
        remote(slab_out.at[i, at, rest], slab.at[i, at, rest], i, group, 0, dy).start()
        for dx in (1, -1):
            src = strips.at[i, pl.ds(rb_own - 1 if dy > 0 else 0, 1), part]
            dst = land.at[i, 0 if dx > 0 else 1, pl.ds(0 if dy > 0 else ext_tiles - 1, 1), part]
            remote(src, dst, i, group, dx, dy).start()

    def beyond_all(i, dy):
        every = counted.at[pl.ds(0, layers[i] + planes[i])]
        return remote(every, every, i, 1 if dy > 0 else 2, 1, 0)

    def clear(side):
        at = 0 if side == 0 else ext_tiles - 1
        slab[:, side] = jnp.zeros_like(slab[:, side])
        land[:, :, at] = jnp.zeros_like(land[:, :, at])

    pl.when(gy == 0)(lambda: clear(0))
    pl.when(gy == ny - 1)(lambda: clear(1))

    lane = lanes()
    sub = iota((8, 128), 0)

    def put_base(t, source, slots):
        for j in slots:
            base[j, band(t), :] = pick(source, (lane & -8) + j)

    def place_loads(ref, slot, sums):
        spread = None
        for t, total in enumerate(sums):
            total = jnp.broadcast_to(jnp.sum(total, axis=0, keepdims=True), (8, 128)) * (1.0 / (BLOCK * HALF))
            mine = pick(total, (lane & 15) * 8 + sub)
            here = lane // cb_own == t + rb_own * (gx % 2)
            spread = jnp.where(here, mine, 0.0 if spread is None else spread)
        ref[slot] = spread.astype(BF16)

    def two_parts(x):
        high = x.astype(BF16).astype(F32)
        return high, x - high

    def pack(i, f):
        ref = (*fields, base)[f]
        for at, t in enumerate((rb_own, 1)):
            if f == 3:
                edge = two_parts(st[(t - 1) * BLOCK : t * BLOCK, :] * (HALF * HALF))
                slab_out[i, at, 12] = jnp.concatenate(edge, axis=0).astype(BF16)
                continue
            for k in range(4):
                both = jnp.concatenate([ref[2 * k, band(t), :], ref[2 * k + 1, band(t), :]], axis=0)
                slab_out[i, at, 4 * f + k] = both.astype(BF16)
        packed = [None] * rb_own
        for j in range(8):
            index = (lane + (128 - 16 * j - 8)) & 127
            for b in range(rb_own):
                moved = pick(ref[j, band(b + 1), :], index)
                packed[b] = moved if j == 0 else jnp.where(lane // 16 == j, moved, packed[b])
        for b in range(rb_own):
            parts = two_parts(packed[b]) if f == 3 else (packed[b],)
            for k, part in enumerate(parts):
                strips[i, b, f + k] = part.astype(BF16)

    def side_of(i, t, planes):
        west, east = (sum(land[i, side, t, k].astype(F32) for k in planes) for side in (0, 1))
        return pick(jnp.where((lane & 8) != 0, east, west), lane ^ 8)

    def assemble(i):
        for f, ref in enumerate(fields):
            for t in range(ext_tiles):
                ref[SIDE, band(t), :] = side_of(i, t, (f,))
            for at, t in enumerate((0, ext_tiles - 1)):
                for k in range(4):
                    both = slab[i, at, 4 * f + k].astype(F32)
                    ref[2 * k, band(t), :] = both[:8]
                    ref[2 * k + 1, band(t), :] = both[8:]

    def finish_base():
        for at, t in enumerate((0, ext_tiles - 1)):
            both = slab[0, at, 12].astype(F32)
            put_base(t, both[:8] + both[8:], range(8))
        for t in range(ext_tiles):
            base[SIDE, band(t), :] = side_of(0, t, (3, 4))

    def table(j, t, first, depth, wet):
        d = base[j, band(t), :]
        w = jnp.where(d > 0.0, 1.0, 0.0)
        part = pl.ds(t * BLOCK, BLOCK)
        for k in range(STEPS):
            depth[k, j, part, :] = d * KEEP ** -(first + k + 1)
            wet[k, j, part, :] = w * KEEP ** (first + k + 1)

    def own_tables(first, depth, wet):
        def fill(t, carry):
            for j in range(8):
                table(j, t, first, depth, wet)
            return carry

        lax.fori_loop(1, ext_tiles - 1, fill, 0)

    def edge_tables(first, depth, wet):
        for t in range(ext_tiles):
            for j in range(8) if t in (0, ext_tiles - 1) else ():
                table(j, t, first, depth, wet)
            table(SIDE, t, first, depth, wet)

    def gather(src, dst, group, device):
        return pltpu.make_async_remote_copy(
            src_ref=src, dst_ref=dst, send_sem=gs_sem.at[group], recv_sem=gr_sem.at[group],
            device_id=device, device_id_type=MESH,
        )

    def band_all():
        part = plane.at[pl.ds(0, nx - 1)]
        return gather(part, part, 0, target_of(1, 0))

    def column_all():
        part = pairs.at[pl.ds(0, ny - 1)]
        return gather(part, part, 1, target_of(1, 0))

    def everyone():
        part = tiles.at[pl.ds(0, n - 1)]
        return gather(part, part, 2, target_of(1, 0))

    def start_halos(i):
        for dx in (1, -1):
            beside(i, dx).start()
        for dy in (1, -1):
            when(dy, True, lambda dy=dy: start_beyond(i, dy))

    def wait_halos(i):
        beside_all(i).wait_recv()
        for dy in (1, -1):
            when(dy, False, lambda dy=dy: beyond_all(i, dy).wait_recv())

    def finish_sends(i):
        beside_all(i).wait_send()
        for dy in (1, -1):
            when(dy, True, lambda dy=dy: beyond_all(i, dy).wait_send())

    def make_turning():
        for e in range(ext_tiles):
            row_ids = gy * rows - HALO + e * BLOCK + iota((BLOCK, cols), 0)
            turn[e] = (CORIOLIS / KEEP) * jnp.sin(latitude(row_ids, rows * ny))

    def make_green():
        t = iota((8, 128), 1)
        north = per_device
        south = north + cb_own
        west = south + cb_own
        east = west + rb_own + 2
        t_row = jnp.where(t < north, t // cb_own, jnp.where(t < south, -1, rb_own))
        t_col = jnp.where(t < north, t % cb_own, jnp.where(t < south, t - north, t - south))
        t_row = jnp.where(t >= east, t - east - 1, jnp.where(t >= west, t - west - 1, t_row))
        t_col = jnp.where(t >= east, cb_own, jnp.where(t >= west, -1, t_col))
        t_row = gy * rb_own + t_row
        t_col = gx * cb_own + t_col
        t_col = jnp.where(t_col < 0, t_col + coarse_cols, t_col)
        t_col = jnp.where(t_col >= coarse_cols, t_col - coarse_cols, t_col)
        target = unit_vectors(latitude(t_row, coarse_rows), longitude(t_col, coarse_cols))
        target = [jnp.broadcast_to(x[:1], (pair_rows, 128)) for x in target]

        def green_group(g, carry):
            p = g * 8 + iota((8, pair_rows), 0)
            k = iota((8, pair_rows), 1)
            s_col = ((p % (nx // 2)) * 2 + k // per_device) * cb_own + k % cb_own
            s_row = (p // (nx // 2)) * rb_own + (k % per_device) // cb_own
            source = unit_vectors(latitude(s_row, coarse_rows), longitude(s_col, coarse_cols))
            source = [jnp.transpose(x) for x in source]
            for j in range(8):
                square = None
                for s, t_vec in zip(source, target):
                    diff = jnp.broadcast_to(s[:, j : j + 1], (pair_rows, 128)) - t_vec
                    square = diff * diff if square is None else square + diff * diff
                value = GREEN_SCALE / (1.0 + jnp.sqrt(square) * (coarse_rows / math.pi))
                green[g * 8 + j] = value.astype(BF16)
            return carry

        lax.fori_loop(0, n // 16, green_group, 0)

    def load(i):
        half = n // 4
        group = math.gcd(8, half)

        def pair(p):
            if i == 0:
                return pairs[p // (nx // 2), p % (nx // 2)].astype(F32)
            return tiles[2 * p].astype(F32) + tiles[2 * p + 1].astype(F32)

        def add_group(g, total):
            left, right = [], []
            for k in range(group):
                q = g * group + k
                left.append(jnp.concatenate([pair(q), pair(q + half)], axis=0).astype(BF16))
                right.append(jnp.concatenate([green[q], green[q + half]], axis=1))
            return total + jnp.dot(
                jnp.concatenate(left, axis=1), jnp.concatenate(right, axis=0), preferred_element_type=F32
            )

        both = lax.fori_loop(0, half // group, add_group, jnp.zeros((2 * members, 256), F32))
        loading = both[:members, :128] + both[members:, 128:]
        l_out[...] = loading
        loading = loading * HALF
        north = per_device
        south = north + cb_own
        west = south + cb_own
        east = west + rb_own + 2
        own_member = (lane & 7) == sub
        for t in range(ext_tiles):
            first = north if t == 0 else south if t == ext_tiles - 1 else (t - 1) * cb_own
            main = pick(loading, lane // 8 + first)
            side = pick(loading, jnp.where((lane & 8) != 0, west + t, east + t))
            both = []
            for value in (main, side):
                value = jnp.where(own_member, value, 0.0)
                if t == 0:
                    value = jnp.where(gy == 0, 0.0, value)
                if t == ext_tiles - 1:
                    value = jnp.where(gy == ny - 1, 0.0, value)
                both.append(jnp.broadcast_to(jnp.sum(value, axis=0, keepdims=True), (8, 128)))
            fine[t] = both[0]
            for j in range(8):
                eta[j, band(t), :] = eta[j, band(t), :] - both[0]
            eta[SIDE, band(t), :] = eta[SIDE, band(t), :] - both[1]

    def interval(i):
        def step(n, carry):
            move_flow(ext_tiles, n, False, eta, pp, qq, pp, qq, depth0, turn)
            move_surface(ext_tiles, n, eta, eta, pp, qq, wet0)
            return carry

        lax.fori_loop(0, STEPS - 1, step, 0)
        move_flow(ext_tiles, STEPS - 1, True, eta, pp, qq, pp, qq, depth0, turn)
        sums = []
        for t in range(1, ext_tiles - 1):
            change = surface_change(t, STEPS - 1, False, pp, qq, wet0)
            total = None
            for j in range(8):
                value = eta[j, band(t), :] - change[j] + fine[t]
                eta[j, band(t), :] = value
                value = value * wet0[STEPS - 1, j, t * BLOCK : (t + 1) * BLOCK, :]
                total = value if total is None else total + value
            sums.append(total * KEEP ** -STEPS)
        return sums

    for copy in inputs[:3]:
        copy.wait()
    st[...] = jnp.where(in_o[...] > 0, in_d[...], 0.0)
    sums = []
    for t in range(1, ext_tiles - 1):
        part = slice((t - 1) * BLOCK, t * BLOCK)
        put_base(t, st[part, :] * (HALF * HALF), range(8))
        total = None
        for j, value in enumerate(exchange([in3[0, m, part, :] for m in range(8)])):
            value = value * HALF
            eta[j, band(t), :] = value
            value = jnp.where(base[j, band(t), :] > 0.0, value, 0.0)
            total = value if total is None else total + value
        sums.append(total)
    place_loads(plane, gx, sums)
    for copy in inputs[3:]:
        copy.wait()
    for f in (1, 2):
        for t in range(1, ext_tiles - 1):
            part = slice((t - 1) * BLOCK, t * BLOCK)
            for j, value in enumerate(exchange([in3[f, m, part, :] for m in range(8)])):
                fields[f][j, band(t), :] = value * base[j, band(t), :]
    for f in range(4):
        pack(0, f)
    pl.semaphore_wait(barrier, greeted)
    to_band(lambda device: gather(plane.at[gx], plane.at[gx], 0, device).start())
    start_halos(0)

    make_turning()
    make_green()
    band_all().wait_recv()
    for k in range(nx // 2):
        pairs[gy, k] = (plane[2 * k].astype(F32) + plane[2 * k + 1].astype(F32)).astype(BF16)
    to_column(lambda device: gather(pairs.at[gy], pairs.at[gy], 1, device).start())
    own_tables(0, depth0, wet0)
    wait_halos(0)
    assemble(0)
    finish_base()
    edge_tables(0, depth0, wet0)
    column_all().wait_recv()
    load(0)
    place_loads(tiles, my_slot, interval(0))
    to_all_others(lambda device: gather(tiles.at[my_slot], tiles.at[my_slot], 2, device).start())
    for f in range(3):
        pack(1, f)
    start_halos(1)
    own_tables(STEPS, depth1, wet1)
    edge_tables(STEPS, depth1, wet1)
    for j in range(8):
        d = base[j, 2 * BLOCK : 2 * BLOCK + rows, :]
        restore[j] = jnp.where(d > 0.0, KEEP ** (2 * STEPS) / jnp.where(d > 0.0, d, 1.0), 0.0)
    band_all().wait_send()
    column_all().wait_send()
    finish_sends(0)
    wait_halos(1)
    assemble(1)
    everyone().wait_recv()
    load(1)
    finish_sends(1)
    everyone().wait_send()


def finish(
    members, rows, cols,
    eta_in, p_in, q_in, depth, wet, turn, restore, fine, l_in,
    h_out, u_out, v_out, l_out,
    eta, pp, qq, staged, l_staged, sem,
):
    ext_tiles = (rows + 2 * HALO) // BLOCK
    blocks, width = l_staged.shape[1:]
    for b in range(blocks):
        l_staged[:, b, :] = l_in[:, b * width : (b + 1) * width]
    l_copy = pltpu.make_async_copy(l_staged, l_out, sem.at[3])
    l_copy.start()

    move_flow(ext_tiles, 0, False, eta_in, p_in, q_in, pp, qq, depth, turn)
    move_surface(ext_tiles, 0, eta_in, eta, pp, qq, wet)

    def step(n, carry):
        move_flow(ext_tiles, n, False, eta, pp, qq, pp, qq, depth, turn)
        move_surface(ext_tiles, n, eta, eta, pp, qq, wet)
        return carry

    lax.fori_loop(1, STEPS - 1, step, 0)
    move_flow(ext_tiles, STEPS - 1, True, eta, pp, qq, pp, qq, depth, turn)
    copies = [pltpu.make_async_copy(staged.at[f], out, sem.at[f]) for f, out in ((1, u_out), (2, v_out))]
    for t in range(rows // BLOCK):
        part = pl.ds(t * BLOCK, BLOCK)
        copies.append(pltpu.make_async_copy(staged.at[0, :, part], h_out.at[:, part], sem.at[4 + t]))

    def place(f, t, values):
        for m, value in enumerate(exchange(values)):
            staged[f, m, (t - 1) * BLOCK : t * BLOCK, :] = value

    for f, ref in ((1, pp), (2, qq)):
        for t in range(1, ext_tiles - 1):
            part = slice((t - 1) * BLOCK, t * BLOCK)
            place(f, t, [ref[j, band(t), :] * restore[j, part, :] for j in range(8)])
        copies[f - 1].start()
    for t in range(1, ext_tiles - 1):
        change = surface_change(t, STEPS - 1, False, pp, qq, wet)
        place(0, t, [(eta[j, band(t), :] - change[j] + fine[t]) * (1.0 / HALF) for j in range(8)])
        copies[1 + t].start()
    for copy in copies:
        copy.wait()
    l_copy.wait()


def shards(nx, ny, elevation, east_velocity, north_velocity, water_depth, land_sea):
    members, rows, cols = elevation.shape
    rb_own, cb_own = rows // BLOCK, cols // BLOCK
    n = nx * ny
    ext = rows + 2 * HALO
    tiles = ext // BLOCK
    hbm_spec = pl.BlockSpec(memory_space=pltpu.HBM)
    vmem_spec = pl.BlockSpec(memory_space=pltpu.VMEM)
    dma = pltpu.SemaphoreType.DMA
    field = (SLOTS, ext + 2 * BLOCK, cols)
    table = (STEPS, SLOTS, ext, cols)
    shape = (members, rows, cols)
    outs = tuple(
        jax.ShapeDtypeStruct(s, F32)
        for s in (
            field, field, field, table, table, (tiles, BLOCK, cols), (8, rows, cols), (tiles, BLOCK, cols),
            (members, 128),
        )
    )
    state = pl.pallas_call(
        functools.partial(kernel, nx, ny, members, rows, cols),
        out_shape=outs,
        in_specs=[hbm_spec] * 5,
        out_specs=(vmem_spec,) * len(outs),
        scratch_shapes=[
            pltpu.VMEM((3,) + shape, F32),
            pltpu.VMEM((rows, cols), F32),
            pltpu.VMEM((rows, cols), jnp.int32),
            pltpu.VMEM((INTERVALS, rb_own, 5, 8, cols), BF16),
            pltpu.VMEM((INTERVALS, 2, tiles, 5, 8, cols), BF16),
            pltpu.VMEM((INTERVALS, 2, 13, 16, cols), BF16),
            pltpu.VMEM((INTERVALS, 2, 13, 16, cols), BF16),
            pltpu.VMEM((18, 16, cols), BF16),
            pltpu.VMEM((rows, cols), F32),
            pltpu.VMEM(field, F32),
            pltpu.VMEM(table, F32),
            pltpu.VMEM(table, F32),
            pltpu.VMEM((n // 2, 2 * rb_own * cb_own, 128), BF16),
            pltpu.VMEM((nx, members, 2 * rb_own * cb_own), BF16),
            pltpu.VMEM((ny, nx // 2, members, 2 * rb_own * cb_own), BF16),
            pltpu.VMEM((n, members, 2 * rb_own * cb_own), BF16),
            dma((5,)),
            dma((3,)),
            dma((3,)),
            dma((INTERVALS, 3)),
            dma((INTERVALS, 3)),
        ],
        compiler_params=pltpu.CompilerParams(
            collective_id=0, has_side_effects=True, vmem_limit_bytes=40 * 1024 * 1024
        ),
        name="tide",
    )(
        *(
            pltpu.with_memory_space_constraint(x, pltpu.HBM)
            for x in (elevation, east_velocity, north_velocity, water_depth, land_sea)
        )
    )
    coarse = jax.ShapeDtypeStruct((members, rb_own, cb_own), F32)
    whole = jax.ShapeDtypeStruct(shape, F32)
    return pl.pallas_call(
        functools.partial(finish, members, rows, cols),
        out_shape=(whole, whole, whole, coarse),
        in_specs=[vmem_spec] * len(outs),
        out_specs=(hbm_spec,) * 4,
        scratch_shapes=[
            pltpu.VMEM(field, F32),
            pltpu.VMEM(field, F32),
            pltpu.VMEM(field, F32),
            pltpu.VMEM((3,) + shape, F32),
            pltpu.VMEM(coarse.shape, F32),
            dma((4 + rb_own,)),
        ],
        compiler_params=pltpu.CompilerParams(vmem_limit_bytes=8 * 1024 * 1024),
        name="finish",
    )(*state)


def solution(mesh):
    nx, ny = mesh.shape["gx"], mesh.shape["gy"]
    tile = P(None, "gy", "gx")
    return jax.shard_map(
        functools.partial(shards, nx, ny),
        mesh=mesh,
        in_specs=(tile, tile, tile, P("gy", "gx"), P("gy", "gx")),
        out_specs=(tile, tile, tile, tile),
        check_vma=False,
    )
```

```python
import functools
import math

import jax
import jax.numpy as jnp
from jax import lax
from jax.experimental import pallas as pl
from jax.experimental.pallas import tpu as pltpu
from jax.sharding import PartitionSpec as P

STEPS = 4
INTERVALS = 2
BLOCK = 8
HALO = 2 * STEPS

COURANT = 0.35
FRICTION = 0.02
CORIOLIS = 0.3
GREEN_SCALE = 0.25
KEEP = 1.0 - FRICTION
HALF = 0.5 * COURANT

MESH = pl.DeviceIdType.MESH
F32 = jnp.float32
BF16 = jnp.bfloat16

SIDE = 8
SLOTS = 9


def iota(shape, dim):
    return lax.broadcasted_iota(jnp.int32, shape, dim)


def latitude(row_ids, row_count):
    return ((row_ids.astype(F32) + 0.5) / row_count - 0.5) * jnp.pi


def longitude(col_ids, col_count):
    return (col_ids.astype(F32) + 0.5) / col_count * (2.0 * jnp.pi)


def unit_vectors(lat_angle, lon_angle):
    cos_lat = jnp.cos(lat_angle)
    return (cos_lat * jnp.cos(lon_angle), cos_lat * jnp.sin(lon_angle), jnp.sin(lat_angle))


def lanes():
    return iota((8, 128), 1)


def pick(x, index):
    return jnp.take_along_axis(x, index, axis=1)


def exchange(values):
    lane = lanes()
    values = list(values)
    for bit in range(3):
        step = 1 << bit
        low = (lane & step) == 0
        index = lane ^ step
        for a in range(8):
            if a & step:
                continue
            b = a | step
            moved = pick(jnp.where(low, values[b], values[a]), index)
            values[a], values[b] = jnp.where(low, values[a], moved), jnp.where(low, moved, values[b])
    return values


def band(t):
    return pl.ds(BLOCK + t * BLOCK, BLOCK)


def shifted(t, by):
    return pl.ds(BLOCK + t * BLOCK + by, BLOCK)


def x_differences(values, with_side=True):
    lane = lanes()
    first, last = lane < 8, lane >= 120
    edge_east, edge_west = pltpu.roll(values[7], 8, 1), pltpu.roll(values[0], 120, 1)
    side = values[SIDE]
    left = [jnp.where(first, pltpu.roll(side, 8, 1), edge_east)] + values[:7]
    right = values[1:8] + [jnp.where(last, pltpu.roll(side, 120, 1), edge_west)]
    if with_side:
        left.append(jnp.where(first, edge_east, pltpu.roll(side, 16, 1)))
        right.append(jnp.where(last, edge_west, pltpu.roll(side, 112, 1)))
    return [r - l for l, r in zip(left, right)]


def move_flow(tiles, n, last, eta, p_in, q_in, p_out, q_out, depth, turn):
    for t in range(tiles):
        inner = not last or 0 < t < tiles - 1
        coriolis = turn[t]
        if inner:
            diff = x_differences([eta[j, band(t), :] for j in range(SLOTS)])
        for j in range(SLOTS if inner else SIDE):
            d = depth[n, j, t * BLOCK : (t + 1) * BLOCK, :]
            p, q = p_in[j, band(t), :], q_in[j, band(t), :]
            if inner:
                p_out[j, band(t), :] = p + coriolis * q - d * diff[j]
            north = eta[j, shifted(t, 1), :] - eta[j, shifted(t, -1), :]
            q_out[j, band(t), :] = q - coriolis * p - d * north


def surface_change(t, n, with_side, p, q, wet):
    diff = x_differences([p[j, band(t), :] for j in range(SLOTS)], with_side)
    return [
        wet[n, j, t * BLOCK : (t + 1) * BLOCK, :]
        * (diff[j] + (q[j, shifted(t, 1), :] - q[j, shifted(t, -1), :]))
        for j in range(SLOTS if with_side else SIDE)
    ]


def move_surface(tiles, n, eta_in, eta_out, p, q, wet):
    for t in range(tiles):
        change = surface_change(t, n, True, p, q, wet)
        for j in range(SLOTS):
            eta_out[j, band(t), :] = eta_in[j, band(t), :] - change[j]


def kernel(
    nx, ny, members, rows, cols,
    h_in, u_in, v_in, d_in, o_in,
    eta, pp, qq, depth1, wet1, turn, restore, fine, l_out,
    in3, in_d, in_o, strips, land, slab_out, slab, counted, st, base, depth0, wet0, green, plane, pairs, tiles,
    in_sem, gs_sem, gr_sem, hs_sem, hr_sem, up_sem,
):
    gx, gy = lax.axis_index("gx"), lax.axis_index("gy")
    n = nx * ny
    rb_own, cb_own = rows // BLOCK, cols // BLOCK
    per_device = rb_own * cb_own
    pair_rows = 2 * per_device
    coarse_rows, coarse_cols = rb_own * ny, cb_own * nx
    ext = rows + 2 * HALO
    ext_tiles = ext // BLOCK
    my_slot = gy * nx + gx
    fields = (eta, pp, qq)

    inputs = [
        pltpu.make_async_copy(src, dst, in_sem.at[k])
        for k, (src, dst) in enumerate(
            ((d_in, in_d), (o_in, in_o), (h_in, in3.at[0]), (u_in, in3.at[1]), (v_in, in3.at[2]))
        )
    ]
    for copy in inputs:
        copy.start()

    def wrap(index, size):
        return jnp.where(index >= size, index - size, index)

    def to_all_others(fn):
        others = [wrap(gy + dy, ny) for dy in range(ny)]
        for y in others[1:]:
            fn({"gx": gx, "gy": y})

        def column(dx, carry):
            x = wrap(gx + dx, nx)
            for y in others:
                fn({"gx": x, "gy": y})
            return carry

        lax.fori_loop(1, nx, column, 0)

    def to_band(fn):
        def one(dx, carry):
            fn({"gx": wrap(gx + dx, nx), "gy": gy})
            return carry

        lax.fori_loop(1, nx, one, 0)

    def to_column(fn):
        for dy in range(1, ny):
            fn({"gx": gx, "gy": wrap(gy + dy, ny)})

    barrier = pltpu.get_barrier_semaphore()

    def greet(device):
        pl.semaphore_signal(barrier, inc=1, device_id=device, device_id_type=MESH)


    def target_of(dx, dy):
        return {"gx": wrap(jnp.where(gx + dx < 0, gx + dx + nx, gx + dx), nx), "gy": gy + dy}

    def when(dy, sending, fn):
        if dy == 0:
            fn()
        else:
            beyond = gy + (dy if sending else -dy)
            pl.when((beyond >= 0) & (beyond < ny))(fn)

    def further(up, fn):
        for dy in range(2, ny):
            inside = gy + dy < ny if up else gy - dy >= 0
            pl.when(inside)(lambda dy=dy: fn({"gx": gx, "gy": gy + dy if up else gy - dy}))

    def greet_beyond(dy):
        for dx in (0, 1, -1):
            greet(target_of(dx, dy))

    to_band(greet)
    for dy in (1, -1):
        when(dy, True, lambda dy=dy: greet_beyond(dy))
    further(True, greet)

    def meet():
        below, above = jnp.where(gy > 0, gy + 2, 0), jnp.where(gy < ny - 1, 3, 0)
        pl.semaphore_wait(barrier, nx - 1 + below + above)
        further(
            False,
            lambda device: pl.semaphore_signal(up_sem, inc=1, device_id=device, device_id_type=MESH),
        )

    def hear_answers():
        pl.when(gy < ny - 2)(lambda: pl.semaphore_wait(up_sem, ny - 2 - gy))

    meets_early = (gx // 2 == nx // 2 - 1) & (gy == ny - 1)
    pl.when(meets_early)(meet)

    planes, layers = (5, 3), (13, 12)

    def remote(src, dst, i, group, dx, dy):
        return pltpu.make_async_remote_copy(
            src_ref=src, dst_ref=dst, send_sem=hs_sem.at[i, group], recv_sem=hr_sem.at[i, group],
            device_id=target_of(dx, dy), device_id_type=MESH,
        )

    def beside(i, dx):
        part = pl.ds(0, planes[i])
        return remote(
            strips.at[i, :, part], land.at[i, 0 if dx > 0 else 1, pl.ds(1, rb_own), part], i, 0, dx, 0
        )

    def beside_all(i):
        both = land.at[i, :, pl.ds(1, rb_own), pl.ds(0, planes[i])]
        return remote(both, both, i, 0, 1, 0)

    def start_beyond(i, dy):
        at, group = (0, 1) if dy > 0 else (1, 2)
        part, rest = pl.ds(0, planes[i]), pl.ds(0, layers[i])
        remote(slab_out.at[i, at, rest], slab.at[i, at, rest], i, group, 0, dy).start()
        for dx in (1, -1):
            src = strips.at[i, pl.ds(rb_own - 1 if dy > 0 else 0, 1), part]
            dst = land.at[i, 0 if dx > 0 else 1, pl.ds(0 if dy > 0 else ext_tiles - 1, 1), part]
            remote(src, dst, i, group, dx, dy).start()

    def beyond_all(i, dy):
        every = counted.at[pl.ds(0, layers[i] + planes[i])]
        return remote(every, every, i, 1 if dy > 0 else 2, 1, 0)

    def clear(side):
        at = 0 if side == 0 else ext_tiles - 1
        slab[:, side] = jnp.zeros_like(slab[:, side])
        land[:, :, at] = jnp.zeros_like(land[:, :, at])

    pl.when(gy == 0)(lambda: clear(0))
    pl.when(gy == ny - 1)(lambda: clear(1))

    lane = lanes()
    sub = iota((8, 128), 0)

    def put_base(t, source, slots):
        for j in slots:
            base[j, band(t), :] = pick(source, (lane & -8) + j)

    def place_loads(ref, slot, sums):
        spread = None
        for t, total in enumerate(sums):
            total = jnp.broadcast_to(jnp.sum(total, axis=0, keepdims=True), (8, 128)) * (1.0 / (BLOCK * HALF))
            mine = pick(total, (lane & 15) * 8 + sub)
            here = lane // cb_own == t + rb_own * (gx % 2)
            spread = jnp.where(here, mine, 0.0 if spread is None else spread)
        ref[slot] = spread.astype(BF16)

    def two_parts(x):
        high = x.astype(BF16).astype(F32)
        return high, x - high

    def pack(i, f):
        ref = (*fields, base)[f]
        for at, t in enumerate((rb_own, 1)):
            if f == 3:
                edge = two_parts(st[(t - 1) * BLOCK : t * BLOCK, :] * (HALF * HALF))
                slab_out[i, at, 12] = jnp.concatenate(edge, axis=0).astype(BF16)
                continue
            for k in range(4):
                both = jnp.concatenate([ref[2 * k, band(t), :], ref[2 * k + 1, band(t), :]], axis=0)
                slab_out[i, at, 4 * f + k] = both.astype(BF16)
        packed = [None] * rb_own
        for j in range(8):
            index = (lane + (128 - 16 * j - 8)) & 127
            for b in range(rb_own):
                moved = pick(ref[j, band(b + 1), :], index)
                packed[b] = moved if j == 0 else jnp.where(lane // 16 == j, moved, packed[b])
        for b in range(rb_own):
            parts = two_parts(packed[b]) if f == 3 else (packed[b],)
            for k, part in enumerate(parts):
                strips[i, b, f + k] = part.astype(BF16)

    def side_of(i, t, planes):
        west, east = (sum(land[i, side, t, k].astype(F32) for k in planes) for side in (0, 1))
        return pick(jnp.where((lane & 8) != 0, east, west), lane ^ 8)

    def assemble(i):
        for f, ref in enumerate(fields):
            for t in range(ext_tiles):
                ref[SIDE, band(t), :] = side_of(i, t, (f,))
            for at, t in enumerate((0, ext_tiles - 1)):
                for k in range(4):
                    both = slab[i, at, 4 * f + k].astype(F32)
                    ref[2 * k, band(t), :] = both[:8]
                    ref[2 * k + 1, band(t), :] = both[8:]

    def finish_base():
        for at, t in enumerate((0, ext_tiles - 1)):
            both = slab[0, at, 12].astype(F32)
            put_base(t, both[:8] + both[8:], range(8))
        for t in range(ext_tiles):
            base[SIDE, band(t), :] = side_of(0, t, (3, 4))

    def table(j, t, first, depth, wet):
        d = base[j, band(t), :]
        w = jnp.where(d > 0.0, 1.0, 0.0)
        part = pl.ds(t * BLOCK, BLOCK)
        for k in range(STEPS):
            depth[k, j, part, :] = d * KEEP ** -(first + k + 1)
            wet[k, j, part, :] = w * KEEP ** (first + k + 1)

    def own_tables(first, depth, wet):
        def fill(t, carry):
            for j in range(8):
                table(j, t, first, depth, wet)
            return carry

        lax.fori_loop(1, ext_tiles - 1, fill, 0)

    def edge_tables(first, depth, wet):
        for t in range(ext_tiles):
            for j in range(8) if t in (0, ext_tiles - 1) else ():
                table(j, t, first, depth, wet)
            table(SIDE, t, first, depth, wet)

    def gather(src, dst, group, device):
        return pltpu.make_async_remote_copy(
            src_ref=src, dst_ref=dst, send_sem=gs_sem.at[group], recv_sem=gr_sem.at[group],
            device_id=device, device_id_type=MESH,
        )

    def band_all():
        part = plane.at[pl.ds(0, nx - 1)]
        return gather(part, part, 0, target_of(1, 0))

    def column_all():
        part = pairs.at[pl.ds(0, ny - 1)]
        return gather(part, part, 1, target_of(1, 0))

    def everyone():
        part = tiles.at[pl.ds(0, n - 1)]
        return gather(part, part, 2, target_of(1, 0))

    def start_beside(i):
        for dx in (1, -1):
            beside(i, dx).start()

    def start_halos(i):
        start_beside(i)
        for dy in (1, -1):
            when(dy, True, lambda dy=dy: start_beyond(i, dy))

    def wait_halos(i):
        beside_all(i).wait_recv()
        for dy in (1, -1):
            when(dy, False, lambda dy=dy: beyond_all(i, dy).wait_recv())

    def finish_sends(i):
        beside_all(i).wait_send()
        for dy in (1, -1):
            when(dy, True, lambda dy=dy: beyond_all(i, dy).wait_send())

    def make_turning():
        for e in range(ext_tiles):
            row_ids = gy * rows - HALO + e * BLOCK + iota((BLOCK, cols), 0)
            turn[e] = (CORIOLIS / KEEP) * jnp.sin(latitude(row_ids, rows * ny))

    def make_green():
        t = iota((8, 128), 1)
        north = per_device
        south = north + cb_own
        west = south + cb_own
        east = west + rb_own + 2
        t_row = jnp.where(t < north, t // cb_own, jnp.where(t < south, -1, rb_own))
        t_col = jnp.where(t < north, t % cb_own, jnp.where(t < south, t - north, t - south))
        t_row = jnp.where(t >= east, t - east - 1, jnp.where(t >= west, t - west - 1, t_row))
        t_col = jnp.where(t >= east, cb_own, jnp.where(t >= west, -1, t_col))
        t_row = gy * rb_own + t_row
        t_col = gx * cb_own + t_col
        t_col = jnp.where(t_col < 0, t_col + coarse_cols, t_col)
        t_col = jnp.where(t_col >= coarse_cols, t_col - coarse_cols, t_col)
        target = unit_vectors(latitude(t_row, coarse_rows), longitude(t_col, coarse_cols))
        target = [jnp.broadcast_to(x[:1], (pair_rows, 128)) for x in target]

        def green_group(g, carry):
            p = g * 8 + iota((8, pair_rows), 0)
            k = iota((8, pair_rows), 1)
            s_col = ((p % (nx // 2)) * 2 + k // per_device) * cb_own + k % cb_own
            s_row = (p // (nx // 2)) * rb_own + (k % per_device) // cb_own
            source = unit_vectors(latitude(s_row, coarse_rows), longitude(s_col, coarse_cols))
            source = [jnp.transpose(x) for x in source]
            for j in range(8):
                square = None
                for s, t_vec in zip(source, target):
                    diff = jnp.broadcast_to(s[:, j : j + 1], (pair_rows, 128)) - t_vec
                    square = diff * diff if square is None else square + diff * diff
                value = GREEN_SCALE / (1.0 + jnp.sqrt(square) * (coarse_rows / math.pi))
                green[g * 8 + j] = value.astype(BF16)
            return carry

        lax.fori_loop(0, n // 16, green_group, 0)

    def load(i):
        half = n // 4
        group = math.gcd(8, half)

        def pair(p):
            if i == 0:
                return pairs[p // (nx // 2), p % (nx // 2)].astype(F32)
            return tiles[2 * p].astype(F32) + tiles[2 * p + 1].astype(F32)

        def add_group(g, total):
            left, right = [], []
            for k in range(group):
                q = g * group + k
                left.append(jnp.concatenate([pair(q), pair(q + half)], axis=0).astype(BF16))
                right.append(jnp.concatenate([green[q], green[q + half]], axis=1))
            return total + jnp.dot(
                jnp.concatenate(left, axis=1), jnp.concatenate(right, axis=0), preferred_element_type=F32
            )

        both = lax.fori_loop(0, half // group, add_group, jnp.zeros((2 * members, 256), F32))
        loading = both[:members, :128] + both[members:, 128:]
        l_out[...] = loading
        loading = loading * HALF
        north = per_device
        south = north + cb_own
        west = south + cb_own
        east = west + rb_own + 2
        own_member = (lane & 7) == sub
        for t in range(ext_tiles):
            first = north if t == 0 else south if t == ext_tiles - 1 else (t - 1) * cb_own
            main = pick(loading, lane // 8 + first)
            side = pick(loading, jnp.where((lane & 8) != 0, west + t, east + t))
            both = []
            for value in (main, side):
                value = jnp.where(own_member, value, 0.0)
                if t == 0:
                    value = jnp.where(gy == 0, 0.0, value)
                if t == ext_tiles - 1:
                    value = jnp.where(gy == ny - 1, 0.0, value)
                both.append(jnp.broadcast_to(jnp.sum(value, axis=0, keepdims=True), (8, 128)))
            fine[t] = both[0]
            for j in range(8):
                eta[j, band(t), :] = eta[j, band(t), :] - both[0]
            eta[SIDE, band(t), :] = eta[SIDE, band(t), :] - both[1]

    def interval(i):
        def step(n, carry):
            move_flow(ext_tiles, n, False, eta, pp, qq, pp, qq, depth0, turn)
            move_surface(ext_tiles, n, eta, eta, pp, qq, wet0)
            return carry

        lax.fori_loop(0, STEPS - 1, step, 0)
        move_flow(ext_tiles, STEPS - 1, True, eta, pp, qq, pp, qq, depth0, turn)
        sums = []
        for t in range(1, ext_tiles - 1):
            change = surface_change(t, STEPS - 1, False, pp, qq, wet0)
            total = None
            for j in range(8):
                value = eta[j, band(t), :] - change[j] + fine[t]
                eta[j, band(t), :] = value
                value = value * wet0[STEPS - 1, j, t * BLOCK : (t + 1) * BLOCK, :]
                total = value if total is None else total + value
            sums.append(total * KEEP ** -STEPS)
        return sums

    for copy in inputs[:3]:
        copy.wait()
    st[...] = jnp.where(in_o[...] > 0, in_d[...], 0.0)
    sums = []
    for t in range(1, ext_tiles - 1):
        part = slice((t - 1) * BLOCK, t * BLOCK)
        put_base(t, st[part, :] * (HALF * HALF), range(8))
        total = None
        for j, value in enumerate(exchange([in3[0, m, part, :] for m in range(8)])):
            value = value * HALF
            eta[j, band(t), :] = value
            value = jnp.where(base[j, band(t), :] > 0.0, value, 0.0)
            total = value if total is None else total + value
        sums.append(total)
    place_loads(plane, gx, sums)

    def send_band():
        to_band(lambda device: gather(plane.at[gx], plane.at[gx], 0, device).start())

    pl.when(meets_early)(send_band)
    for copy in inputs[3:]:
        copy.wait()
    for f in (1, 2):
        for t in range(1, ext_tiles - 1):
            part = slice((t - 1) * BLOCK, t * BLOCK)
            for j, value in enumerate(exchange([in3[f, m, part, :] for m in range(8)])):
                fields[f][j, band(t), :] = value * base[j, band(t), :]
    for f in range(4):
        pack(0, f)

    def meet_late():
        meet()
        send_band()

    pl.when(jnp.logical_not(meets_early))(meet_late)
    start_halos(0)

    make_turning()
    make_green()
    band_all().wait_recv()
    for k in range(nx // 2):
        pairs[gy, k] = (plane[2 * k].astype(F32) + plane[2 * k + 1].astype(F32)).astype(BF16)
    hear_answers()
    to_column(lambda device: gather(pairs.at[gy], pairs.at[gy], 1, device).start())
    own_tables(0, depth0, wet0)
    wait_halos(0)
    assemble(0)
    finish_base()
    edge_tables(0, depth0, wet0)
    column_all().wait_recv()
    load(0)
    place_loads(tiles, my_slot, interval(0))
    to_all_others(lambda device: gather(tiles.at[my_slot], tiles.at[my_slot], 2, device).start())
    for f in range(3):
        pack(1, f)
    start_halos(1)
    own_tables(STEPS, depth1, wet1)
    edge_tables(STEPS, depth1, wet1)
    for j in range(8):
        d = base[j, 2 * BLOCK : 2 * BLOCK + rows, :]
        restore[j] = jnp.where(d > 0.0, KEEP ** (2 * STEPS) / jnp.where(d > 0.0, d, 1.0), 0.0)
    band_all().wait_send()
    column_all().wait_send()
    finish_sends(0)
    wait_halos(1)
    assemble(1)
    finish_sends(1)
    everyone().wait_send()
    everyone().wait_recv()
    load(1)


def finish(
    members, rows, cols,
    eta_in, p_in, q_in, depth, wet, turn, restore, fine, l_in,
    h_out, u_out, v_out, l_out,
    eta, pp, qq, staged, l_staged, sem,
):
    ext_tiles = (rows + 2 * HALO) // BLOCK
    blocks, width = l_staged.shape[1:]
    for b in range(blocks):
        l_staged[:, b, :] = l_in[:, b * width : (b + 1) * width]
    l_copy = pltpu.make_async_copy(l_staged, l_out, sem.at[3])
    l_copy.start()

    move_flow(ext_tiles, 0, False, eta_in, p_in, q_in, pp, qq, depth, turn)
    move_surface(ext_tiles, 0, eta_in, eta, pp, qq, wet)

    def step(n, carry):
        move_flow(ext_tiles, n, False, eta, pp, qq, pp, qq, depth, turn)
        move_surface(ext_tiles, n, eta, eta, pp, qq, wet)
        return carry

    lax.fori_loop(1, STEPS - 1, step, 0)
    move_flow(ext_tiles, STEPS - 1, True, eta, pp, qq, pp, qq, depth, turn)
    copies = [pltpu.make_async_copy(staged.at[f], out, sem.at[f]) for f, out in ((1, u_out), (2, v_out))]
    for t in range(rows // BLOCK):
        part = pl.ds(t * BLOCK, BLOCK)
        copies.append(pltpu.make_async_copy(staged.at[0, :, part], h_out.at[:, part], sem.at[4 + t]))

    def place(f, t, values):
        for m, value in enumerate(exchange(values)):
            staged[f, m, (t - 1) * BLOCK : t * BLOCK, :] = value

    for f, ref in ((1, pp), (2, qq)):
        for t in range(1, ext_tiles - 1):
            part = slice((t - 1) * BLOCK, t * BLOCK)
            place(f, t, [ref[j, band(t), :] * restore[j, part, :] for j in range(8)])
        copies[f - 1].start()
    for t in range(1, ext_tiles - 1):
        change = surface_change(t, STEPS - 1, False, pp, qq, wet)
        place(0, t, [(eta[j, band(t), :] - change[j] + fine[t]) * (1.0 / HALF) for j in range(8)])
        copies[1 + t].start()
    for copy in copies:
        copy.wait()
    l_copy.wait()


def shards(nx, ny, elevation, east_velocity, north_velocity, water_depth, land_sea):
    members, rows, cols = elevation.shape
    rb_own, cb_own = rows // BLOCK, cols // BLOCK
    n = nx * ny
    ext = rows + 2 * HALO
    tiles = ext // BLOCK
    hbm_spec = pl.BlockSpec(memory_space=pltpu.HBM)
    vmem_spec = pl.BlockSpec(memory_space=pltpu.VMEM)
    dma = pltpu.SemaphoreType.DMA
    field = (SLOTS, ext + 2 * BLOCK, cols)
    table = (STEPS, SLOTS, ext, cols)
    shape = (members, rows, cols)
    outs = tuple(
        jax.ShapeDtypeStruct(s, F32)
        for s in (
            field, field, field, table, table, (tiles, BLOCK, cols), (8, rows, cols), (tiles, BLOCK, cols),
            (members, 128),
        )
    )
    state = pl.pallas_call(
        functools.partial(kernel, nx, ny, members, rows, cols),
        out_shape=outs,
        in_specs=[hbm_spec] * 5,
        out_specs=(vmem_spec,) * len(outs),
        scratch_shapes=[
            pltpu.VMEM((3,) + shape, F32),
            pltpu.VMEM((rows, cols), F32),
            pltpu.VMEM((rows, cols), jnp.int32),
            pltpu.VMEM((INTERVALS, rb_own, 5, 8, cols), BF16),
            pltpu.VMEM((INTERVALS, 2, tiles, 5, 8, cols), BF16),
            pltpu.VMEM((INTERVALS, 2, 13, 16, cols), BF16),
            pltpu.VMEM((INTERVALS, 2, 13, 16, cols), BF16),
            pltpu.VMEM((18, 16, cols), BF16),
            pltpu.VMEM((rows, cols), F32),
            pltpu.VMEM(field, F32),
            pltpu.VMEM(table, F32),
            pltpu.VMEM(table, F32),
            pltpu.VMEM((n // 2, 2 * rb_own * cb_own, 128), BF16),
            pltpu.VMEM((nx, members, 2 * rb_own * cb_own), BF16),
            pltpu.VMEM((ny, nx // 2, members, 2 * rb_own * cb_own), BF16),
            pltpu.VMEM((n, members, 2 * rb_own * cb_own), BF16),
            dma((5,)),
            dma((3,)),
            dma((3,)),
            dma((INTERVALS, 3)),
            dma((INTERVALS, 3)),
            pltpu.SemaphoreType.REGULAR,
        ],
        compiler_params=pltpu.CompilerParams(
            collective_id=0, has_side_effects=True, vmem_limit_bytes=40 * 1024 * 1024
        ),
        name="tide",
    )(
        *(
            pltpu.with_memory_space_constraint(x, pltpu.HBM)
            for x in (elevation, east_velocity, north_velocity, water_depth, land_sea)
        )
    )
    coarse = jax.ShapeDtypeStruct((members, rb_own, cb_own), F32)
    whole = jax.ShapeDtypeStruct(shape, F32)
    return pl.pallas_call(
        functools.partial(finish, members, rows, cols),
        out_shape=(whole, whole, whole, coarse),
        in_specs=[vmem_spec] * len(outs),
        out_specs=(hbm_spec,) * 4,
        scratch_shapes=[
            pltpu.VMEM(field, F32),
            pltpu.VMEM(field, F32),
            pltpu.VMEM(field, F32),
            pltpu.VMEM((3,) + shape, F32),
            pltpu.VMEM(coarse.shape, F32),
            dma((4 + rb_own,)),
        ],
        compiler_params=pltpu.CompilerParams(vmem_limit_bytes=8 * 1024 * 1024),
        name="finish",
    )(*state)


def solution(mesh):
    nx, ny = mesh.shape["gx"], mesh.shape["gy"]
    tile = P(None, "gy", "gx")
    return jax.shard_map(
        functools.partial(shards, nx, ny),
        mesh=mesh,
        in_specs=(tile, tile, tile, P("gy", "gx"), P("gy", "gx")),
        out_specs=(tile, tile, tile, tile),
        check_vma=False,
    )
```

```python
import functools
import math

import jax
import jax.numpy as jnp
from jax import lax
from jax.experimental import pallas as pl
from jax.experimental.pallas import tpu as pltpu
from jax.sharding import PartitionSpec as P

STEPS = 4
INTERVALS = 2
BLOCK = 8
HALO = 2 * STEPS

COURANT = 0.35
FRICTION = 0.02
CORIOLIS = 0.3
GREEN_SCALE = 0.25
KEEP = 1.0 - FRICTION
HALF = 0.5 * COURANT

MESH = pl.DeviceIdType.MESH
F32 = jnp.float32
BF16 = jnp.bfloat16

SIDE = 8
TOGETHER = 4
SLOTS = 9


def iota(shape, dim):
    return lax.broadcasted_iota(jnp.int32, shape, dim)


def latitude(row_ids, row_count):
    return ((row_ids.astype(F32) + 0.5) / row_count - 0.5) * jnp.pi


def longitude(col_ids, col_count):
    return (col_ids.astype(F32) + 0.5) / col_count * (2.0 * jnp.pi)


def unit_vectors(lat_angle, lon_angle):
    cos_lat = jnp.cos(lat_angle)
    return (cos_lat * jnp.cos(lon_angle), cos_lat * jnp.sin(lon_angle), jnp.sin(lat_angle))


def lanes():
    return iota((8, 128), 1)


def pick(x, index):
    return jnp.take_along_axis(x, index, axis=1)


def exchange(groups):
    lane = lanes()
    groups = [list(values) for values in groups]
    for bit in range(3):
        step = 1 << bit
        low = (lane & step) == 0
        index = lane ^ step
        for values in groups:
            for a in range(8):
                if a & step:
                    continue
                b = a | step
                moved = pick(jnp.where(low, values[b], values[a]), index)
                values[a], values[b] = jnp.where(low, values[a], moved), jnp.where(low, moved, values[b])
    return groups


def band(t):
    return pl.ds(BLOCK + t * BLOCK, BLOCK)


def shifted(t, by):
    return pl.ds(BLOCK + t * BLOCK + by, BLOCK)


def x_differences(values, with_side=True):
    lane = lanes()
    first, last = lane < 8, lane >= 120
    up_main, up_side = pltpu.roll(values[7], 8, 1), pltpu.roll(values[SIDE], 8, 1)
    down_main, down_side = pltpu.roll(values[0], 120, 1), pltpu.roll(values[SIDE], 120, 1)
    left = [jnp.where(first, up_side, up_main)] + values[:7]
    right = values[1:8] + [jnp.where(last, down_side, down_main)]
    if with_side:
        left.append(jnp.where(first, up_main, up_side))
        right.append(jnp.where(last, down_main, down_side))
    return [r - l for l, r in zip(left, right)]


def move_flow(tiles, n, last, eta, p_in, q_in, p_out, q_out, depth, turn):
    for t in range(tiles):
        inner = not last or 0 < t < tiles - 1
        coriolis = turn[t]
        if inner:
            diff = x_differences([eta[j, band(t), :] for j in range(SLOTS)])
        for j in range(SLOTS if inner else SIDE):
            d = depth[n, j, t * BLOCK : (t + 1) * BLOCK, :]
            p, q = p_in[j, band(t), :], q_in[j, band(t), :]
            if inner:
                p_out[j, band(t), :] = p + coriolis * q - d * diff[j]
            north = eta[j, shifted(t, 1), :] - eta[j, shifted(t, -1), :]
            q_out[j, band(t), :] = q - coriolis * p - d * north


def surface_change(t, n, with_side, p, q, wet):
    diff = x_differences([p[j, band(t), :] for j in range(SLOTS)], with_side)
    return [
        wet[n, j, t * BLOCK : (t + 1) * BLOCK, :]
        * (diff[j] + (q[j, shifted(t, 1), :] - q[j, shifted(t, -1), :]))
        for j in range(SLOTS if with_side else SIDE)
    ]


def move_surface(tiles, n, eta_in, eta_out, p, q, wet):
    for t in range(tiles):
        change = surface_change(t, n, True, p, q, wet)
        for j in range(SLOTS):
            eta_out[j, band(t), :] = eta_in[j, band(t), :] - change[j]


def kernel(
    nx, ny, members, rows, cols,
    h_in, u_in, v_in, d_in, o_in,
    eta, pp, qq, depth1, wet1, turn, restore, fine, l_out,
    in3, in_d, in_o, strips, land, slab_out, slab, counted, st, base, depth0, wet0, green, plane, pairs, tiles,
    in_sem, gs_sem, gr_sem, hs_sem, hr_sem, up_sem,
):
    gx, gy = lax.axis_index("gx"), lax.axis_index("gy")
    n = nx * ny
    rb_own, cb_own = rows // BLOCK, cols // BLOCK
    per_device = rb_own * cb_own
    pair_rows = 2 * per_device
    coarse_rows, coarse_cols = rb_own * ny, cb_own * nx
    ext = rows + 2 * HALO
    ext_tiles = ext // BLOCK
    my_slot = gy * nx + gx
    fields = (eta, pp, qq)

    inputs = [
        pltpu.make_async_copy(src, dst, done)
        for src, dst, done in (
            (d_in, in_d, hs_sem.at[0]), (o_in, in_o, hs_sem.at[1]), (h_in, in3.at[0], hs_sem.at[2]),
            (u_in, in3.at[1], in_sem.at[0]), (v_in, in3.at[2], in_sem.at[1]),
        )
    ]
    for copy in inputs:
        copy.start()

    def wrap(index, size):
        return jnp.where(index >= size, index - size, index)

    def to_all_others(fn):
        others = [wrap(gy + dy, ny) for dy in range(ny)]
        for y in others[1:]:
            fn({"gx": gx, "gy": y})

        def column(dx, carry):
            x = wrap(gx + dx, nx)
            for y in others:
                fn({"gx": x, "gy": y})
            return carry

        lax.fori_loop(1, nx, column, 0)

    def to_band(fn):
        def one(dx, carry):
            fn({"gx": wrap(gx + dx, nx), "gy": gy})
            return carry

        lax.fori_loop(1, nx, one, 0)

    def to_column(fn):
        for dy in range(1, ny):
            fn({"gx": gx, "gy": wrap(gy + dy, ny)})

    barrier = pltpu.get_barrier_semaphore()

    def greet(device):
        pl.semaphore_signal(barrier, inc=1, device_id=device, device_id_type=MESH)


    def target_of(dx, dy):
        return {"gx": wrap(jnp.where(gx + dx < 0, gx + dx + nx, gx + dx), nx), "gy": gy + dy}

    def when(dy, sending, fn):
        if dy == 0:
            fn()
        else:
            beyond = gy + (dy if sending else -dy)
            pl.when((beyond >= 0) & (beyond < ny))(fn)

    def further(up, fn):
        for dy in range(2, ny):
            inside = gy + dy < ny if up else gy - dy >= 0
            pl.when(inside)(lambda dy=dy: fn({"gx": gx, "gy": gy + dy if up else gy - dy}))

    def greet_beyond(dy):
        for dx in (0, 1, -1):
            greet(target_of(dx, dy))

    to_band(greet)
    for dy in (1, -1):
        when(dy, True, lambda dy=dy: greet_beyond(dy))
    further(True, greet)

    def meet():
        below, above = jnp.where(gy > 0, gy + 2, 0), jnp.where(gy < ny - 1, 3, 0)
        pl.semaphore_wait(barrier, nx - 1 + below + above)
        further(
            False,
            lambda device: pl.semaphore_signal(up_sem, inc=1, device_id=device, device_id_type=MESH),
        )

    def hear_answers():
        pl.when(gy < ny - 2)(lambda: pl.semaphore_wait(up_sem, ny - 2 - gy))

    meets_early = (gx // 2 == nx // 2 - 1) & (gy == ny - 1)
    pl.when(meets_early)(meet)

    planes, layers = (5, 3), (13, 12)

    def remote(src, dst, i, group, dx, dy):
        return pltpu.make_async_remote_copy(
            src_ref=src, dst_ref=dst, send_sem=hs_sem.at[group], recv_sem=hr_sem.at[i, group],
            device_id=target_of(dx, dy), device_id_type=MESH,
        )

    def beside(i, dx):
        part = pl.ds(0, planes[i])
        return remote(
            strips.at[i, :, part], land.at[i, 0 if dx > 0 else 1, pl.ds(1, rb_own), part], i, 0, dx, 0
        )

    def beside_all(i):
        both = land.at[i, :, pl.ds(1, rb_own), pl.ds(0, planes[i])]
        return remote(both, both, i, 0, 1, 0)

    def start_beyond(i, dy):
        at, group = (0, 1) if dy > 0 else (1, 2)
        part, rest = pl.ds(0, planes[i]), pl.ds(0, layers[i])
        remote(slab_out.at[i, at, rest], slab.at[i, at, rest], i, group, 0, dy).start()
        for dx in (1, -1):
            src = strips.at[i, pl.ds(rb_own - 1 if dy > 0 else 0, 1), part]
            dst = land.at[i, 0 if dx > 0 else 1, pl.ds(0 if dy > 0 else ext_tiles - 1, 1), part]
            remote(src, dst, i, group, dx, dy).start()

    def beyond_all(i, dy):
        every = counted.at[pl.ds(0, layers[i] + planes[i])]
        return remote(every, every, i, 1 if dy > 0 else 2, 1, 0)

    def clear(side):
        at = 0 if side == 0 else ext_tiles - 1
        slab[:, side] = jnp.zeros_like(slab[:, side])
        land[:, :, at] = jnp.zeros_like(land[:, :, at])

    pl.when(gy == 0)(lambda: clear(0))
    pl.when(gy == ny - 1)(lambda: clear(1))

    lane = lanes()
    sub = iota((8, 128), 0)

    def put_base(t, source, slots):
        for j in slots:
            base[j, band(t), :] = pick(source, (lane & -8) + j)

    def place_loads(ref, slot, sums):
        spread = None
        for t, total in enumerate(sums):
            total = jnp.broadcast_to(jnp.sum(total, axis=0, keepdims=True), (8, 128)) * (1.0 / (BLOCK * HALF))
            mine = pick(total, (lane & 15) * 8 + sub)
            here = lane // cb_own == t + rb_own * (gx % 2)
            spread = jnp.where(here, mine, 0.0 if spread is None else spread)
        ref[slot] = spread.astype(BF16)

    def two_parts(x):
        high = x.astype(BF16).astype(F32)
        return high, x - high

    def pack(i, f):
        ref = (*fields, base)[f]
        for at, t in enumerate((rb_own, 1)):
            if f == 3:
                edge = two_parts(st[(t - 1) * BLOCK : t * BLOCK, :] * (HALF * HALF))
                slab_out[i, at, 12] = jnp.concatenate(edge, axis=0).astype(BF16)
                continue
            for k in range(4):
                both = jnp.concatenate([ref[2 * k, band(t), :], ref[2 * k + 1, band(t), :]], axis=0)
                slab_out[i, at, 4 * f + k] = both.astype(BF16)
        packed = [None] * rb_own
        index = (lane & 7) + jnp.where(lane >= 64, cols - 8, 0)
        for j in range(8):
            here = (lane // 8) % 8 == j
            for b in range(rb_own):
                moved = pick(ref[j, band(b + 1), :], index)
                packed[b] = moved if j == 0 else jnp.where(here, moved, packed[b])
        for b in range(rb_own):
            parts = two_parts(packed[b]) if f == 3 else (packed[b],)
            for k, part in enumerate(parts):
                strips[i, b, f + k] = part.astype(BF16)

    def side_of(i, t, planes):
        west, east = (sum(land[i, side, t, k].astype(F32) for k in planes) for side in (0, 1))
        return jnp.where(lane >= 64, west, east)

    def assemble(i):
        for f, ref in enumerate(fields):
            for t in range(ext_tiles):
                ref[SIDE, band(t), :] = side_of(i, t, (f,))
            for at, t in enumerate((0, ext_tiles - 1)):
                for k in range(4):
                    both = slab[i, at, 4 * f + k].astype(F32)
                    ref[2 * k, band(t), :] = both[:8]
                    ref[2 * k + 1, band(t), :] = both[8:]

    def finish_base():
        for at, t in enumerate((0, ext_tiles - 1)):
            both = slab[0, at, 12].astype(F32)
            put_base(t, both[:8] + both[8:], range(8))
        for t in range(ext_tiles):
            base[SIDE, band(t), :] = side_of(0, t, (3, 4))

    def table(j, t, first, depth, wet):
        d = base[j, band(t), :]
        w = jnp.where(d > 0.0, 1.0, 0.0)
        part = pl.ds(t * BLOCK, BLOCK)
        for k in range(STEPS):
            depth[k, j, part, :] = d * KEEP ** -(first + k + 1)
            wet[k, j, part, :] = w * KEEP ** (first + k + 1)

    def own_tables(first, depth, wet):
        def fill(t, carry):
            for j in range(8):
                table(j, t, first, depth, wet)
            return carry

        lax.fori_loop(1, ext_tiles - 1, fill, 0)

    def edge_tables(first, depth, wet):
        for t in range(ext_tiles):
            for j in range(8) if t in (0, ext_tiles - 1) else ():
                table(j, t, first, depth, wet)
            table(SIDE, t, first, depth, wet)

    def gather(src, dst, group, device):
        return pltpu.make_async_remote_copy(
            src_ref=src, dst_ref=dst, send_sem=gs_sem, recv_sem=gr_sem.at[group],
            device_id=device, device_id_type=MESH,
        )

    def band_all():
        part = plane.at[pl.ds(0, nx - 1)]
        return gather(part, part, 0, target_of(1, 0))

    def column_all():
        part = pairs.at[pl.ds(0, ny - 1)]
        return gather(part, part, 1, target_of(1, 0))

    def everyone():
        part = tiles.at[pl.ds(0, n - 1)]
        return gather(part, part, 2, target_of(1, 0))

    def start_beside(i):
        for dx in (1, -1):
            beside(i, dx).start()

    def start_halos(i):
        start_beside(i)
        for dy in (1, -1):
            when(dy, True, lambda dy=dy: start_beyond(i, dy))

    def wait_halos(i):
        beside_all(i).wait_recv()
        for dy in (1, -1):
            when(dy, False, lambda dy=dy: beyond_all(i, dy).wait_recv())

    def finish_sends(i):
        beside_all(i).wait_send()
        for dy in (1, -1):
            when(dy, True, lambda dy=dy: beyond_all(i, dy).wait_send())

    def make_turning():
        for e in range(ext_tiles):
            row_ids = gy * rows - HALO + e * BLOCK + iota((BLOCK, cols), 0)
            turn[e] = (CORIOLIS / KEEP) * jnp.sin(latitude(row_ids, rows * ny))

    def make_green():
        t = iota((8, 128), 1)
        north = per_device
        south = north + cb_own
        west = south + cb_own
        east = west + rb_own + 2
        t_row = jnp.where(t < north, t // cb_own, jnp.where(t < south, -1, rb_own))
        t_col = jnp.where(t < north, t % cb_own, jnp.where(t < south, t - north, t - south))
        t_row = jnp.where(t >= east, t - east - 1, jnp.where(t >= west, t - west - 1, t_row))
        t_col = jnp.where(t >= east, cb_own, jnp.where(t >= west, -1, t_col))
        t_row = gy * rb_own + t_row
        t_col = gx * cb_own + t_col
        t_col = jnp.where(t_col < 0, t_col + coarse_cols, t_col)
        t_col = jnp.where(t_col >= coarse_cols, t_col - coarse_cols, t_col)
        target = unit_vectors(latitude(t_row, coarse_rows), longitude(t_col, coarse_cols))
        target = [jnp.broadcast_to(x[:1], (pair_rows, 128)) for x in target]

        def green_group(g, carry):
            p = g * 8 + iota((8, pair_rows), 0)
            k = iota((8, pair_rows), 1)
            s_col = ((p % (nx // 2)) * 2 + k // per_device) * cb_own + k % cb_own
            s_row = (p // (nx // 2)) * rb_own + (k % per_device) // cb_own
            source = unit_vectors(latitude(s_row, coarse_rows), longitude(s_col, coarse_cols))
            source = [jnp.transpose(x) for x in source]
            for j in range(8):
                square = None
                for s, t_vec in zip(source, target):
                    diff = jnp.broadcast_to(s[:, j : j + 1], (pair_rows, 128)) - t_vec
                    square = diff * diff if square is None else square + diff * diff
                value = GREEN_SCALE / (1.0 + jnp.sqrt(square) * (coarse_rows / math.pi))
                green[g * 8 + j] = value.astype(BF16)
            return carry

        lax.fori_loop(0, n // 16, green_group, 0)

    def load(i, ready=None):
        half = n // 4
        group = math.gcd(8, half)

        def pair(p):
            if i == 0:
                return pairs[p // (nx // 2), p % (nx // 2)].astype(F32)
            return tiles[2 * p].astype(F32) + tiles[2 * p + 1].astype(F32)

        def add_group(g, total):
            parts = []
            for first in range(0, group, max(group // 2, 1)):
                left, right = [], []
                for k in range(first, first + max(group // 2, 1)):
                    q = g * group + k
                    left.append(jnp.concatenate([pair(q), pair(q + half)], axis=0).astype(BF16))
                    right.append(jnp.concatenate([green[q], green[q + half]], axis=1))
                parts.append(
                    jnp.dot(jnp.concatenate(left, axis=1), jnp.concatenate(right, axis=0), preferred_element_type=F32)
                )
            return total + sum(parts)

        both = lax.fori_loop(0, half // group, add_group, jnp.zeros((2 * members, 256), F32))
        loading = both[:members, :128] + both[members:, 128:]
        l_out[...] = loading
        loading = loading * HALF
        north = per_device
        south = north + cb_own
        west = south + cb_own
        east = west + rb_own + 2
        own_member = (lane & 7) == sub
        sides = []
        for t in range(ext_tiles):
            first = north if t == 0 else south if t == ext_tiles - 1 else (t - 1) * cb_own
            main = pick(loading, lane // 8 + first)
            side = pick(loading, jnp.where(lane >= 64, west + t, east + t))
            both = []
            for value in (main, side):
                value = jnp.where(own_member, value, 0.0)
                if t == 0:
                    value = jnp.where(gy == 0, 0.0, value)
                if t == ext_tiles - 1:
                    value = jnp.where(gy == ny - 1, 0.0, value)
                both.append(jnp.broadcast_to(jnp.sum(value, axis=0, keepdims=True), (8, 128)))
            fine[t] = both[0]
            sides.append(both[1])
        if ready is not None:
            ready()
        for t in range(ext_tiles):
            for j in range(8):
                eta[j, band(t), :] = eta[j, band(t), :] - fine[t]
            eta[SIDE, band(t), :] = eta[SIDE, band(t), :] - sides[t]

    def interval(i):
        def step(n, carry):
            move_flow(ext_tiles, n, False, eta, pp, qq, pp, qq, depth0, turn)
            move_surface(ext_tiles, n, eta, eta, pp, qq, wet0)
            return carry

        lax.fori_loop(0, STEPS - 1, step, 0)
        move_flow(ext_tiles, STEPS - 1, True, eta, pp, qq, pp, qq, depth0, turn)
        sums = []
        for t in range(1, ext_tiles - 1):
            change = surface_change(t, STEPS - 1, False, pp, qq, wet0)
            total = None
            for j in range(8):
                value = eta[j, band(t), :] - change[j] + fine[t]
                eta[j, band(t), :] = value
                value = value * wet0[STEPS - 1, j, t * BLOCK : (t + 1) * BLOCK, :]
                total = value if total is None else total + value
            sums.append(total * KEEP ** -STEPS)
        return sums

    for copy in inputs[:3]:
        copy.wait()
    st[...] = jnp.where(in_o[...] > 0, in_d[...], 0.0)
    sums = []
    for t in range(1, ext_tiles - 1):
        part = slice((t - 1) * BLOCK, t * BLOCK)
        put_base(t, st[part, :] * (HALF * HALF), range(8))
        total = None
        for j, value in enumerate(exchange([[in3[0, m, part, :] for m in range(8)]])[0]):
            value = value * HALF
            eta[j, band(t), :] = value
            value = jnp.where(base[j, band(t), :] > 0.0, value, 0.0)
            total = value if total is None else total + value
        sums.append(total)
    place_loads(plane, gx, sums)

    def send_band():
        to_band(lambda device: gather(plane.at[gx], plane.at[gx], 0, device).start())

    pl.when(meets_early)(send_band)
    for copy in inputs[3:]:
        copy.wait()
    for f in (1, 2):
        for t in range(1, ext_tiles - 1):
            part = slice((t - 1) * BLOCK, t * BLOCK)
            for j, value in enumerate(exchange([[in3[f, m, part, :] for m in range(8)]])[0]):
                fields[f][j, band(t), :] = value * base[j, band(t), :]
    for f in range(4):
        pack(0, f)

    def meet_late():
        meet()
        send_band()

    pl.when(jnp.logical_not(meets_early))(meet_late)
    start_halos(0)

    make_turning()
    make_green()
    band_all().wait_recv()
    for k in range(nx // 2):
        pairs[gy, k] = (plane[2 * k].astype(F32) + plane[2 * k + 1].astype(F32)).astype(BF16)
    hear_answers()
    band_all().wait_send()
    to_column(lambda device: gather(pairs.at[gy], pairs.at[gy], 1, device).start())
    own_tables(0, depth0, wet0)
    wait_halos(0)
    assemble(0)
    finish_base()
    edge_tables(0, depth0, wet0)
    finish_sends(0)
    column_all().wait_send()
    column_all().wait_recv()
    load(0)
    place_loads(tiles, my_slot, interval(0))
    to_all_others(lambda device: gather(tiles.at[my_slot], tiles.at[my_slot], 2, device).start())
    for f in range(3):
        pack(1, f)
    start_halos(1)
    own_tables(STEPS, depth1, wet1)
    edge_tables(STEPS, depth1, wet1)
    for j in range(8):
        d = base[j, 2 * BLOCK : 2 * BLOCK + rows, :]
        restore[j] = jnp.where(d > 0.0, KEEP ** (2 * STEPS) / jnp.where(d > 0.0, d, 1.0), 0.0)
    finish_sends(1)
    everyone().wait_send()

    def halos_ready():
        wait_halos(1)
        assemble(1)

    everyone().wait_recv()
    load(1, halos_ready)


def finish(
    members, rows, cols,
    eta_in, p_in, q_in, depth, wet, turn, restore, fine, l_in,
    h_out, u_out, v_out, l_out,
    eta, pp, qq, staged, l_staged, sem,
):
    ext_tiles = (rows + 2 * HALO) // BLOCK
    blocks, width = l_staged.shape[1:]
    for b in range(blocks):
        l_staged[:, b, :] = l_in[:, b * width : (b + 1) * width]
    l_copy = pltpu.make_async_copy(l_staged, l_out, sem.at[3])
    l_copy.start()

    move_flow(ext_tiles, 0, False, eta_in, p_in, q_in, pp, qq, depth, turn)
    move_surface(ext_tiles, 0, eta_in, eta, pp, qq, wet)

    def step(n, carry):
        move_flow(ext_tiles, n, False, eta, pp, qq, pp, qq, depth, turn)
        move_surface(ext_tiles, n, eta, eta, pp, qq, wet)
        return carry

    lax.fori_loop(1, STEPS - 1, step, 0)
    move_flow(ext_tiles, STEPS - 1, True, eta, pp, qq, pp, qq, depth, turn)
    copies = [pltpu.make_async_copy(staged.at[f], out, sem.at[f]) for f, out in ((1, u_out), (2, v_out))]
    for t in range(rows // (BLOCK * TOGETHER)):
        part = pl.ds(t * BLOCK * TOGETHER, BLOCK * TOGETHER)
        copies.append(pltpu.make_async_copy(staged.at[0, :, part], h_out.at[:, part], sem.at[4 + t]))

    def place(f, first, groups):
        for k, values in enumerate(exchange(groups)):
            for m, value in enumerate(values):
                staged[f, m, (first + k - 1) * BLOCK : (first + k) * BLOCK, :] = value

    def flow(ref, t):
        return [ref[j, band(t), :] * restore[j, (t - 1) * BLOCK : t * BLOCK, :] for j in range(8)]

    def surface(t):
        change = surface_change(t, STEPS - 1, False, pp, qq, wet)
        return [(eta[j, band(t), :] - change[j] + fine[t]) * (1.0 / HALF) for j in range(8)]

    own = range(1, ext_tiles - 1, TOGETHER)
    for f, make in ((1, functools.partial(flow, pp)), (2, functools.partial(flow, qq)), (0, surface)):
        for first in own:
            place(f, first, [make(t) for t in range(first, first + TOGETHER)])
            if f == 0:
                copies[2 + first // TOGETHER].start()
        if f > 0:
            copies[f - 1].start()
    for copy in copies:
        copy.wait()
    l_copy.wait()


def shards(nx, ny, elevation, east_velocity, north_velocity, water_depth, land_sea):
    members, rows, cols = elevation.shape
    rb_own, cb_own = rows // BLOCK, cols // BLOCK
    n = nx * ny
    ext = rows + 2 * HALO
    tiles = ext // BLOCK
    hbm_spec = pl.BlockSpec(memory_space=pltpu.HBM)
    vmem_spec = pl.BlockSpec(memory_space=pltpu.VMEM)
    dma = pltpu.SemaphoreType.DMA
    field = (SLOTS, ext + 2 * BLOCK, cols)
    table = (STEPS, SLOTS, ext, cols)
    shape = (members, rows, cols)
    outs = tuple(
        jax.ShapeDtypeStruct(s, F32)
        for s in (
            field, field, field, table, table, (tiles, BLOCK, cols), (8, rows, cols), (tiles, BLOCK, cols),
            (members, 128),
        )
    )
    state = pl.pallas_call(
        functools.partial(kernel, nx, ny, members, rows, cols),
        out_shape=outs,
        in_specs=[hbm_spec] * 5,
        out_specs=(vmem_spec,) * len(outs),
        scratch_shapes=[
            pltpu.VMEM((3,) + shape, F32),
            pltpu.VMEM((rows, cols), F32),
            pltpu.VMEM((rows, cols), jnp.int32),
            pltpu.VMEM((INTERVALS, rb_own, 5, 8, cols), BF16),
            pltpu.VMEM((INTERVALS, 2, tiles, 5, 8, cols), BF16),
            pltpu.VMEM((INTERVALS, 2, 13, 16, cols), BF16),
            pltpu.VMEM((INTERVALS, 2, 13, 16, cols), BF16),
            pltpu.VMEM((18, 16, cols), BF16),
            pltpu.VMEM((rows, cols), F32),
            pltpu.VMEM(field, F32),
            pltpu.VMEM(table, F32),
            pltpu.VMEM(table, F32),
            pltpu.VMEM((n // 2, 2 * rb_own * cb_own, 128), BF16),
            pltpu.VMEM((nx, members, 2 * rb_own * cb_own), BF16),
            pltpu.VMEM((ny, nx // 2, members, 2 * rb_own * cb_own), BF16),
            pltpu.VMEM((n, members, 2 * rb_own * cb_own), BF16),
            dma((2,)),
            dma,
            dma((3,)),
            dma((3,)),
            dma((INTERVALS, 3)),
            pltpu.SemaphoreType.REGULAR,
        ],
        compiler_params=pltpu.CompilerParams(
            collective_id=0, has_side_effects=True, vmem_limit_bytes=40 * 1024 * 1024
        ),
        name="tide",
    )(
        *(
            pltpu.with_memory_space_constraint(x, pltpu.HBM)
            for x in (elevation, east_velocity, north_velocity, water_depth, land_sea)
        )
    )
    coarse = jax.ShapeDtypeStruct((members, rb_own, cb_own), F32)
    whole = jax.ShapeDtypeStruct(shape, F32)
    return pl.pallas_call(
        functools.partial(finish, members, rows, cols),
        out_shape=(whole, whole, whole, coarse),
        in_specs=[vmem_spec] * len(outs),
        out_specs=(hbm_spec,) * 4,
        scratch_shapes=[
            pltpu.VMEM(field, F32),
            pltpu.VMEM(field, F32),
            pltpu.VMEM(field, F32),
            pltpu.VMEM((3,) + shape, F32),
            pltpu.VMEM(coarse.shape, F32),
            dma((4 + rb_own,)),
        ],
        compiler_params=pltpu.CompilerParams(vmem_limit_bytes=8 * 1024 * 1024),
        name="finish",
    )(*state)


def solution(mesh):
    nx, ny = mesh.shape["gx"], mesh.shape["gy"]
    tile = P(None, "gy", "gx")
    return jax.shard_map(
        functools.partial(shards, nx, ny),
        mesh=mesh,
        in_specs=(tile, tile, tile, P("gy", "gx"), P("gy", "gx")),
        out_specs=(tile, tile, tile, tile),
        check_vma=False,
    )
```

```python
import functools
import math

import jax
import jax.numpy as jnp
from jax import lax
from jax.experimental import pallas as pl
from jax.experimental.pallas import tpu as pltpu
from jax.sharding import PartitionSpec as P

STEPS = 4
INTERVALS = 2
BLOCK = 8
HALO = 2 * STEPS

COURANT = 0.35
FRICTION = 0.02
CORIOLIS = 0.3
GREEN_SCALE = 0.25
KEEP = 1.0 - FRICTION
HALF = 0.5 * COURANT

MESH = pl.DeviceIdType.MESH
F32 = jnp.float32
BF16 = jnp.bfloat16

SIDE = 8
TOGETHER = 4
SLOTS = 9


def iota(shape, dim):
    return lax.broadcasted_iota(jnp.int32, shape, dim)


def latitude(row_ids, row_count):
    return ((row_ids.astype(F32) + 0.5) / row_count - 0.5) * jnp.pi


def longitude(col_ids, col_count):
    return (col_ids.astype(F32) + 0.5) / col_count * (2.0 * jnp.pi)


def unit_vectors(lat_angle, lon_angle):
    cos_lat = jnp.cos(lat_angle)
    return (cos_lat * jnp.cos(lon_angle), cos_lat * jnp.sin(lon_angle), jnp.sin(lat_angle))


def lanes():
    return iota((8, 128), 1)


def pick(x, index):
    return jnp.take_along_axis(x, index, axis=1)


def exchange(groups):
    lane = lanes()
    groups = [list(values) for values in groups]
    for bit in range(3):
        step = 1 << bit
        low = (lane & step) == 0
        index = lane ^ step
        for values in groups:
            for a in range(8):
                if a & step:
                    continue
                b = a | step
                moved = pick(jnp.where(low, values[b], values[a]), index)
                values[a], values[b] = jnp.where(low, values[a], moved), jnp.where(low, moved, values[b])
    return groups


def band(t):
    return pl.ds(BLOCK + t * BLOCK, BLOCK)


def shifted(t, by):
    return pl.ds(BLOCK + t * BLOCK + by, BLOCK)


def x_differences(values, with_side=True):
    lane = lanes()
    first, last = lane < 8, lane >= 120
    up_main, up_side = pltpu.roll(values[7], 8, 1), pltpu.roll(values[SIDE], 8, 1)
    down_main, down_side = pltpu.roll(values[0], 120, 1), pltpu.roll(values[SIDE], 120, 1)
    left = [jnp.where(first, up_side, up_main)] + values[:7]
    right = values[1:8] + [jnp.where(last, down_side, down_main)]
    if with_side:
        left.append(jnp.where(first, up_main, up_side))
        right.append(jnp.where(last, down_main, down_side))
    return [r - l for l, r in zip(left, right)]


def move_flow(tiles, n, last, eta, p_in, q_in, p_out, q_out, depth, turn):
    for t in range(tiles):
        inner = not last or 0 < t < tiles - 1
        coriolis = turn[t]
        if inner:
            diff = x_differences([eta[j, band(t), :] for j in range(SLOTS)])
        for j in range(SLOTS if inner else SIDE):
            d = depth[n, j, t * BLOCK : (t + 1) * BLOCK, :]
            p, q = p_in[j, band(t), :], q_in[j, band(t), :]
            if inner:
                p_out[j, band(t), :] = p + coriolis * q - d * diff[j]
            north = eta[j, shifted(t, 1), :] - eta[j, shifted(t, -1), :]
            q_out[j, band(t), :] = q - coriolis * p - d * north


def surface_change(t, n, with_side, p, q, wet):
    diff = x_differences([p[j, band(t), :] for j in range(SLOTS)], with_side)
    return [
        wet[n, j, t * BLOCK : (t + 1) * BLOCK, :]
        * (diff[j] + (q[j, shifted(t, 1), :] - q[j, shifted(t, -1), :]))
        for j in range(SLOTS if with_side else SIDE)
    ]


def move_surface(tiles, n, eta_in, eta_out, p, q, wet):
    for t in range(tiles):
        change = surface_change(t, n, True, p, q, wet)
        for j in range(SLOTS):
            eta_out[j, band(t), :] = eta_in[j, band(t), :] - change[j]


def kernel(
    nx, ny, members, rows, cols,
    h_in, u_in, v_in, d_in, o_in,
    eta, pp, qq, depth1, wet1, turn, restore, fine, l_out,
    in3, in_d, in_o, strips, land, slab_out, slab, counted, st, base, depth0, wet0, green, plane, pairs, tiles,
    in_sem, gs_sem, gr_sem, hs_sem, hr_sem, up_sem,
):
    gx, gy = lax.axis_index("gx"), lax.axis_index("gy")
    n = nx * ny
    rb_own, cb_own = rows // BLOCK, cols // BLOCK
    per_device = rb_own * cb_own
    pair_rows = 2 * per_device
    coarse_rows, coarse_cols = rb_own * ny, cb_own * nx
    ext = rows + 2 * HALO
    ext_tiles = ext // BLOCK
    my_slot = gy * nx + gx
    fields = (eta, pp, qq)

    inputs = [
        pltpu.make_async_copy(src, dst, done)
        for src, dst, done in (
            (d_in, in_d, hs_sem.at[0]), (o_in, in_o, hs_sem.at[1]), (h_in, in3.at[0], hs_sem.at[2]),
            (u_in, in3.at[1], in_sem.at[0]), (v_in, in3.at[2], in_sem.at[1]),
        )
    ]
    for copy in inputs:
        copy.start()

    def wrap(index, size):
        return jnp.where(index >= size, index - size, index)

    def to_all_others(fn):
        far = 2 * (nx // 2 - 1 - gx // 2)

        def column(k, carry):
            x = wrap(far + k, nx)

            def all_rows():
                for dy in range(ny):
                    fn({"gx": x, "gy": wrap(ny - 1 - gy + dy, ny)})

            pl.when(x != gx)(all_rows)
            return carry

        lax.fori_loop(0, nx, column, 0)
        to_column(fn)

    def to_band(fn):
        def one(dx, carry):
            fn({"gx": wrap(gx + dx, nx), "gy": gy})
            return carry

        lax.fori_loop(1, nx, one, 0)

    def to_column(fn):
        for dy in range(1, ny):
            fn({"gx": gx, "gy": wrap(gy + dy, ny)})

    barrier = pltpu.get_barrier_semaphore()

    def greet(device):
        pl.semaphore_signal(barrier, inc=1, device_id=device, device_id_type=MESH)


    def target_of(dx, dy):
        return {"gx": wrap(jnp.where(gx + dx < 0, gx + dx + nx, gx + dx), nx), "gy": gy + dy}

    def when(dy, sending, fn):
        if dy == 0:
            fn()
        else:
            beyond = gy + (dy if sending else -dy)
            pl.when((beyond >= 0) & (beyond < ny))(fn)

    def further(up, fn):
        for dy in range(2, ny):
            inside = gy + dy < ny if up else gy - dy >= 0
            pl.when(inside)(lambda dy=dy: fn({"gx": gx, "gy": gy + dy if up else gy - dy}))

    def greet_beyond(dy):
        for dx in (0, 1, -1):
            greet(target_of(dx, dy))

    to_band(greet)
    for dy in (1, -1):
        when(dy, True, lambda dy=dy: greet_beyond(dy))
    further(True, greet)

    def meet():
        below, above = jnp.where(gy > 0, gy + 2, 0), jnp.where(gy < ny - 1, 3, 0)
        pl.semaphore_wait(barrier, nx - 1 + below + above)
        further(
            False,
            lambda device: pl.semaphore_signal(up_sem, inc=1, device_id=device, device_id_type=MESH),
        )

    def hear_answers():
        pl.when(gy < ny - 2)(lambda: pl.semaphore_wait(up_sem, ny - 2 - gy))

    meets_early = (gx // 2 == nx // 2 - 1) & (gy == ny - 1)
    pl.when(meets_early)(meet)

    planes, layers = (5, 3), (13, 12)

    def remote(src, dst, i, group, dx, dy):
        return pltpu.make_async_remote_copy(
            src_ref=src, dst_ref=dst, send_sem=hs_sem.at[group], recv_sem=hr_sem.at[i, group],
            device_id=target_of(dx, dy), device_id_type=MESH,
        )

    def beside(i, dx):
        part = pl.ds(0, planes[i])
        return remote(
            strips.at[i, :, part], land.at[i, 0 if dx > 0 else 1, pl.ds(1, rb_own), part], i, 0, dx, 0
        )

    def beside_all(i):
        both = land.at[i, :, pl.ds(1, rb_own), pl.ds(0, planes[i])]
        return remote(both, both, i, 0, 1, 0)

    def start_beyond(i, dy):
        at, group = (0, 1) if dy > 0 else (1, 2)
        part, rest = pl.ds(0, planes[i]), pl.ds(0, layers[i])
        remote(slab_out.at[i, at, rest], slab.at[i, at, rest], i, group, 0, dy).start()
        for dx in (1, -1):
            src = strips.at[i, pl.ds(rb_own - 1 if dy > 0 else 0, 1), part]
            dst = land.at[i, 0 if dx > 0 else 1, pl.ds(0 if dy > 0 else ext_tiles - 1, 1), part]
            remote(src, dst, i, group, dx, dy).start()

    def beyond_all(i, dy):
        every = counted.at[pl.ds(0, layers[i] + planes[i])]
        return remote(every, every, i, 1 if dy > 0 else 2, 1, 0)

    def clear(side):
        at = 0 if side == 0 else ext_tiles - 1
        slab[:, side] = jnp.zeros_like(slab[:, side])
        land[:, :, at] = jnp.zeros_like(land[:, :, at])

    pl.when(gy == 0)(lambda: clear(0))
    pl.when(gy == ny - 1)(lambda: clear(1))

    lane = lanes()
    sub = iota((8, 128), 0)

    def put_base(t, source, slots):
        for j in slots:
            base[j, band(t), :] = pick(source, (lane & -8) + j)

    def place_loads(ref, slot, sums):
        spread = None
        for t, total in enumerate(sums):
            total = jnp.broadcast_to(jnp.sum(total, axis=0, keepdims=True), (8, 128)) * (1.0 / (BLOCK * HALF))
            mine = pick(total, (lane & 15) * 8 + sub)
            here = lane // cb_own == t + rb_own * (gx % 2)
            spread = jnp.where(here, mine, 0.0 if spread is None else spread)
        ref[slot] = spread.astype(BF16)

    def two_parts(x):
        high = x.astype(BF16).astype(F32)
        return high, x - high

    def pack(i, f):
        ref = (*fields, base)[f]
        for at, t in enumerate((rb_own, 1)):
            if f == 3:
                edge = two_parts(st[(t - 1) * BLOCK : t * BLOCK, :] * (HALF * HALF))
                slab_out[i, at, 12] = jnp.concatenate(edge, axis=0).astype(BF16)
                continue
            for k in range(4):
                both = jnp.concatenate([ref[2 * k, band(t), :], ref[2 * k + 1, band(t), :]], axis=0)
                slab_out[i, at, 4 * f + k] = both.astype(BF16)
        packed = [None] * rb_own
        index = (lane & 7) + jnp.where(lane >= 64, cols - 8, 0)
        for j in range(8):
            here = (lane // 8) % 8 == j
            for b in range(rb_own):
                moved = pick(ref[j, band(b + 1), :], index)
                packed[b] = moved if j == 0 else jnp.where(here, moved, packed[b])
        for b in range(rb_own):
            parts = two_parts(packed[b]) if f == 3 else (packed[b],)
            for k, part in enumerate(parts):
                strips[i, b, f + k] = part.astype(BF16)

    def side_of(i, t, planes):
        west, east = (sum(land[i, side, t, k].astype(F32) for k in planes) for side in (0, 1))
        return jnp.where(lane >= 64, west, east)

    def assemble(i):
        for f, ref in enumerate(fields):
            for t in range(ext_tiles):
                ref[SIDE, band(t), :] = side_of(i, t, (f,))
            for at, t in enumerate((0, ext_tiles - 1)):
                for k in range(4):
                    both = slab[i, at, 4 * f + k].astype(F32)
                    ref[2 * k, band(t), :] = both[:8]
                    ref[2 * k + 1, band(t), :] = both[8:]

    def finish_base():
        for at, t in enumerate((0, ext_tiles - 1)):
            both = slab[0, at, 12].astype(F32)
            put_base(t, both[:8] + both[8:], range(8))
        for t in range(ext_tiles):
            base[SIDE, band(t), :] = side_of(0, t, (3, 4))

    def table(j, t, first, depth, wet):
        d = base[j, band(t), :]
        w = jnp.where(d > 0.0, 1.0, 0.0)
        part = pl.ds(t * BLOCK, BLOCK)
        for k in range(STEPS):
            depth[k, j, part, :] = d * KEEP ** -(first + k + 1)
            wet[k, j, part, :] = w * KEEP ** (first + k + 1)

    def own_tables(first, depth, wet):
        def fill(t, carry):
            for j in range(8):
                table(j, t, first, depth, wet)
            return carry

        lax.fori_loop(1, ext_tiles - 1, fill, 0)

    def edge_tables(first, depth, wet):
        for t in range(ext_tiles):
            for j in range(8) if t in (0, ext_tiles - 1) else ():
                table(j, t, first, depth, wet)
            table(SIDE, t, first, depth, wet)

    def gather(src, dst, group, device):
        return pltpu.make_async_remote_copy(
            src_ref=src, dst_ref=dst, send_sem=gs_sem, recv_sem=gr_sem.at[group],
            device_id=device, device_id_type=MESH,
        )

    def band_all():
        part = plane.at[pl.ds(0, nx - 1)]
        return gather(part, part, 0, target_of(1, 0))

    def column_all():
        part = pairs.at[pl.ds(0, ny - 1)]
        return gather(part, part, 1, target_of(1, 0))

    def everyone():
        part = tiles.at[pl.ds(0, n - 1)]
        return gather(part, part, 2, target_of(1, 0))

    def start_beside(i):
        for dx in (1, -1):
            beside(i, dx).start()

    def start_halos(i):
        start_beside(i)
        for dy in (1, -1):
            when(dy, True, lambda dy=dy: start_beyond(i, dy))

    def wait_halos(i):
        beside_all(i).wait_recv()
        for dy in (1, -1):
            when(dy, False, lambda dy=dy: beyond_all(i, dy).wait_recv())

    def finish_sends(i):
        beside_all(i).wait_send()
        for dy in (1, -1):
            when(dy, True, lambda dy=dy: beyond_all(i, dy).wait_send())

    def make_turning():
        for e in range(ext_tiles):
            row_ids = gy * rows - HALO + e * BLOCK + iota((BLOCK, cols), 0)
            turn[e] = (CORIOLIS / KEEP) * jnp.sin(latitude(row_ids, rows * ny))

    def make_green():
        t = iota((8, 128), 1)
        north = per_device
        south = north + cb_own
        west = south + cb_own
        east = west + rb_own + 2
        t_row = jnp.where(t < north, t // cb_own, jnp.where(t < south, -1, rb_own))
        t_col = jnp.where(t < north, t % cb_own, jnp.where(t < south, t - north, t - south))
        t_row = jnp.where(t >= east, t - east - 1, jnp.where(t >= west, t - west - 1, t_row))
        t_col = jnp.where(t >= east, cb_own, jnp.where(t >= west, -1, t_col))
        t_row = gy * rb_own + t_row
        t_col = gx * cb_own + t_col
        t_col = jnp.where(t_col < 0, t_col + coarse_cols, t_col)
        t_col = jnp.where(t_col >= coarse_cols, t_col - coarse_cols, t_col)
        target = unit_vectors(latitude(t_row, coarse_rows), longitude(t_col, coarse_cols))
        target = [jnp.broadcast_to(x[:1], (pair_rows, 128)) for x in target]

        def green_group(g, carry):
            p = g * 8 + iota((8, pair_rows), 0)
            k = iota((8, pair_rows), 1)
            s_col = ((p % (nx // 2)) * 2 + k // per_device) * cb_own + k % cb_own
            s_row = (p // (nx // 2)) * rb_own + (k % per_device) // cb_own
            source = unit_vectors(latitude(s_row, coarse_rows), longitude(s_col, coarse_cols))
            source = [jnp.transpose(x) for x in source]
            for j in range(8):
                square = None
                for s, t_vec in zip(source, target):
                    diff = jnp.broadcast_to(s[:, j : j + 1], (pair_rows, 128)) - t_vec
                    square = diff * diff if square is None else square + diff * diff
                value = GREEN_SCALE / (1.0 + jnp.sqrt(square) * (coarse_rows / math.pi))
                green[g * 8 + j] = value.astype(BF16)
            return carry

        lax.fori_loop(0, n // 16, green_group, 0)

    def load(i, ready=None):
        half = n // 4
        group = math.gcd(8, half)

        def pair(p):
            if i == 0:
                return pairs[p // (nx // 2), p % (nx // 2)].astype(F32)
            return tiles[2 * p].astype(F32) + tiles[2 * p + 1].astype(F32)

        def add_group(g, total):
            parts = []
            for first in range(0, group, max(group // 2, 1)):
                left, right = [], []
                for k in range(first, first + max(group // 2, 1)):
                    q = g * group + k
                    left.append(jnp.concatenate([pair(q), pair(q + half)], axis=0).astype(BF16))
                    right.append(jnp.concatenate([green[q], green[q + half]], axis=1))
                parts.append(
                    jnp.dot(jnp.concatenate(left, axis=1), jnp.concatenate(right, axis=0), preferred_element_type=F32)
                )
            return total + sum(parts)

        both = lax.fori_loop(0, half // group, add_group, jnp.zeros((2 * members, 256), F32))
        loading = both[:members, :128] + both[members:, 128:]
        l_out[...] = loading
        loading = loading * HALF
        north = per_device
        south = north + cb_own
        west = south + cb_own
        east = west + rb_own + 2
        own_member = (lane & 7) == sub
        sides = []
        for t in range(ext_tiles):
            first = north if t == 0 else south if t == ext_tiles - 1 else (t - 1) * cb_own
            main = pick(loading, lane // 8 + first)
            side = pick(loading, jnp.where(lane >= 64, west + t, east + t))
            both = []
            for value in (main, side):
                value = jnp.where(own_member, value, 0.0)
                if t == 0:
                    value = jnp.where(gy == 0, 0.0, value)
                if t == ext_tiles - 1:
                    value = jnp.where(gy == ny - 1, 0.0, value)
                both.append(jnp.broadcast_to(jnp.sum(value, axis=0, keepdims=True), (8, 128)))
            fine[t] = both[0]
            sides.append(both[1])
        if ready is not None:
            ready()
        for t in range(ext_tiles):
            for j in range(8):
                eta[j, band(t), :] = eta[j, band(t), :] - fine[t]
            eta[SIDE, band(t), :] = eta[SIDE, band(t), :] - sides[t]

    def interval(i):
        def step(n, carry):
            move_flow(ext_tiles, n, False, eta, pp, qq, pp, qq, depth0, turn)
            move_surface(ext_tiles, n, eta, eta, pp, qq, wet0)
            return carry

        lax.fori_loop(0, STEPS - 1, step, 0)
        move_flow(ext_tiles, STEPS - 1, True, eta, pp, qq, pp, qq, depth0, turn)
        sums = []
        for t in range(1, ext_tiles - 1):
            change = surface_change(t, STEPS - 1, False, pp, qq, wet0)
            total = None
            for j in range(8):
                value = eta[j, band(t), :] - change[j] + fine[t]
                eta[j, band(t), :] = value
                value = value * wet0[STEPS - 1, j, t * BLOCK : (t + 1) * BLOCK, :]
                total = value if total is None else total + value
            sums.append(total * KEEP ** -STEPS)
        return sums

    for copy in inputs[:3]:
        copy.wait()
    st[...] = jnp.where(in_o[...] > 0, in_d[...], 0.0)
    sums = []
    for t in range(1, ext_tiles - 1):
        part = slice((t - 1) * BLOCK, t * BLOCK)
        put_base(t, st[part, :] * (HALF * HALF), range(8))
        total = None
        for j, value in enumerate(exchange([[in3[0, m, part, :] for m in range(8)]])[0]):
            value = value * HALF
            eta[j, band(t), :] = value
            value = jnp.where(base[j, band(t), :] > 0.0, value, 0.0)
            total = value if total is None else total + value
        sums.append(total)
    place_loads(plane, gx, sums)

    def send_band():
        to_band(lambda device: gather(plane.at[gx], plane.at[gx], 0, device).start())

    pl.when(meets_early)(send_band)
    for copy in inputs[3:]:
        copy.wait()
    for f in (1, 2):
        for t in range(1, ext_tiles - 1):
            part = slice((t - 1) * BLOCK, t * BLOCK)
            for j, value in enumerate(exchange([[in3[f, m, part, :] for m in range(8)]])[0]):
                fields[f][j, band(t), :] = value * base[j, band(t), :]
    for f in range(4):
        pack(0, f)

    def meet_late():
        meet()
        send_band()

    pl.when(jnp.logical_not(meets_early))(meet_late)
    start_halos(0)

    make_turning()
    make_green()
    band_all().wait_recv()
    for k in range(nx // 2):
        pairs[gy, k] = (plane[2 * k].astype(F32) + plane[2 * k + 1].astype(F32)).astype(BF16)
    hear_answers()
    band_all().wait_send()
    to_column(lambda device: gather(pairs.at[gy], pairs.at[gy], 1, device).start())
    own_tables(0, depth0, wet0)
    wait_halos(0)
    assemble(0)
    finish_base()
    edge_tables(0, depth0, wet0)
    finish_sends(0)
    column_all().wait_send()
    column_all().wait_recv()
    load(0)
    place_loads(tiles, my_slot, interval(0))
    to_all_others(lambda device: gather(tiles.at[my_slot], tiles.at[my_slot], 2, device).start())
    for f in range(3):
        pack(1, f)
    start_halos(1)
    own_tables(STEPS, depth1, wet1)
    edge_tables(STEPS, depth1, wet1)
    for j in range(8):
        d = base[j, 2 * BLOCK : 2 * BLOCK + rows, :]
        restore[j] = jnp.where(d > 0.0, KEEP ** (2 * STEPS) / jnp.where(d > 0.0, d, 1.0), 0.0)
    finish_sends(1)
    everyone().wait_send()

    def halos_ready():
        wait_halos(1)
        assemble(1)

    everyone().wait_recv()
    load(1, halos_ready)


def finish(
    members, rows, cols,
    eta_in, p_in, q_in, depth, wet, turn, restore, fine, l_in,
    h_out, u_out, v_out, l_out,
    eta, pp, qq, staged, l_staged, sem,
):
    ext_tiles = (rows + 2 * HALO) // BLOCK
    blocks, width = l_staged.shape[1:]
    for b in range(blocks):
        l_staged[:, b, :] = l_in[:, b * width : (b + 1) * width]
    l_copy = pltpu.make_async_copy(l_staged, l_out, sem.at[3])
    l_copy.start()

    move_flow(ext_tiles, 0, False, eta_in, p_in, q_in, pp, qq, depth, turn)
    move_surface(ext_tiles, 0, eta_in, eta, pp, qq, wet)

    def step(n, carry):
        move_flow(ext_tiles, n, False, eta, pp, qq, pp, qq, depth, turn)
        move_surface(ext_tiles, n, eta, eta, pp, qq, wet)
        return carry

    lax.fori_loop(1, STEPS - 1, step, 0)
    move_flow(ext_tiles, STEPS - 1, True, eta, pp, qq, pp, qq, depth, turn)
    copies = [pltpu.make_async_copy(staged.at[f], out, sem.at[f]) for f, out in ((1, u_out), (2, v_out))]
    for t in range(rows // (BLOCK * TOGETHER)):
        part = pl.ds(t * BLOCK * TOGETHER, BLOCK * TOGETHER)
        copies.append(pltpu.make_async_copy(staged.at[0, :, part], h_out.at[:, part], sem.at[4 + t]))

    def place(f, first, groups):
        for k, values in enumerate(exchange(groups)):
            for m, value in enumerate(values):
                staged[f, m, (first + k - 1) * BLOCK : (first + k) * BLOCK, :] = value

    def flow(ref, t):
        return [ref[j, band(t), :] * restore[j, (t - 1) * BLOCK : t * BLOCK, :] for j in range(8)]

    def surface(t):
        change = surface_change(t, STEPS - 1, False, pp, qq, wet)
        return [(eta[j, band(t), :] - change[j] + fine[t]) * (1.0 / HALF) for j in range(8)]

    own = range(1, ext_tiles - 1, TOGETHER)
    for f, make in ((1, functools.partial(flow, pp)), (2, functools.partial(flow, qq)), (0, surface)):
        for first in own:
            place(f, first, [make(t) for t in range(first, first + TOGETHER)])
            if f == 0:
                copies[2 + first // TOGETHER].start()
        if f > 0:
            copies[f - 1].start()
    for copy in copies:
        copy.wait()
    l_copy.wait()


def shards(nx, ny, elevation, east_velocity, north_velocity, water_depth, land_sea):
    members, rows, cols = elevation.shape
    rb_own, cb_own = rows // BLOCK, cols // BLOCK
    n = nx * ny
    ext = rows + 2 * HALO
    tiles = ext // BLOCK
    hbm_spec = pl.BlockSpec(memory_space=pltpu.HBM)
    vmem_spec = pl.BlockSpec(memory_space=pltpu.VMEM)
    dma = pltpu.SemaphoreType.DMA
    field = (SLOTS, ext + 2 * BLOCK, cols)
    table = (STEPS, SLOTS, ext, cols)
    shape = (members, rows, cols)
    outs = tuple(
        jax.ShapeDtypeStruct(s, F32)
        for s in (
            field, field, field, table, table, (tiles, BLOCK, cols), (8, rows, cols), (tiles, BLOCK, cols),
            (members, 128),
        )
    )
    state = pl.pallas_call(
        functools.partial(kernel, nx, ny, members, rows, cols),
        out_shape=outs,
        in_specs=[hbm_spec] * 5,
        out_specs=(vmem_spec,) * len(outs),
        scratch_shapes=[
            pltpu.VMEM((3,) + shape, F32),
            pltpu.VMEM((rows, cols), F32),
            pltpu.VMEM((rows, cols), jnp.int32),
            pltpu.VMEM((INTERVALS, rb_own, 5, 8, cols), BF16),
            pltpu.VMEM((INTERVALS, 2, tiles, 5, 8, cols), BF16),
            pltpu.VMEM((INTERVALS, 2, 13, 16, cols), BF16),
            pltpu.VMEM((INTERVALS, 2, 13, 16, cols), BF16),
            pltpu.VMEM((18, 16, cols), BF16),
            pltpu.VMEM((rows, cols), F32),
            pltpu.VMEM(field, F32),
            pltpu.VMEM(table, F32),
            pltpu.VMEM(table, F32),
            pltpu.VMEM((n // 2, 2 * rb_own * cb_own, 128), BF16),
            pltpu.VMEM((nx, members, 2 * rb_own * cb_own), BF16),
            pltpu.VMEM((ny, nx // 2, members, 2 * rb_own * cb_own), BF16),
            pltpu.VMEM((n, members, 2 * rb_own * cb_own), BF16),
            dma((2,)),
            dma,
            dma((3,)),
            dma((3,)),
            dma((INTERVALS, 3)),
            pltpu.SemaphoreType.REGULAR,
        ],
        compiler_params=pltpu.CompilerParams(
            collective_id=0, has_side_effects=True, vmem_limit_bytes=40 * 1024 * 1024
        ),
        name="tide",
    )(
        *(
            pltpu.with_memory_space_constraint(x, pltpu.HBM)
            for x in (elevation, east_velocity, north_velocity, water_depth, land_sea)
        )
    )
    coarse = jax.ShapeDtypeStruct((members, rb_own, cb_own), F32)
    whole = jax.ShapeDtypeStruct(shape, F32)
    return pl.pallas_call(
        functools.partial(finish, members, rows, cols),
        out_shape=(whole, whole, whole, coarse),
        in_specs=[vmem_spec] * len(outs),
        out_specs=(hbm_spec,) * 4,
        scratch_shapes=[
            pltpu.VMEM(field, F32),
            pltpu.VMEM(field, F32),
            pltpu.VMEM(field, F32),
            pltpu.VMEM((3,) + shape, F32),
            pltpu.VMEM(coarse.shape, F32),
            dma((4 + rb_own,)),
        ],
        compiler_params=pltpu.CompilerParams(vmem_limit_bytes=8 * 1024 * 1024),
        name="finish",
    )(*state)


def solution(mesh):
    nx, ny = mesh.shape["gx"], mesh.shape["gy"]
    tile = P(None, "gy", "gx")
    return jax.shard_map(
        functools.partial(shards, nx, ny),
        mesh=mesh,
        in_specs=(tile, tile, tile, P("gy", "gx"), P("gy", "gx")),
        out_specs=(tile, tile, tile, tile),
        check_vma=False,
    )
```

```python
import functools
import math

import jax
import jax.numpy as jnp
from jax import lax
from jax.experimental import pallas as pl
from jax.experimental.pallas import tpu as pltpu
from jax.sharding import PartitionSpec as P

STEPS = 4
INTERVALS = 2
BLOCK = 8
HALO = 2 * STEPS

COURANT = 0.35
FRICTION = 0.02
CORIOLIS = 0.3
GREEN_SCALE = 0.25
KEEP = 1.0 - FRICTION
HALF = 0.5 * COURANT

MESH = pl.DeviceIdType.MESH
F32 = jnp.float32
BF16 = jnp.bfloat16

SIDE = 8
TOGETHER = 4
SLOTS = 9


def iota(shape, dim):
    return lax.broadcasted_iota(jnp.int32, shape, dim)


def latitude(row_ids, row_count):
    return ((row_ids.astype(F32) + 0.5) / row_count - 0.5) * jnp.pi


def longitude(col_ids, col_count):
    return (col_ids.astype(F32) + 0.5) / col_count * (2.0 * jnp.pi)


def unit_vectors(lat_angle, lon_angle):
    cos_lat = jnp.cos(lat_angle)
    return (cos_lat * jnp.cos(lon_angle), cos_lat * jnp.sin(lon_angle), jnp.sin(lat_angle))


def lanes():
    return iota((8, 128), 1)


def pick(x, index):
    return jnp.take_along_axis(x, index, axis=1)


def exchange(groups):
    lane = lanes()
    groups = [list(values) for values in groups]
    for bit in range(3):
        step = 1 << bit
        low = (lane & step) == 0
        index = lane ^ step
        for values in groups:
            for a in range(8):
                if a & step:
                    continue
                b = a | step
                moved = pick(jnp.where(low, values[b], values[a]), index)
                values[a], values[b] = jnp.where(low, values[a], moved), jnp.where(low, moved, values[b])
    return groups


def band(t):
    return pl.ds(BLOCK + t * BLOCK, BLOCK)


def shifted(t, by):
    return pl.ds(BLOCK + t * BLOCK + by, BLOCK)


def x_differences(values, with_side=True):
    lane = lanes()
    first, last = lane < 8, lane >= 120
    up_main, up_side = pltpu.roll(values[7], 8, 1), pltpu.roll(values[SIDE], 8, 1)
    down_main, down_side = pltpu.roll(values[0], 120, 1), pltpu.roll(values[SIDE], 120, 1)
    left = [jnp.where(first, up_side, up_main)] + values[:7]
    right = values[1:8] + [jnp.where(last, down_side, down_main)]
    if with_side:
        left.append(jnp.where(first, up_main, up_side))
        right.append(jnp.where(last, down_main, down_side))
    return [r - l for l, r in zip(left, right)]


def move_flow(tiles, n, last, eta, p_in, q_in, p_out, q_out, depth, turn):
    for t in range(tiles):
        inner = not last or 0 < t < tiles - 1
        coriolis = turn[t]
        if inner:
            diff = x_differences([eta[j, band(t), :] for j in range(SLOTS)])
        for j in range(SLOTS if inner else SIDE):
            d = depth[n, j, t * BLOCK : (t + 1) * BLOCK, :]
            p, q = p_in[j, band(t), :], q_in[j, band(t), :]
            if inner:
                p_out[j, band(t), :] = p + coriolis * q - d * diff[j]
            north = eta[j, shifted(t, 1), :] - eta[j, shifted(t, -1), :]
            q_out[j, band(t), :] = q - coriolis * p - d * north


def surface_change(t, n, with_side, p, q, wet):
    diff = x_differences([p[j, band(t), :] for j in range(SLOTS)], with_side)
    return [
        wet[n, j, t * BLOCK : (t + 1) * BLOCK, :]
        * (diff[j] + (q[j, shifted(t, 1), :] - q[j, shifted(t, -1), :]))
        for j in range(SLOTS if with_side else SIDE)
    ]


def move_surface(tiles, n, eta_in, eta_out, p, q, wet):
    for t in range(tiles):
        change = surface_change(t, n, True, p, q, wet)
        for j in range(SLOTS):
            eta_out[j, band(t), :] = eta_in[j, band(t), :] - change[j]


def kernel(
    nx, ny, members, rows, cols,
    h_in, u_in, v_in, d_in, o_in,
    eta, pp, qq, depth1, wet1, turn, restore, fine, l_out,
    in3, in_d, in_o, strips, land, slab_out, slab, counted, st, base, depth0, wet0, green, plane, pairs, tiles,
    in_sem, gs_sem, gr_sem, hs_sem, hr_sem, up_sem,
):
    gx, gy = lax.axis_index("gx"), lax.axis_index("gy")
    n = nx * ny
    rb_own, cb_own = rows // BLOCK, cols // BLOCK
    per_device = rb_own * cb_own
    pair_rows = 2 * per_device
    coarse_rows, coarse_cols = rb_own * ny, cb_own * nx
    ext = rows + 2 * HALO
    ext_tiles = ext // BLOCK
    my_slot = gy * nx + gx
    fields = (eta, pp, qq)

    inputs = [
        pltpu.make_async_copy(src, dst, done)
        for src, dst, done in (
            (d_in, in_d, hs_sem.at[0]), (o_in, in_o, hs_sem.at[1]), (h_in, in3.at[0], hs_sem.at[2]),
            (u_in, in3.at[1], in_sem.at[0]), (v_in, in3.at[2], in_sem.at[1]),
        )
    ]
    for copy in inputs:
        copy.start()

    def wrap(index, size):
        return jnp.where(index >= size, index - size, index)

    far = 2 * (nx // 2 - 1 - gx // 2)

    def to_column(fn):
        for dy in range(ny):
            y = wrap(ny - 1 - gy + dy, ny)
            pl.when(y != gy)(lambda y=y: fn({"gx": gx, "gy": y}))

    def to_band(fn):
        def one(k, carry):
            x = wrap(far + k, nx)
            pl.when(x != gx)(lambda: fn({"gx": x, "gy": gy}))
            return carry

        lax.fori_loop(0, nx, one, 0)

    def to_all_others(fn):
        def column(k, carry):
            x = wrap(far + k, nx)

            def all_rows():
                for dy in range(ny):
                    fn({"gx": x, "gy": wrap(ny - 1 - gy + dy, ny)})

            pl.when(x != gx)(all_rows)
            return carry

        lax.fori_loop(0, nx, column, 0)
        to_column(fn)

    barrier = pltpu.get_barrier_semaphore()

    def greet(device):
        pl.semaphore_signal(barrier, inc=1, device_id=device, device_id_type=MESH)


    def target_of(dx, dy):
        return {"gx": wrap(jnp.where(gx + dx < 0, gx + dx + nx, gx + dx), nx), "gy": gy + dy}

    def when(dy, sending, fn):
        if dy == 0:
            fn()
        else:
            beyond = gy + (dy if sending else -dy)
            pl.when((beyond >= 0) & (beyond < ny))(fn)

    def further(up, fn):
        for dy in range(2, ny):
            inside = gy + dy < ny if up else gy - dy >= 0
            pl.when(inside)(lambda dy=dy: fn({"gx": gx, "gy": gy + dy if up else gy - dy}))

    def greet_beyond(dy):
        for dx in (0, 1, -1):
            greet(target_of(dx, dy))

    for dy in (-1, 1):
        when(dy, True, lambda dy=dy: greet_beyond(dy))
    to_band(greet)
    further(True, greet)

    def meet():
        below, above = jnp.where(gy > 0, gy + 2, 0), jnp.where(gy < ny - 1, 3, 0)
        pl.semaphore_wait(barrier, nx - 1 + below + above)
        further(
            False,
            lambda device: pl.semaphore_signal(up_sem, inc=1, device_id=device, device_id_type=MESH),
        )

    def hear_answers():
        pl.when(gy < ny - 2)(lambda: pl.semaphore_wait(up_sem, ny - 2 - gy))

    meets_early = (gx // 2 == nx // 2 - 1) & (gy == ny - 1)
    pl.when(meets_early)(meet)

    planes, layers = (5, 3), (13, 12)

    def remote(src, dst, i, group, dx, dy):
        return pltpu.make_async_remote_copy(
            src_ref=src, dst_ref=dst, send_sem=hs_sem.at[group], recv_sem=hr_sem.at[i, group],
            device_id=target_of(dx, dy), device_id_type=MESH,
        )

    def beside(i, dx):
        part = pl.ds(0, planes[i])
        return remote(
            strips.at[i, :, part], land.at[i, 0 if dx > 0 else 1, pl.ds(1, rb_own), part], i, 0, dx, 0
        )

    def beside_all(i):
        both = land.at[i, :, pl.ds(1, rb_own), pl.ds(0, planes[i])]
        return remote(both, both, i, 0, 1, 0)

    def start_beyond(i, dy):
        at, group = (0, 1) if dy > 0 else (1, 2)
        part, rest = pl.ds(0, planes[i]), pl.ds(0, layers[i])
        remote(slab_out.at[i, at, rest], slab.at[i, at, rest], i, group, 0, dy).start()
        for dx in (1, -1):
            src = strips.at[i, pl.ds(rb_own - 1 if dy > 0 else 0, 1), part]
            dst = land.at[i, 0 if dx > 0 else 1, pl.ds(0 if dy > 0 else ext_tiles - 1, 1), part]
            remote(src, dst, i, group, dx, dy).start()

    def beyond_all(i, dy):
        every = counted.at[pl.ds(0, layers[i] + planes[i])]
        return remote(every, every, i, 1 if dy > 0 else 2, 1, 0)

    def clear(side):
        at = 0 if side == 0 else ext_tiles - 1
        slab[:, side] = jnp.zeros_like(slab[:, side])
        land[:, :, at] = jnp.zeros_like(land[:, :, at])

    pl.when(gy == 0)(lambda: clear(0))
    pl.when(gy == ny - 1)(lambda: clear(1))

    lane = lanes()
    sub = iota((8, 128), 0)

    def put_base(t, source, slots):
        for j in slots:
            base[j, band(t), :] = pick(source, (lane & -8) + j)

    def place_loads(ref, slot, sums):
        spread = None
        for t, total in enumerate(sums):
            total = jnp.broadcast_to(jnp.sum(total, axis=0, keepdims=True), (8, 128)) * (1.0 / (BLOCK * HALF))
            mine = pick(total, (lane & 15) * 8 + sub)
            here = lane // cb_own == t + rb_own * (gx % 2)
            spread = jnp.where(here, mine, 0.0 if spread is None else spread)
        ref[slot] = spread.astype(BF16)

    def two_parts(x):
        high = x.astype(BF16).astype(F32)
        return high, x - high

    def pack(i, f):
        ref = (*fields, base)[f]
        for at, t in enumerate((rb_own, 1)):
            if f == 3:
                edge = two_parts(st[(t - 1) * BLOCK : t * BLOCK, :] * (HALF * HALF))
                slab_out[i, at, 12] = jnp.concatenate(edge, axis=0).astype(BF16)
                continue
            for k in range(4):
                both = jnp.concatenate([ref[2 * k, band(t), :], ref[2 * k + 1, band(t), :]], axis=0)
                slab_out[i, at, 4 * f + k] = both.astype(BF16)
        packed = [None] * rb_own
        index = (lane & 7) + jnp.where(lane >= 64, cols - 8, 0)
        for j in range(8):
            here = (lane // 8) % 8 == j
            for b in range(rb_own):
                moved = pick(ref[j, band(b + 1), :], index)
                packed[b] = moved if j == 0 else jnp.where(here, moved, packed[b])
        for b in range(rb_own):
            parts = two_parts(packed[b]) if f == 3 else (packed[b],)
            for k, part in enumerate(parts):
                strips[i, b, f + k] = part.astype(BF16)

    def side_of(i, t, planes):
        west, east = (sum(land[i, side, t, k].astype(F32) for k in planes) for side in (0, 1))
        return jnp.where(lane >= 64, west, east)

    def assemble(i):
        for f, ref in enumerate(fields):
            for t in range(ext_tiles):
                ref[SIDE, band(t), :] = side_of(i, t, (f,))
            for at, t in enumerate((0, ext_tiles - 1)):
                for k in range(4):
                    both = slab[i, at, 4 * f + k].astype(F32)
                    ref[2 * k, band(t), :] = both[:8]
                    ref[2 * k + 1, band(t), :] = both[8:]

    def finish_base():
        for at, t in enumerate((0, ext_tiles - 1)):
            both = slab[0, at, 12].astype(F32)
            put_base(t, both[:8] + both[8:], range(8))
        for t in range(ext_tiles):
            base[SIDE, band(t), :] = side_of(0, t, (3, 4))

    def table(j, t, first, depth, wet):
        d = base[j, band(t), :]
        w = jnp.where(d > 0.0, 1.0, 0.0)
        part = pl.ds(t * BLOCK, BLOCK)
        for k in range(STEPS):
            depth[k, j, part, :] = d * KEEP ** -(first + k + 1)
            wet[k, j, part, :] = w * KEEP ** (first + k + 1)

    def own_tables(first, depth, wet):
        def fill(t, carry):
            for j in range(8):
                table(j, t, first, depth, wet)
            return carry

        lax.fori_loop(1, ext_tiles - 1, fill, 0)

    def edge_tables(first, depth, wet):
        for t in range(ext_tiles):
            for j in range(8) if t in (0, ext_tiles - 1) else ():
                table(j, t, first, depth, wet)
            table(SIDE, t, first, depth, wet)

    def gather(src, dst, group, device):
        return pltpu.make_async_remote_copy(
            src_ref=src, dst_ref=dst, send_sem=gs_sem, recv_sem=gr_sem.at[group],
            device_id=device, device_id_type=MESH,
        )

    def band_all():
        part = plane.at[pl.ds(0, nx - 1)]
        return gather(part, part, 0, target_of(1, 0))

    def column_all():
        part = pairs.at[pl.ds(0, ny - 1)]
        return gather(part, part, 1, target_of(1, 0))

    def everyone():
        part = tiles.at[pl.ds(0, n - 1)]
        return gather(part, part, 2, target_of(1, 0))

    def start_beside(i):
        for dx in (1, -1):
            beside(i, dx).start()

    def start_halos(i):
        start_beside(i)
        for dy in (1, -1):
            when(dy, True, lambda dy=dy: start_beyond(i, dy))

    def wait_halos(i):
        beside_all(i).wait_recv()
        for dy in (1, -1):
            when(dy, False, lambda dy=dy: beyond_all(i, dy).wait_recv())

    def finish_sends(i):
        beside_all(i).wait_send()
        for dy in (1, -1):
            when(dy, True, lambda dy=dy: beyond_all(i, dy).wait_send())

    def make_turning():
        for e in range(ext_tiles):
            row_ids = gy * rows - HALO + e * BLOCK + iota((BLOCK, cols), 0)
            turn[e] = (CORIOLIS / KEEP) * jnp.sin(latitude(row_ids, rows * ny))

    def make_green():
        t = iota((8, 128), 1)
        north = per_device
        south = north + cb_own
        west = south + cb_own
        east = west + rb_own + 2
        t_row = jnp.where(t < north, t // cb_own, jnp.where(t < south, -1, rb_own))
        t_col = jnp.where(t < north, t % cb_own, jnp.where(t < south, t - north, t - south))
        t_row = jnp.where(t >= east, t - east - 1, jnp.where(t >= west, t - west - 1, t_row))
        t_col = jnp.where(t >= east, cb_own, jnp.where(t >= west, -1, t_col))
        t_row = gy * rb_own + t_row
        t_col = gx * cb_own + t_col
        t_col = jnp.where(t_col < 0, t_col + coarse_cols, t_col)
        t_col = jnp.where(t_col >= coarse_cols, t_col - coarse_cols, t_col)
        target = unit_vectors(latitude(t_row, coarse_rows), longitude(t_col, coarse_cols))
        target = [jnp.broadcast_to(x[:1], (pair_rows, 128)) for x in target]

        def green_group(g, carry):
            p = g * 8 + iota((8, pair_rows), 0)
            k = iota((8, pair_rows), 1)
            s_col = ((p % (nx // 2)) * 2 + k // per_device) * cb_own + k % cb_own
            s_row = (p // (nx // 2)) * rb_own + (k % per_device) // cb_own
            source = unit_vectors(latitude(s_row, coarse_rows), longitude(s_col, coarse_cols))
            source = [jnp.transpose(x) for x in source]
            for j in range(8):
                square = None
                for s, t_vec in zip(source, target):
                    diff = jnp.broadcast_to(s[:, j : j + 1], (pair_rows, 128)) - t_vec
                    square = diff * diff if square is None else square + diff * diff
                value = GREEN_SCALE / (1.0 + jnp.sqrt(square) * (coarse_rows / math.pi))
                green[g * 8 + j] = value.astype(BF16)
            return carry

        lax.fori_loop(0, n // 16, green_group, 0)

    def load(i, ready=None):
        half = n // 4
        group = math.gcd(8, half)

        def pair(p):
            if i == 0:
                return pairs[p // (nx // 2), p % (nx // 2)].astype(F32)
            return tiles[2 * p].astype(F32) + tiles[2 * p + 1].astype(F32)

        def add_group(g, total):
            parts = []
            for first in range(0, group, max(group // 2, 1)):
                left, right = [], []
                for k in range(first, first + max(group // 2, 1)):
                    q = g * group + k
                    left.append(jnp.concatenate([pair(q), pair(q + half)], axis=0).astype(BF16))
                    right.append(jnp.concatenate([green[q], green[q + half]], axis=1))
                parts.append(
                    jnp.dot(jnp.concatenate(left, axis=1), jnp.concatenate(right, axis=0), preferred_element_type=F32)
                )
            return total + sum(parts)

        both = lax.fori_loop(0, half // group, add_group, jnp.zeros((2 * members, 256), F32))
        loading = both[:members, :128] + both[members:, 128:]
        l_out[...] = loading
        loading = loading * HALF
        north = per_device
        south = north + cb_own
        west = south + cb_own
        east = west + rb_own + 2
        own_member = (lane & 7) == sub
        sides = []
        for t in range(ext_tiles):
            first = north if t == 0 else south if t == ext_tiles - 1 else (t - 1) * cb_own
            main = pick(loading, lane // 8 + first)
            side = pick(loading, jnp.where(lane >= 64, west + t, east + t))
            both = []
            for value in (main, side):
                value = jnp.where(own_member, value, 0.0)
                if t == 0:
                    value = jnp.where(gy == 0, 0.0, value)
                if t == ext_tiles - 1:
                    value = jnp.where(gy == ny - 1, 0.0, value)
                both.append(jnp.broadcast_to(jnp.sum(value, axis=0, keepdims=True), (8, 128)))
            fine[t] = both[0]
            sides.append(both[1])
        if ready is not None:
            ready()
        for t in range(ext_tiles):
            for j in range(8):
                eta[j, band(t), :] = eta[j, band(t), :] - fine[t]
            eta[SIDE, band(t), :] = eta[SIDE, band(t), :] - sides[t]

    def interval(i):
        def step(n, carry):
            move_flow(ext_tiles, n, False, eta, pp, qq, pp, qq, depth0, turn)
            move_surface(ext_tiles, n, eta, eta, pp, qq, wet0)
            return carry

        lax.fori_loop(0, STEPS - 1, step, 0)
        move_flow(ext_tiles, STEPS - 1, True, eta, pp, qq, pp, qq, depth0, turn)
        sums = []
        for t in range(1, ext_tiles - 1):
            change = surface_change(t, STEPS - 1, False, pp, qq, wet0)
            total = None
            for j in range(8):
                value = eta[j, band(t), :] - change[j] + fine[t]
                eta[j, band(t), :] = value
                value = value * wet0[STEPS - 1, j, t * BLOCK : (t + 1) * BLOCK, :]
                total = value if total is None else total + value
            sums.append(total * KEEP ** -STEPS)
        return sums

    for copy in inputs[:3]:
        copy.wait()
    st[...] = jnp.where(in_o[...] > 0, in_d[...], 0.0)
    sums = []
    for t in range(1, ext_tiles - 1):
        part = slice((t - 1) * BLOCK, t * BLOCK)
        put_base(t, st[part, :] * (HALF * HALF), range(8))
        total = None
        for j, value in enumerate(exchange([[in3[0, m, part, :] for m in range(8)]])[0]):
            value = value * HALF
            eta[j, band(t), :] = value
            value = jnp.where(base[j, band(t), :] > 0.0, value, 0.0)
            total = value if total is None else total + value
        sums.append(total)
    place_loads(plane, gx, sums)

    def send_band():
        to_band(lambda device: gather(plane.at[gx], plane.at[gx], 0, device).start())

    pl.when(meets_early)(send_band)
    for copy in inputs[3:]:
        copy.wait()
    for f in (1, 2):
        for t in range(1, ext_tiles - 1):
            part = slice((t - 1) * BLOCK, t * BLOCK)
            for j, value in enumerate(exchange([[in3[f, m, part, :] for m in range(8)]])[0]):
                fields[f][j, band(t), :] = value * base[j, band(t), :]
    for f in range(4):
        pack(0, f)

    def meet_late():
        meet()
        send_band()

    pl.when(jnp.logical_not(meets_early))(meet_late)
    start_halos(0)

    make_turning()
    make_green()
    band_all().wait_recv()
    for k in range(nx // 2):
        pairs[gy, k] = (plane[2 * k].astype(F32) + plane[2 * k + 1].astype(F32)).astype(BF16)
    hear_answers()
    band_all().wait_send()
    to_column(lambda device: gather(pairs.at[gy], pairs.at[gy], 1, device).start())
    own_tables(0, depth0, wet0)
    wait_halos(0)
    assemble(0)
    finish_base()
    edge_tables(0, depth0, wet0)
    finish_sends(0)
    column_all().wait_send()
    column_all().wait_recv()
    load(0)
    place_loads(tiles, my_slot, interval(0))
    to_all_others(lambda device: gather(tiles.at[my_slot], tiles.at[my_slot], 2, device).start())
    for f in range(3):
        pack(1, f)
    start_halos(1)
    own_tables(STEPS, depth1, wet1)
    edge_tables(STEPS, depth1, wet1)
    for j in range(8):
        d = base[j, 2 * BLOCK : 2 * BLOCK + rows, :]
        restore[j] = jnp.where(d > 0.0, KEEP ** (2 * STEPS) / jnp.where(d > 0.0, d, 1.0), 0.0)
    finish_sends(1)
    everyone().wait_send()

    def halos_ready():
        wait_halos(1)
        assemble(1)

    everyone().wait_recv()
    load(1, halos_ready)


def finish(
    members, rows, cols,
    eta_in, p_in, q_in, depth, wet, turn, restore, fine, l_in,
    h_out, u_out, v_out, l_out,
    eta, pp, qq, staged, l_staged, sem,
):
    ext_tiles = (rows + 2 * HALO) // BLOCK
    blocks, width = l_staged.shape[1:]
    for b in range(blocks):
        l_staged[:, b, :] = l_in[:, b * width : (b + 1) * width]
    l_copy = pltpu.make_async_copy(l_staged, l_out, sem.at[3])
    l_copy.start()

    move_flow(ext_tiles, 0, False, eta_in, p_in, q_in, pp, qq, depth, turn)
    move_surface(ext_tiles, 0, eta_in, eta, pp, qq, wet)

    def step(n, carry):
        move_flow(ext_tiles, n, False, eta, pp, qq, pp, qq, depth, turn)
        move_surface(ext_tiles, n, eta, eta, pp, qq, wet)
        return carry

    lax.fori_loop(1, STEPS - 1, step, 0)
    move_flow(ext_tiles, STEPS - 1, True, eta, pp, qq, pp, qq, depth, turn)
    copies = [pltpu.make_async_copy(staged.at[f], out, sem.at[f]) for f, out in ((1, u_out), (2, v_out))]
    for t in range(rows // (BLOCK * TOGETHER)):
        part = pl.ds(t * BLOCK * TOGETHER, BLOCK * TOGETHER)
        copies.append(pltpu.make_async_copy(staged.at[0, :, part], h_out.at[:, part], sem.at[4 + t]))

    def place(f, first, groups):
        for k, values in enumerate(exchange(groups)):
            for m, value in enumerate(values):
                staged[f, m, (first + k - 1) * BLOCK : (first + k) * BLOCK, :] = value

    def flow(ref, t):
        return [ref[j, band(t), :] * restore[j, (t - 1) * BLOCK : t * BLOCK, :] for j in range(8)]

    def surface(t):
        change = surface_change(t, STEPS - 1, False, pp, qq, wet)
        return [(eta[j, band(t), :] - change[j] + fine[t]) * (1.0 / HALF) for j in range(8)]

    own = range(1, ext_tiles - 1, TOGETHER)
    for f, make in ((1, functools.partial(flow, pp)), (2, functools.partial(flow, qq)), (0, surface)):
        for first in own:
            place(f, first, [make(t) for t in range(first, first + TOGETHER)])
            if f == 0:
                copies[2 + first // TOGETHER].start()
        if f > 0:
            copies[f - 1].start()
    for copy in copies:
        copy.wait()
    l_copy.wait()


def shards(nx, ny, elevation, east_velocity, north_velocity, water_depth, land_sea):
    members, rows, cols = elevation.shape
    rb_own, cb_own = rows // BLOCK, cols // BLOCK
    n = nx * ny
    ext = rows + 2 * HALO
    tiles = ext // BLOCK
    hbm_spec = pl.BlockSpec(memory_space=pltpu.HBM)
    vmem_spec = pl.BlockSpec(memory_space=pltpu.VMEM)
    dma = pltpu.SemaphoreType.DMA
    field = (SLOTS, ext + 2 * BLOCK, cols)
    table = (STEPS, SLOTS, ext, cols)
    shape = (members, rows, cols)
    outs = tuple(
        jax.ShapeDtypeStruct(s, F32)
        for s in (
            field, field, field, table, table, (tiles, BLOCK, cols), (8, rows, cols), (tiles, BLOCK, cols),
            (members, 128),
        )
    )
    state = pl.pallas_call(
        functools.partial(kernel, nx, ny, members, rows, cols),
        out_shape=outs,
        in_specs=[hbm_spec] * 5,
        out_specs=(vmem_spec,) * len(outs),
        scratch_shapes=[
            pltpu.VMEM((3,) + shape, F32),
            pltpu.VMEM((rows, cols), F32),
            pltpu.VMEM((rows, cols), jnp.int32),
            pltpu.VMEM((INTERVALS, rb_own, 5, 8, cols), BF16),
            pltpu.VMEM((INTERVALS, 2, tiles, 5, 8, cols), BF16),
            pltpu.VMEM((INTERVALS, 2, 13, 16, cols), BF16),
            pltpu.VMEM((INTERVALS, 2, 13, 16, cols), BF16),
            pltpu.VMEM((18, 16, cols), BF16),
            pltpu.VMEM((rows, cols), F32),
            pltpu.VMEM(field, F32),
            pltpu.VMEM(table, F32),
            pltpu.VMEM(table, F32),
            pltpu.VMEM((n // 2, 2 * rb_own * cb_own, 128), BF16),
            pltpu.VMEM((nx, members, 2 * rb_own * cb_own), BF16),
            pltpu.VMEM((ny, nx // 2, members, 2 * rb_own * cb_own), BF16),
            pltpu.VMEM((n, members, 2 * rb_own * cb_own), BF16),
            dma((2,)),
            dma,
            dma((3,)),
            dma((3,)),
            dma((INTERVALS, 3)),
            pltpu.SemaphoreType.REGULAR,
        ],
        compiler_params=pltpu.CompilerParams(
            collective_id=0, has_side_effects=True, vmem_limit_bytes=40 * 1024 * 1024
        ),
        name="tide",
    )(
        *(
            pltpu.with_memory_space_constraint(x, pltpu.HBM)
            for x in (elevation, east_velocity, north_velocity, water_depth, land_sea)
        )
    )
    coarse = jax.ShapeDtypeStruct((members, rb_own, cb_own), F32)
    whole = jax.ShapeDtypeStruct(shape, F32)
    return pl.pallas_call(
        functools.partial(finish, members, rows, cols),
        out_shape=(whole, whole, whole, coarse),
        in_specs=[vmem_spec] * len(outs),
        out_specs=(hbm_spec,) * 4,
        scratch_shapes=[
            pltpu.VMEM(field, F32),
            pltpu.VMEM(field, F32),
            pltpu.VMEM(field, F32),
            pltpu.VMEM((3,) + shape, F32),
            pltpu.VMEM(coarse.shape, F32),
            dma((4 + rb_own,)),
        ],
        compiler_params=pltpu.CompilerParams(vmem_limit_bytes=8 * 1024 * 1024),
        name="finish",
    )(*state)


def solution(mesh):
    nx, ny = mesh.shape["gx"], mesh.shape["gy"]
    tile = P(None, "gy", "gx")
    return jax.shard_map(
        functools.partial(shards, nx, ny),
        mesh=mesh,
        in_specs=(tile, tile, tile, P("gy", "gx"), P("gy", "gx")),
        out_specs=(tile, tile, tile, tile),
        check_vma=False,
    )
```

```python
import functools
import math

import jax
import jax.numpy as jnp
from jax import lax
from jax.experimental import pallas as pl
from jax.experimental.pallas import tpu as pltpu
from jax.sharding import PartitionSpec as P

STEPS = 4
INTERVALS = 2
BLOCK = 8
HALO = 2 * STEPS

COURANT = 0.35
FRICTION = 0.02
CORIOLIS = 0.3
GREEN_SCALE = 0.25
KEEP = 1.0 - FRICTION
HALF = 0.5 * COURANT

MESH = pl.DeviceIdType.MESH
F32 = jnp.float32
BF16 = jnp.bfloat16

SIDE = 8
TOGETHER = 4
SLOTS = 9


def iota(shape, dim):
    return lax.broadcasted_iota(jnp.int32, shape, dim)


def latitude(row_ids, row_count):
    return ((row_ids.astype(F32) + 0.5) / row_count - 0.5) * jnp.pi


def longitude(col_ids, col_count):
    return (col_ids.astype(F32) + 0.5) / col_count * (2.0 * jnp.pi)


def unit_vectors(lat_angle, lon_angle):
    cos_lat = jnp.cos(lat_angle)
    return (cos_lat * jnp.cos(lon_angle), cos_lat * jnp.sin(lon_angle), jnp.sin(lat_angle))


def lanes():
    return iota((8, 128), 1)


def pick(x, index):
    return jnp.take_along_axis(x, index, axis=1)


def exchange(groups):
    lane = lanes()
    groups = [list(values) for values in groups]
    for bit in range(3):
        step = 1 << bit
        low = (lane & step) == 0
        index = lane ^ step
        for values in groups:
            for a in range(8):
                if a & step:
                    continue
                b = a | step
                moved = pick(jnp.where(low, values[b], values[a]), index)
                values[a], values[b] = jnp.where(low, values[a], moved), jnp.where(low, moved, values[b])
    return groups


def band(t):
    return pl.ds(BLOCK + t * BLOCK, BLOCK)


def shifted(t, by):
    return pl.ds(BLOCK + t * BLOCK + by, BLOCK)


def x_differences(values, with_side=True):
    lane = lanes()
    first, last = lane < 8, lane >= 120
    up_main, up_side = pltpu.roll(values[7], 8, 1), pltpu.roll(values[SIDE], 8, 1)
    down_main, down_side = pltpu.roll(values[0], 120, 1), pltpu.roll(values[SIDE], 120, 1)
    left = [jnp.where(first, up_side, up_main)] + values[:7]
    right = values[1:8] + [jnp.where(last, down_side, down_main)]
    if with_side:
        left.append(jnp.where(first, up_main, up_side))
        right.append(jnp.where(last, down_main, down_side))
    return [r - l for l, r in zip(left, right)]


def move_flow(tiles, n, last, eta, p_in, q_in, p_out, q_out, depth, turn):
    for t in range(tiles):
        inner = not last or 0 < t < tiles - 1
        coriolis = turn[t]
        if inner:
            diff = x_differences([eta[j, band(t), :] for j in range(SLOTS)])
        for j in range(SLOTS if inner else SIDE):
            d = depth[n, j, t * BLOCK : (t + 1) * BLOCK, :]
            p, q = p_in[j, band(t), :], q_in[j, band(t), :]
            if inner:
                p_out[j, band(t), :] = p + coriolis * q - d * diff[j]
            north = eta[j, shifted(t, 1), :] - eta[j, shifted(t, -1), :]
            q_out[j, band(t), :] = q - coriolis * p - d * north


def surface_change(t, n, with_side, p, q, wet):
    diff = x_differences([p[j, band(t), :] for j in range(SLOTS)], with_side)
    return [
        wet[n, j, t * BLOCK : (t + 1) * BLOCK, :]
        * (diff[j] + (q[j, shifted(t, 1), :] - q[j, shifted(t, -1), :]))
        for j in range(SLOTS if with_side else SIDE)
    ]


def move_surface(tiles, n, eta_in, eta_out, p, q, wet):
    for t in range(tiles):
        change = surface_change(t, n, True, p, q, wet)
        for j in range(SLOTS):
            eta_out[j, band(t), :] = eta_in[j, band(t), :] - change[j]


def kernel(
    nx, ny, members, rows, cols,
    h_in, u_in, v_in, d_in, o_in,
    eta, pp, qq, depth1, wet1, turn, restore, fine, l_out,
    in3, in_d, in_o, strips, land, slab_out, slab, counted, st, base, depth0, wet0, green, plane, pairs, tiles,
    in_sem, gs_sem, gr_sem, hs_sem, hr_sem, up_sem,
):
    gx, gy = lax.axis_index("gx"), lax.axis_index("gy")
    n = nx * ny
    rb_own, cb_own = rows // BLOCK, cols // BLOCK
    per_device = rb_own * cb_own
    pair_rows = 2 * per_device
    coarse_rows, coarse_cols = rb_own * ny, cb_own * nx
    ext = rows + 2 * HALO
    ext_tiles = ext // BLOCK
    my_slot = gy * nx + gx
    fields = (eta, pp, qq)

    inputs = [
        pltpu.make_async_copy(src, dst, done)
        for src, dst, done in (
            (d_in, in_d, hs_sem.at[0]), (o_in, in_o, hs_sem.at[1]), (h_in, in3.at[0], hs_sem.at[2]),
            (u_in, in3.at[1], in_sem.at[0]), (v_in, in3.at[2], in_sem.at[1]),
        )
    ]
    def wrap(index, size):
        return jnp.where(index >= size, index - size, index)

    far = 2 * (nx // 2 - 1 - gx // 2)

    def to_column(fn):
        for dy in range(ny):
            y = wrap(ny - 1 - gy + dy, ny)
            pl.when(y != gy)(lambda y=y: fn({"gx": gx, "gy": y}))

    def to_band(fn):
        def one(k, carry):
            x = wrap(far + k, nx)
            pl.when(x != gx)(lambda: fn({"gx": x, "gy": gy}))
            return carry

        lax.fori_loop(0, nx, one, 0)

    def to_all_others(fn):
        def column(k, carry):
            x = wrap(far + k, nx)

            def all_rows():
                for dy in range(ny):
                    fn({"gx": x, "gy": wrap(ny - 1 - gy + dy, ny)})

            pl.when(x != gx)(all_rows)
            return carry

        lax.fori_loop(0, nx, column, 0)
        to_column(fn)

    barrier = pltpu.get_barrier_semaphore()

    def greet(device):
        pl.semaphore_signal(barrier, inc=1, device_id=device, device_id_type=MESH)


    def target_of(dx, dy):
        return {"gx": wrap(jnp.where(gx + dx < 0, gx + dx + nx, gx + dx), nx), "gy": gy + dy}

    def when(dy, sending, fn):
        if dy == 0:
            fn()
        else:
            beyond = gy + (dy if sending else -dy)
            pl.when((beyond >= 0) & (beyond < ny))(fn)

    def further(up, fn):
        for dy in range(2, ny):
            inside = gy + dy < ny if up else gy - dy >= 0
            pl.when(inside)(lambda dy=dy: fn({"gx": gx, "gy": gy + dy if up else gy - dy}))

    def greet_beyond(dy):
        for dx in (0, 1, -1):
            greet(target_of(dx, dy))

    for dy in (-1, 1):
        when(dy, True, lambda dy=dy: greet_beyond(dy))
    to_band(greet)
    for copy in inputs:
        copy.start()
    further(True, greet)

    def meet():
        below, above = jnp.where(gy > 0, gy + 2, 0), jnp.where(gy < ny - 1, 3, 0)
        pl.semaphore_wait(barrier, nx - 1 + below + above)
        further(
            False,
            lambda device: pl.semaphore_signal(up_sem, inc=1, device_id=device, device_id_type=MESH),
        )

    def hear_answers():
        pl.when(gy < ny - 2)(lambda: pl.semaphore_wait(up_sem, ny - 2 - gy))

    meets_early = (gx // 2 == nx // 2 - 1) & (gy == ny - 1)
    pl.when(meets_early)(meet)

    planes, layers = (5, 3), (13, 12)

    def remote(src, dst, i, group, dx, dy):
        return pltpu.make_async_remote_copy(
            src_ref=src, dst_ref=dst, send_sem=hs_sem.at[group], recv_sem=hr_sem.at[i, group],
            device_id=target_of(dx, dy), device_id_type=MESH,
        )

    def beside(i, dx):
        part = pl.ds(0, planes[i])
        return remote(
            strips.at[i, :, part], land.at[i, 0 if dx > 0 else 1, pl.ds(1, rb_own), part], i, 0, dx, 0
        )

    def beside_all(i):
        both = land.at[i, :, pl.ds(1, rb_own), pl.ds(0, planes[i])]
        return remote(both, both, i, 0, 1, 0)

    def start_beyond(i, dy):
        at, group = (0, 1) if dy > 0 else (1, 2)
        part, rest = pl.ds(0, planes[i]), pl.ds(0, layers[i])
        remote(slab_out.at[i, at, rest], slab.at[i, at, rest], i, group, 0, dy).start()
        for dx in (1, -1):
            src = strips.at[i, pl.ds(rb_own - 1 if dy > 0 else 0, 1), part]
            dst = land.at[i, 0 if dx > 0 else 1, pl.ds(0 if dy > 0 else ext_tiles - 1, 1), part]
            remote(src, dst, i, group, dx, dy).start()

    def beyond_all(i, dy):
        every = counted.at[pl.ds(0, layers[i] + planes[i])]
        return remote(every, every, i, 1 if dy > 0 else 2, 1, 0)

    def clear(side):
        at = 0 if side == 0 else ext_tiles - 1
        slab[:, side] = jnp.zeros_like(slab[:, side])
        land[:, :, at] = jnp.zeros_like(land[:, :, at])

    pl.when(gy == 0)(lambda: clear(0))
    pl.when(gy == ny - 1)(lambda: clear(1))

    lane = lanes()
    sub = iota((8, 128), 0)

    def put_base(t, source, slots):
        for j in slots:
            base[j, band(t), :] = pick(source, (lane & -8) + j)

    def place_loads(ref, slot, sums):
        spread = None
        for t, total in enumerate(sums):
            total = jnp.broadcast_to(jnp.sum(total, axis=0, keepdims=True), (8, 128)) * (1.0 / (BLOCK * HALF))
            mine = pick(total, (lane & 15) * 8 + sub)
            here = lane // cb_own == t + rb_own * (gx % 2)
            spread = jnp.where(here, mine, 0.0 if spread is None else spread)
        ref[slot] = spread.astype(BF16)

    def two_parts(x):
        high = x.astype(BF16).astype(F32)
        return high, x - high

    def pack(i, f):
        ref = (*fields, base)[f]
        for at, t in enumerate((rb_own, 1)):
            if f == 3:
                edge = two_parts(st[(t - 1) * BLOCK : t * BLOCK, :] * (HALF * HALF))
                slab_out[i, at, 12] = jnp.concatenate(edge, axis=0).astype(BF16)
                continue
            for k in range(4):
                both = jnp.concatenate([ref[2 * k, band(t), :], ref[2 * k + 1, band(t), :]], axis=0)
                slab_out[i, at, 4 * f + k] = both.astype(BF16)
        packed = [None] * rb_own
        index = (lane & 7) + jnp.where(lane >= 64, cols - 8, 0)
        for j in range(8):
            here = (lane // 8) % 8 == j
            for b in range(rb_own):
                moved = pick(ref[j, band(b + 1), :], index)
                packed[b] = moved if j == 0 else jnp.where(here, moved, packed[b])
        for b in range(rb_own):
            parts = two_parts(packed[b]) if f == 3 else (packed[b],)
            for k, part in enumerate(parts):
                strips[i, b, f + k] = part.astype(BF16)

    def side_of(i, t, planes):
        west, east = (sum(land[i, side, t, k].astype(F32) for k in planes) for side in (0, 1))
        return jnp.where(lane >= 64, west, east)

    def assemble(i):
        for f, ref in enumerate(fields):
            for t in range(ext_tiles):
                ref[SIDE, band(t), :] = side_of(i, t, (f,))
            for at, t in enumerate((0, ext_tiles - 1)):
                for k in range(4):
                    both = slab[i, at, 4 * f + k].astype(F32)
                    ref[2 * k, band(t), :] = both[:8]
                    ref[2 * k + 1, band(t), :] = both[8:]

    def finish_base():
        for at, t in enumerate((0, ext_tiles - 1)):
            both = slab[0, at, 12].astype(F32)
            put_base(t, both[:8] + both[8:], range(8))
        for t in range(ext_tiles):
            base[SIDE, band(t), :] = side_of(0, t, (3, 4))

    def table(j, t, first, depth, wet):
        d = base[j, band(t), :]
        w = jnp.where(d > 0.0, 1.0, 0.0)
        part = pl.ds(t * BLOCK, BLOCK)
        for k in range(STEPS):
            depth[k, j, part, :] = d * KEEP ** -(first + k + 1)
            wet[k, j, part, :] = w * KEEP ** (first + k + 1)

    def own_tables(first, depth, wet):
        def fill(t, carry):
            for j in range(8):
                table(j, t, first, depth, wet)
            return carry

        lax.fori_loop(1, ext_tiles - 1, fill, 0)

    def edge_tables(first, depth, wet):
        for t in range(ext_tiles):
            for j in range(8) if t in (0, ext_tiles - 1) else ():
                table(j, t, first, depth, wet)
            table(SIDE, t, first, depth, wet)

    def gather(src, dst, group, device):
        return pltpu.make_async_remote_copy(
            src_ref=src, dst_ref=dst, send_sem=gs_sem, recv_sem=gr_sem.at[group],
            device_id=device, device_id_type=MESH,
        )

    def band_all():
        part = plane.at[pl.ds(0, nx - 1)]
        return gather(part, part, 0, target_of(1, 0))

    def column_all():
        part = pairs.at[pl.ds(0, ny - 1)]
        return gather(part, part, 1, target_of(1, 0))

    def everyone():
        part = tiles.at[pl.ds(0, n - 1)]
        return gather(part, part, 2, target_of(1, 0))

    def start_beside(i):
        for dx in (1, -1):
            beside(i, dx).start()

    def start_halos(i):
        start_beside(i)
        for dy in (1, -1):
            when(dy, True, lambda dy=dy: start_beyond(i, dy))

    def wait_halos(i):
        beside_all(i).wait_recv()
        for dy in (1, -1):
            when(dy, False, lambda dy=dy: beyond_all(i, dy).wait_recv())

    def finish_sends(i):
        beside_all(i).wait_send()
        for dy in (1, -1):
            when(dy, True, lambda dy=dy: beyond_all(i, dy).wait_send())

    def make_turning():
        for e in range(ext_tiles):
            row_ids = gy * rows - HALO + e * BLOCK + iota((BLOCK, cols), 0)
            turn[e] = (CORIOLIS / KEEP) * jnp.sin(latitude(row_ids, rows * ny))

    def make_green():
        t = iota((8, 128), 1)
        north = per_device
        south = north + cb_own
        west = south + cb_own
        east = west + rb_own + 2
        t_row = jnp.where(t < north, t // cb_own, jnp.where(t < south, -1, rb_own))
        t_col = jnp.where(t < north, t % cb_own, jnp.where(t < south, t - north, t - south))
        t_row = jnp.where(t >= east, t - east - 1, jnp.where(t >= west, t - west - 1, t_row))
        t_col = jnp.where(t >= east, cb_own, jnp.where(t >= west, -1, t_col))
        t_row = gy * rb_own + t_row
        t_col = gx * cb_own + t_col
        t_col = jnp.where(t_col < 0, t_col + coarse_cols, t_col)
        t_col = jnp.where(t_col >= coarse_cols, t_col - coarse_cols, t_col)
        target = unit_vectors(latitude(t_row, coarse_rows), longitude(t_col, coarse_cols))
        target = [jnp.broadcast_to(x[:1], (pair_rows, 128)) for x in target]

        def green_group(g, carry):
            p = g * 8 + iota((8, pair_rows), 0)
            k = iota((8, pair_rows), 1)
            s_col = ((p % (nx // 2)) * 2 + k // per_device) * cb_own + k % cb_own
            s_row = (p // (nx // 2)) * rb_own + (k % per_device) // cb_own
            source = unit_vectors(latitude(s_row, coarse_rows), longitude(s_col, coarse_cols))
            source = [jnp.transpose(x) for x in source]
            for j in range(8):
                square = None
                for s, t_vec in zip(source, target):
                    diff = jnp.broadcast_to(s[:, j : j + 1], (pair_rows, 128)) - t_vec
                    square = diff * diff if square is None else square + diff * diff
                value = GREEN_SCALE / (1.0 + jnp.sqrt(square) * (coarse_rows / math.pi))
                green[g * 8 + j] = value.astype(BF16)
            return carry

        lax.fori_loop(0, n // 16, green_group, 0)

    def load(i, ready=None):
        half = n // 4
        group = math.gcd(8, half)

        def pair(p):
            if i == 0:
                return pairs[p // (nx // 2), p % (nx // 2)].astype(F32)
            return tiles[2 * p].astype(F32) + tiles[2 * p + 1].astype(F32)

        def add_group(g, total):
            parts = []
            for first in range(0, group, max(group // 2, 1)):
                left, right = [], []
                for k in range(first, first + max(group // 2, 1)):
                    q = g * group + k
                    left.append(jnp.concatenate([pair(q), pair(q + half)], axis=0).astype(BF16))
                    right.append(jnp.concatenate([green[q], green[q + half]], axis=1))
                parts.append(
                    jnp.dot(jnp.concatenate(left, axis=1), jnp.concatenate(right, axis=0), preferred_element_type=F32)
                )
            return total + sum(parts)

        both = lax.fori_loop(0, half // group, add_group, jnp.zeros((2 * members, 256), F32))
        loading = both[:members, :128] + both[members:, 128:]
        l_out[...] = loading
        loading = loading * HALF
        north = per_device
        south = north + cb_own
        west = south + cb_own
        east = west + rb_own + 2
        own_member = (lane & 7) == sub
        sides = []
        for t in range(ext_tiles):
            first = north if t == 0 else south if t == ext_tiles - 1 else (t - 1) * cb_own
            main = pick(loading, lane // 8 + first)
            side = pick(loading, jnp.where(lane >= 64, west + t, east + t))
            both = []
            for value in (main, side):
                value = jnp.where(own_member, value, 0.0)
                if t == 0:
                    value = jnp.where(gy == 0, 0.0, value)
                if t == ext_tiles - 1:
                    value = jnp.where(gy == ny - 1, 0.0, value)
                both.append(jnp.broadcast_to(jnp.sum(value, axis=0, keepdims=True), (8, 128)))
            fine[t] = both[0]
            sides.append(both[1])
        if ready is not None:
            ready()
        for t in range(ext_tiles):
            for j in range(8):
                eta[j, band(t), :] = eta[j, band(t), :] - fine[t]
            eta[SIDE, band(t), :] = eta[SIDE, band(t), :] - sides[t]

    def interval(i):
        def step(n, carry):
            move_flow(ext_tiles, n, False, eta, pp, qq, pp, qq, depth0, turn)
            move_surface(ext_tiles, n, eta, eta, pp, qq, wet0)
            return carry

        lax.fori_loop(0, STEPS - 1, step, 0)
        move_flow(ext_tiles, STEPS - 1, True, eta, pp, qq, pp, qq, depth0, turn)
        sums = []
        for t in range(1, ext_tiles - 1):
            change = surface_change(t, STEPS - 1, False, pp, qq, wet0)
            total = None
            for j in range(8):
                value = eta[j, band(t), :] - change[j] + fine[t]
                eta[j, band(t), :] = value
                value = value * wet0[STEPS - 1, j, t * BLOCK : (t + 1) * BLOCK, :]
                total = value if total is None else total + value
            sums.append(total * KEEP ** -STEPS)
        return sums

    for copy in inputs[:3]:
        copy.wait()
    st[...] = jnp.where(in_o[...] > 0, in_d[...], 0.0)
    sums = []
    for t in range(1, ext_tiles - 1):
        part = slice((t - 1) * BLOCK, t * BLOCK)
        put_base(t, st[part, :] * (HALF * HALF), range(8))
        total = None
        for j, value in enumerate(exchange([[in3[0, m, part, :] for m in range(8)]])[0]):
            value = value * HALF
            eta[j, band(t), :] = value
            value = jnp.where(base[j, band(t), :] > 0.0, value, 0.0)
            total = value if total is None else total + value
        sums.append(total)
    place_loads(plane, gx, sums)

    def send_band():
        to_band(lambda device: gather(plane.at[gx], plane.at[gx], 0, device).start())

    pl.when(meets_early)(send_band)
    for copy in inputs[3:]:
        copy.wait()
    for f in (1, 2):
        for t in range(1, ext_tiles - 1):
            part = slice((t - 1) * BLOCK, t * BLOCK)
            for j, value in enumerate(exchange([[in3[f, m, part, :] for m in range(8)]])[0]):
                fields[f][j, band(t), :] = value * base[j, band(t), :]
    for f in range(4):
        pack(0, f)

    def meet_late():
        meet()
        send_band()

    pl.when(jnp.logical_not(meets_early))(meet_late)
    start_halos(0)

    make_turning()
    make_green()
    band_all().wait_recv()
    for k in range(nx // 2):
        pairs[gy, k] = (plane[2 * k].astype(F32) + plane[2 * k + 1].astype(F32)).astype(BF16)
    hear_answers()
    band_all().wait_send()
    to_column(lambda device: gather(pairs.at[gy], pairs.at[gy], 1, device).start())
    own_tables(0, depth0, wet0)
    wait_halos(0)
    assemble(0)
    finish_base()
    edge_tables(0, depth0, wet0)
    finish_sends(0)
    column_all().wait_send()
    column_all().wait_recv()
    load(0)
    place_loads(tiles, my_slot, interval(0))
    to_all_others(lambda device: gather(tiles.at[my_slot], tiles.at[my_slot], 2, device).start())
    for f in range(3):
        pack(1, f)
    start_halos(1)
    own_tables(STEPS, depth1, wet1)
    edge_tables(STEPS, depth1, wet1)
    for j in range(8):
        d = base[j, 2 * BLOCK : 2 * BLOCK + rows, :]
        restore[j] = jnp.where(d > 0.0, KEEP ** (2 * STEPS) / jnp.where(d > 0.0, d, 1.0), 0.0)
    finish_sends(1)
    everyone().wait_send()

    def halos_ready():
        wait_halos(1)
        assemble(1)

    everyone().wait_recv()
    load(1, halos_ready)


def finish(
    members, rows, cols,
    eta_in, p_in, q_in, depth, wet, turn, restore, fine, l_in,
    h_out, u_out, v_out, l_out,
    eta, pp, qq, staged, l_staged, sem,
):
    ext_tiles = (rows + 2 * HALO) // BLOCK
    blocks, width = l_staged.shape[1:]
    for b in range(blocks):
        l_staged[:, b, :] = l_in[:, b * width : (b + 1) * width]
    l_copy = pltpu.make_async_copy(l_staged, l_out, sem.at[3])
    l_copy.start()

    move_flow(ext_tiles, 0, False, eta_in, p_in, q_in, pp, qq, depth, turn)
    move_surface(ext_tiles, 0, eta_in, eta, pp, qq, wet)

    def step(n, carry):
        move_flow(ext_tiles, n, False, eta, pp, qq, pp, qq, depth, turn)
        move_surface(ext_tiles, n, eta, eta, pp, qq, wet)
        return carry

    lax.fori_loop(1, STEPS - 1, step, 0)
    move_flow(ext_tiles, STEPS - 1, True, eta, pp, qq, pp, qq, depth, turn)
    copies = [pltpu.make_async_copy(staged.at[f], out, sem.at[f]) for f, out in ((1, u_out), (2, v_out))]
    for t in range(rows // (BLOCK * TOGETHER)):
        part = pl.ds(t * BLOCK * TOGETHER, BLOCK * TOGETHER)
        copies.append(pltpu.make_async_copy(staged.at[0, :, part], h_out.at[:, part], sem.at[4 + t]))

    def place(f, first, groups):
        for k, values in enumerate(exchange(groups)):
            for m, value in enumerate(values):
                staged[f, m, (first + k - 1) * BLOCK : (first + k) * BLOCK, :] = value

    def flow(ref, t):
        return [ref[j, band(t), :] * restore[j, (t - 1) * BLOCK : t * BLOCK, :] for j in range(8)]

    def surface(t):
        change = surface_change(t, STEPS - 1, False, pp, qq, wet)
        return [(eta[j, band(t), :] - change[j] + fine[t]) * (1.0 / HALF) for j in range(8)]

    own = range(1, ext_tiles - 1, TOGETHER)
    for f, make in ((1, functools.partial(flow, pp)), (2, functools.partial(flow, qq)), (0, surface)):
        for first in own:
            place(f, first, [make(t) for t in range(first, first + TOGETHER)])
            if f == 0:
                copies[2 + first // TOGETHER].start()
        if f > 0:
            copies[f - 1].start()
    for copy in copies:
        copy.wait()
    l_copy.wait()


def shards(nx, ny, elevation, east_velocity, north_velocity, water_depth, land_sea):
    members, rows, cols = elevation.shape
    rb_own, cb_own = rows // BLOCK, cols // BLOCK
    n = nx * ny
    ext = rows + 2 * HALO
    tiles = ext // BLOCK
    hbm_spec = pl.BlockSpec(memory_space=pltpu.HBM)
    vmem_spec = pl.BlockSpec(memory_space=pltpu.VMEM)
    dma = pltpu.SemaphoreType.DMA
    field = (SLOTS, ext + 2 * BLOCK, cols)
    table = (STEPS, SLOTS, ext, cols)
    shape = (members, rows, cols)
    outs = tuple(
        jax.ShapeDtypeStruct(s, F32)
        for s in (
            field, field, field, table, table, (tiles, BLOCK, cols), (8, rows, cols), (tiles, BLOCK, cols),
            (members, 128),
        )
    )
    state = pl.pallas_call(
        functools.partial(kernel, nx, ny, members, rows, cols),
        out_shape=outs,
        in_specs=[hbm_spec] * 5,
        out_specs=(vmem_spec,) * len(outs),
        scratch_shapes=[
            pltpu.VMEM((3,) + shape, F32),
            pltpu.VMEM((rows, cols), F32),
            pltpu.VMEM((rows, cols), jnp.int32),
            pltpu.VMEM((INTERVALS, rb_own, 5, 8, cols), BF16),
            pltpu.VMEM((INTERVALS, 2, tiles, 5, 8, cols), BF16),
            pltpu.VMEM((INTERVALS, 2, 13, 16, cols), BF16),
            pltpu.VMEM((INTERVALS, 2, 13, 16, cols), BF16),
            pltpu.VMEM((18, 16, cols), BF16),
            pltpu.VMEM((rows, cols), F32),
            pltpu.VMEM(field, F32),
            pltpu.VMEM(table, F32),
            pltpu.VMEM(table, F32),
            pltpu.VMEM((n // 2, 2 * rb_own * cb_own, 128), BF16),
            pltpu.VMEM((nx, members, 2 * rb_own * cb_own), BF16),
            pltpu.VMEM((ny, nx // 2, members, 2 * rb_own * cb_own), BF16),
            pltpu.VMEM((n, members, 2 * rb_own * cb_own), BF16),
            dma((2,)),
            dma,
            dma((3,)),
            dma((3,)),
            dma((INTERVALS, 3)),
            pltpu.SemaphoreType.REGULAR,
        ],
        compiler_params=pltpu.CompilerParams(
            collective_id=0, has_side_effects=True, vmem_limit_bytes=40 * 1024 * 1024
        ),
        name="tide",
    )(
        *(
            pltpu.with_memory_space_constraint(x, pltpu.HBM)
            for x in (elevation, east_velocity, north_velocity, water_depth, land_sea)
        )
    )
    coarse = jax.ShapeDtypeStruct((members, rb_own, cb_own), F32)
    whole = jax.ShapeDtypeStruct(shape, F32)
    return pl.pallas_call(
        functools.partial(finish, members, rows, cols),
        out_shape=(whole, whole, whole, coarse),
        in_specs=[vmem_spec] * len(outs),
        out_specs=(hbm_spec,) * 4,
        scratch_shapes=[
            pltpu.VMEM(field, F32),
            pltpu.VMEM(field, F32),
            pltpu.VMEM(field, F32),
            pltpu.VMEM((3,) + shape, F32),
            pltpu.VMEM(coarse.shape, F32),
            dma((4 + rb_own,)),
        ],
        compiler_params=pltpu.CompilerParams(vmem_limit_bytes=8 * 1024 * 1024),
        name="finish",
    )(*state)


def solution(mesh):
    nx, ny = mesh.shape["gx"], mesh.shape["gy"]
    tile = P(None, "gy", "gx")
    return jax.shard_map(
        functools.partial(shards, nx, ny),
        mesh=mesh,
        in_specs=(tile, tile, tile, P("gy", "gx"), P("gy", "gx")),
        out_specs=(tile, tile, tile, tile),
        check_vma=False,
    )
```
